512 devices in a mesh: img: 32 (over z, core), row: 16 (over y, x).
Axes of the slice: x: 4, y: 4, z: 16, core: 2. Of those that a mesh axis runs over, the one named last changes fastest.
Arguments:
- features: float32 [128, 1024, 256], P('img', 'row'), may hold values from -8 to 8
- partners: int32 [128, 2], replicated, may hold values from 0 to 127, as said below
- counts: int32 [128], replicated, may hold values from 256 to 1024, as said below
- shared_proj: bfloat16 [256, 256], replicated, may hold values from -0.375 to 0.375
- value_proj: bfloat16 [256, 256], replicated, may hold values from -0.375 to 0.375
- out_proj: bfloat16 [256, 256], replicated, may hold values from -0.375 to 0.375
- ffn_in: bfloat16 [512, 512], replicated, may hold values from -0.25 to 0.25
- ffn_in_bias: float32 [512], replicated, may hold values from -3 to 3
- norm_gain: float32 [512], replicated, may hold values from 0.1 to 1.9
- norm_bias: float32 [512], replicated, may hold values from -3 to 3
- ffn_out: bfloat16 [512, 256], replicated, may hold values from -0.25 to 0.25
- ffn_out_bias: float32 [256], replicated, may hold values from -3 to 3
Outputs:
- refined: float32 [128, 1024, 256], P('img', 'row')
The draws below stay inside these ranges and needn't reach their ends.
Inputs may be any that keep to these rules, and one draw needn't show every extreme that they name: Images form blocks of 4 consecutive ones around a cycle of blocks. Both partners of an image lie in a block at distance 1 or 2 from its own block in either direction around the cycle. Of the 8 partner entries of one block, at most 3 lie in any one of those four blocks, and in every block exactly 3 lie in one of them. Keypoint slots at positions counts[i] and beyond of image i are padding; counts may equal 1024.
All inputs are finite; a program needn't handle non-finite values.
Results may differ from the reference program's by a relative error of at most 0.004.
Values may be sent and summed in bfloat16 or wider, within the bound.
A program may use at most 64 MiB of HBM per device.

```python
import jax
import jax.numpy as jnp
from jax import lax

D = 256
HEADS = 4
FFN = 512
KP = 1024
IMG_DEV = 4
CAP = 3
IMAGES = 128


def draw_partners(key, part):
    block_total = IMAGES // IMG_DEV
    edge_count = 2 * IMG_DEV

    def one_block(block_key, block_id):
        pick_key, rest_key, order_key, slot_key = jax.random.split(block_key, 4)
        full_offset = jax.random.randint(pick_key, (), 0, 4)
        remaining = (jnp.arange(3 * CAP, dtype=jnp.int32) // CAP + 1 + full_offset) % 4
        remaining = jax.random.permutation(rest_key, remaining)
        picks = jnp.concatenate([jnp.full((CAP,), full_offset, jnp.int32), remaining])[:edge_count]
        picks = jax.random.permutation(order_key, picks)
        offsets = jnp.array([1, -1, 2, -2], jnp.int32)[picks]
        target = (block_id + offsets) % block_total
        slot_idx = jax.random.randint(slot_key, (edge_count,), 0, IMG_DEV)
        return (target * IMG_DEV + slot_idx).reshape(IMG_DEV, 2)
    block_keys = jax.random.split(key, block_total)
    drawn = jax.vmap(one_block)(block_keys, jnp.arange(block_total, dtype=jnp.int32))
    return drawn.reshape(IMAGES, 2).astype(jnp.int32)


def draw_counts(key, part):
    drawn = jax.random.randint(key, (IMAGES,), KP // 4, KP + KP // 2)
    return jnp.minimum(drawn, KP).astype(jnp.int32)


def draw_features(key, part):
    draw_key = jax.random.fold_in(key, 0)
    return jnp.clip(jax.random.normal(draw_key, (IMAGES, KP, D)), -8.0, 8.0).astype(jnp.float32)


def normal_values(key, shape, scale, bound, held_as=jnp.bfloat16):
    values = scale * jax.random.normal(key, shape, jnp.float32)
    return jnp.clip(values, min=-bound, max=bound).astype(held_as)


def setup_inputs(seed: int = 0) -> dict:
    keys = jax.random.split(jax.random.key(seed), 13)
    return {
        "features": draw_features(jax.random.fold_in(keys[12], 71), 0),
        "partners": draw_partners(jax.random.fold_in(keys[12], 71), 0),
        "counts": draw_counts(jax.random.fold_in(keys[12], 71), 0),
        "shared_proj": normal_values(keys[3], (D, D), D ** -0.5, 0.375),
        "value_proj": normal_values(keys[4], (D, D), D ** -0.5, 0.375),
        "out_proj": normal_values(keys[5], (D, D), D ** -0.5, 0.375),
        "ffn_in": normal_values(keys[6], (FFN, FFN), FFN ** -0.5, 0.25),
        "ffn_in_bias": normal_values(keys[7], (FFN,), 0.5, 3.0, jnp.float32),
        "norm_gain": jnp.clip(1.0 + 0.18 * jax.random.normal(keys[8], (FFN,), jnp.float32), 0.1, 1.9),
        "norm_bias": normal_values(keys[9], (FFN,), 0.5, 3.0, jnp.float32),
        "ffn_out": normal_values(keys[10], (FFN, D), FFN ** -0.5, 0.25),
        "ffn_out_bias": normal_values(keys[11], (D,), 0.5, 3.0, jnp.float32),
    }


NEGATIVE = -1e+30

def masked_softmax(scores, allowed, axis_num):
    peak_value = lax.optimization_barrier(jnp.max(jnp.where(allowed, scores, NEGATIVE), axis=axis_num, keepdims=True))
    raised = jnp.where(allowed, jnp.exp(scores - peak_value), 0.0)
    return (raised / lax.optimization_barrier(jnp.sum(raised, axis=axis_num, keepdims=True))).astype(jnp.bfloat16)

def reference(features, partners, counts, shared_proj, value_proj, out_proj, ffn_in, ffn_in_bias, norm_gain, norm_bias, ffn_out, ffn_out_bias):
    head_dim = D // HEADS
    scale_factor = head_dim ** (-0.5)
    rounded = features.astype(jnp.bfloat16)
    flat_rows = rounded.reshape(IMAGES * KP, D)
    shared = jnp.dot(flat_rows, shared_proj, preferred_element_type=jnp.float32).astype(jnp.bfloat16).reshape(IMAGES, KP, HEADS, head_dim)
    values = jnp.dot(flat_rows, value_proj, preferred_element_type=jnp.float32).astype(jnp.bfloat16).reshape(IMAGES, KP, HEADS, head_dim)
    positions = jnp.arange(KP, dtype=jnp.int32)

    def one_edge(inboxes, edge_id):
        image_id = edge_id // 2
        partner = partners[image_id, edge_id % 2]
        query_side = lax.dynamic_index_in_dim(shared, image_id, 0, False).astype(jnp.float32)
        key_side = lax.dynamic_index_in_dim(shared, partner, 0, False).astype(jnp.float32)
        own_values = lax.dynamic_index_in_dim(values, image_id, 0, False).astype(jnp.float32)
        value_side = lax.dynamic_index_in_dim(values, partner, 0, False).astype(jnp.float32)
        scores = jnp.einsum('ahd,bhd->hab', query_side, key_side) * scale_factor
        row_weights = masked_softmax(scores, (positions < counts[partner])[None, None, :], 2)
        column_weights = masked_softmax(scores, (positions < counts[image_id])[None, :, None], 1)
        to_own = jnp.einsum('hab,bhd->ahd', row_weights.astype(jnp.float32), value_side).reshape(KP, D)
        to_partner = jnp.einsum('hab,ahd->bhd', column_weights.astype(jnp.float32), own_values).reshape(KP, D)
        inboxes = inboxes.at[image_id].add(to_own)
        inboxes = inboxes.at[partner].add(to_partner)
        return (inboxes, None)
    inbox, _ = lax.scan(one_edge, jnp.zeros((IMAGES, KP, D), jnp.float32), jnp.arange(IMAGES * 2, dtype=jnp.int32))
    degree = lax.optimization_barrier(jnp.sum((partners.reshape(1, -1) == jnp.arange(IMAGES, dtype=jnp.int32)[:, None]).astype(jnp.float32), axis=1))
    averaged = (inbox / (2.0 + degree)[:, None, None]).astype(jnp.bfloat16)
    projected = jnp.dot(averaged.reshape(IMAGES * KP, D), out_proj, preferred_element_type=jnp.float32).astype(jnp.bfloat16)
    joined = jnp.concatenate([flat_rows, projected], axis=1)
    hidden = jnp.dot(joined, ffn_in, preferred_element_type=jnp.float32) + ffn_in_bias
    center = lax.optimization_barrier(jnp.mean(hidden, axis=1, keepdims=True))
    spread = lax.optimization_barrier(jnp.mean((hidden - center) ** 2, axis=1, keepdims=True))
    normed = (hidden - center) * lax.rsqrt(spread + 1e-05) * norm_gain + norm_bias
    activated = jax.nn.gelu(normed, approximate=False).astype(jnp.bfloat16)
    update = jnp.dot(activated, ffn_out, preferred_element_type=jnp.float32) + ffn_out_bias
    return features + update.reshape(IMAGES, KP, D)
```

```python
import functools

import jax
import jax.numpy as jnp
from jax import lax
from jax.experimental import pallas as pl
from jax.experimental.pallas import tpu as pltpu
from jax.sharding import PartitionSpec as P

HEADS = 4
CAP = 3
OFFSETS = (1, -1, 2, -2)
PENALTY = -1e30
MESH = pl.DeviceIdType.MESH
F32 = jnp.float32
BF16 = jnp.bfloat16


def peer_order(count):
    if count == 16:
        return (1, 4, 15, 12, 5, 11, 3, 13, 2, 8, 6, 9, 14, 7, 10)
    return tuple(range(1, count))


def lanes(shape):
    return lax.broadcasted_iota(jnp.int32, shape, len(shape) - 1)


def kernel(
    img_count,
    row_devices,
    partners,
    counts,
    x_ref,
    wq_ref,
    wv_ref,
    wo_ref,
    f1_ref,
    b1_ref,
    gain_ref,
    nbias_ref,
    f2_ref,
    b2_ref,
    out_ref,
    xb,
    wh,
    w2,
    hid,
    zrecv,
    own_send,
    own_recv,
    part_send,
    part_recv,
    k_own,
    v_own,
    k_part,
    v_part,
    ret_acc,
    ret_send,
    msg_recv,
    sum_recv,
    back_send,
    back_recv,
    proj,
    z_send_sem,
    z_recv_sem,
    a_send_sem,
    a_recv_sem,
    l_sem,
    b_send_sem,
    b_recv_sem,
):
    per_dev, rows, width = x_ref.shape
    half = rows // 2
    head_dim = width // HEADS_OF(width)
    heads = width // head_dim
    pair = 2 * head_dim
    keypoints = rows * row_devices
    edges = 2 * per_dev
    scale = head_dim ** (-0.5)
    block = lax.axis_index("img")
    me = lax.axis_index("row")
    my_image = lax.div(me, heads)
    order = peer_order(row_devices)

    def img_peer(offset):
        return lax.rem(block + (offset + img_count), img_count)

    def row_peer(offset):
        return lax.rem(me + offset, row_devices)

    barrier = pltpu.get_barrier_semaphore()
    for offset in OFFSETS:
        pl.semaphore_signal(barrier, inc=1, device_id=(img_peer(offset), me), device_id_type=MESH)
    for offset in order:
        pl.semaphore_signal(
            barrier, inc=1, device_id=(block, row_peer(offset)), device_id_type=MESH
        )

    xb[...] = x_ref[...].astype(BF16)

    low = lanes((width, pair)) < head_dim
    for t in range(width // pair):
        q_t = wq_ref[:, t * pair : (t + 1) * pair].astype(F32)
        v_t = wv_ref[:, t * pair : (t + 1) * pair].astype(F32)
        first = jnp.where(low, q_t, pltpu.roll(v_t, head_dim, 1))
        second = jnp.where(low, pltpu.roll(q_t, head_dim, 1), v_t)
        wh[:, 2 * t * pair : (2 * t + 1) * pair] = first.astype(BF16)
        wh[:, (2 * t + 1) * pair : (2 * t + 2) * pair] = second.astype(BF16)

    pl.semaphore_wait(barrier, len(OFFSETS) + len(order))

    z_copies = []
    for kind, offset in enumerate(OFFSETS):
        copy = pltpu.make_async_remote_copy(
            src_ref=xb,
            dst_ref=zrecv.at[pl.ds(kind * per_dev, per_dev)],
            send_sem=z_send_sem.at[kind],
            recv_sem=z_recv_sem.at[kind],
            device_id=(img_peer(-offset), me),
            device_id_type=MESH,
        )
        copy.start()
        z_copies.append(copy)

    def spread(phase, send, recv):
        for offset in order:
            peer = row_peer(offset)
            pltpu.make_async_remote_copy(
                src_ref=send.at[peer],
                dst_ref=recv.at[me],
                send_sem=a_send_sem.at[phase],
                recv_sem=a_recv_sem.at[phase],
                device_id=(block, peer),
                device_id_type=MESH,
            ).start()
        pltpu.make_async_copy(send.at[me], recv.at[me], l_sem.at[phase]).start()

    def arrived(phase, send, recv):
        rest = pl.ds(0, row_devices - 1)
        pltpu.make_async_copy(recv.at[rest], recv.at[rest], a_recv_sem.at[phase]).wait()
        pltpu.make_async_copy(send.at[me], recv.at[me], l_sem.at[phase]).wait()

    def left(phase, send):
        rest = pl.ds(0, row_devices - 1)
        pltpu.make_async_copy(send.at[rest], send.at[rest], a_send_sem.at[phase]).wait()

    def projected_heads(source, send, image):
        both = jnp.dot(source, wh[...], preferred_element_type=F32).astype(BF16)
        for h in range(heads):
            send[image * heads + h] = both[:, h * pair : (h + 1) * pair]

    for image in range(per_dev):
        projected_heads(xb[image], own_send, image)
    spread(0, own_send, own_recv)

    def kind_of(entry, home):
        away = lax.rem(lax.div(entry, per_dev) - home + 2 * img_count, img_count)
        return jnp.where(
            away == 1, 0, jnp.where(away == img_count - 1, 1, jnp.where(away == 2, 2, 3))
        )

    my_entries = [partners[block * edges + e] for e in range(edges)]
    my_kinds = [kind_of(entry, block) for entry in my_entries]

    hid[...] = (
        jnp.dot(
            xb[...].reshape(per_dev * rows, width),
            f1_ref[0:width, :],
            preferred_element_type=F32,
        )
        + b1_ref[...]
    )
    for h in range(heads):
        piece = wo_ref[h * head_dim : (h + 1) * head_dim, :]
        blank = jnp.zeros_like(piece)
        w2[h * pair : h * pair + head_dim, 0:width] = blank
        w2[h * pair : h * pair + head_dim, width : 2 * width] = piece
        w2[h * pair + head_dim : (h + 1) * pair, 0:width] = piece
        w2[h * pair + head_dim : (h + 1) * pair, width : 2 * width] = blank

    for copy in z_copies:
        copy.wait()
    for j in range(2):
        for image in range(per_dev):
            e = 2 * image + j
            at = my_kinds[e] * per_dev + lax.rem(my_entries[e], per_dev)
            projected_heads(zrecv[at], part_send.at[j], image)
        spread(1 + j, part_send.at[j], part_recv.at[j])

    chunk = min(256, keypoints)
    lane = lanes((keypoints, pair))
    place = lax.broadcasted_iota(jnp.int32, (keypoints, pair), 0)

    def prepare(source, count, k_ref, v_ref):
        flat = source[...].reshape(keypoints, pair).astype(F32)
        penalty = jnp.where((lane == head_dim) & (place >= count), PENALTY, 0.0)
        k_ref[...] = jnp.where(lane < head_dim, flat * scale, penalty).astype(BF16).T
        v_ref[...] = jnp.where(
            lane >= head_dim, flat, jnp.where(lane == 0, 1.0, 0.0)
        ).astype(BF16)

    def attend(asking, k_ref, v_ref, finish):
        per_chunk = chunk // rows
        low_chunk = lanes((chunk, pair)) < head_dim
        low_half = lanes((chunk // 2, pair)) < head_dim

        def one_chunk(c, carry):
            q = asking[pl.ds(c * per_chunk, per_chunk)].reshape(chunk, pair)
            q = jnp.where(low_chunk, q, jnp.ones((), BF16))
            scores = jnp.dot(q, k_ref[...], preferred_element_type=F32)
            peak = jnp.max(scores, axis=1, keepdims=True)
            raised = jnp.exp(scores - peak).astype(BF16)
            total = jnp.dot(raised, v_ref[...], preferred_element_type=F32)
            message = total / total[:, 0:1]
            split = message.reshape(per_chunk, 2, half, pair)
            upper = split[:, 0].reshape(chunk // 2, pair)
            lower = pltpu.roll(split[:, 1].reshape(chunk // 2, pair), head_dim, 1)
            finish(c, per_chunk, jnp.where(low_half, lower, upper).reshape(per_chunk, half, pair))
            return carry

        lax.fori_loop(0, keypoints // chunk, one_chunk, 0)

    arrived(0, own_send, own_recv)
    prepare(own_recv, counts[block * per_dev + my_image], k_own, v_own)
    for j in range(2):
        arrived(1 + j, part_send.at[j], part_recv.at[j])
        asked = partners[block * edges + 2 * my_image + j]
        prepare(part_recv.at[j], counts[asked], k_part, v_part)

        def to_partner(c, n, message, j=j):
            ret_send[j, pl.ds(c * n, n)] = message.astype(BF16)

        def to_own(c, n, message, j=j):
            if j == 0:
                ret_acc[pl.ds(c * n, n)] = message
            else:
                ret_send[2, pl.ds(c * n, n)] = (ret_acc[pl.ds(c * n, n)] + message).astype(BF16)

        attend(part_recv.at[j], k_own, v_own, to_partner)
        spread(3 + j, ret_send.at[j], msg_recv.at[j])
        attend(own_recv, k_part, v_part, to_own)
    spread(5, ret_send.at[2], sum_recv)

    def ranks_of(kinds):
        ranks = []
        for e in range(edges):
            rank = jnp.int32(0)
            for before in range(e):
                rank = rank + jnp.where(kinds[before] == kinds[e], 1, 0)
            ranks.append(rank)
        return ranks

    my_ranks = ranks_of(my_kinds)
    arrived(3, ret_send.at[0], msg_recv.at[0])
    arrived(4, ret_send.at[1], msg_recv.at[1])
    back_copies = []
    for kind, offset in enumerate(OFFSETS):
        for c in range(CAP):
            edge = jnp.int32(0)
            for e in range(edges):
                edge = edge + jnp.where((my_kinds[e] == kind) & (my_ranks[e] == c), e, 0)
            image, j = lax.div(edge, 2), lax.rem(edge, 2)
            back_send[kind, c] = msg_recv[j, pl.ds(image * heads, heads)]
        copy = pltpu.make_async_remote_copy(
            src_ref=back_send.at[kind],
            dst_ref=back_recv.at[kind],
            send_sem=b_send_sem.at[kind],
            recv_sem=b_recv_sem.at[kind],
            device_id=(img_peer(offset), me),
            device_id_type=MESH,
        )
        copy.start()
        back_copies.append(copy)

    weights = []
    for kind, offset in enumerate(OFFSETS):
        source = img_peer(-offset)
        entries = [partners[source * edges + e] for e in range(edges)]
        kinds = [kind_of(entry, source) for entry in entries]
        ranks = ranks_of(kinds)
        for c in range(CAP):
            row = []
            for image in range(per_dev):
                hit = jnp.int32(0)
                for e in range(edges):
                    hit = hit + jnp.where(
                        (kinds[e] == kind)
                        & (ranks[e] == c)
                        & (lax.rem(entries[e], per_dev) == image),
                        1,
                        0,
                    )
                row.append(hit)
            weights.append(row)

    arrived(5, ret_send.at[2], sum_recv)
    for copy in back_copies:
        copy.wait()

    packed = []
    for image in range(per_dev):
        inbox = sum_recv[image * heads : (image + 1) * heads].astype(F32)
        degree = jnp.int32(2)
        for kind in range(len(OFFSETS)):
            for c in range(CAP):
                hit = weights[kind * CAP + c][image]
                degree = degree + hit
                inbox = inbox + hit.astype(F32) * back_recv[kind, c].astype(F32)
        packed.append((inbox / degree.astype(F32)).astype(BF16))
    stacked = jnp.concatenate(
        [jnp.concatenate([packed[i][h] for i in range(per_dev)], axis=0) for h in range(heads)],
        axis=1,
    )
    both = jnp.dot(stacked, w2[...], preferred_element_type=F32).astype(BF16)
    for image in range(per_dev):
        mine = both[image * half : (image + 1) * half]
        proj[image * rows : image * rows + half, :] = mine[:, 0:width]
        proj[image * rows + half : (image + 1) * rows, :] = mine[:, width : 2 * width]

    for image in range(per_dev):
        part = pl.ds(image * rows, rows)
        hidden = hid[part, :] + jnp.dot(
            proj[part, :], f1_ref[width : 2 * width, :], preferred_element_type=F32
        )
        center = jnp.mean(hidden, axis=1, keepdims=True)
        away = hidden - center
        spreads = jnp.mean(away * away, axis=1, keepdims=True)
        normed = away * lax.rsqrt(spreads + 1e-5) * gain_ref[...] + nbias_ref[...]
        active = (0.5 * normed * (1.0 + lax.erf(normed * (0.5**0.5)))).astype(BF16)
        out_ref[image] = (
            x_ref[image]
            + jnp.dot(active, f2_ref[...], preferred_element_type=F32)
            + b2_ref[...]
        )

    for phase, send in (
        (0, own_send),
        (1, part_send.at[0]),
        (2, part_send.at[1]),
        (3, ret_send.at[0]),
        (4, ret_send.at[1]),
        (5, ret_send.at[2]),
    ):
        left(phase, send)


def HEADS_OF(width):
    return width // 64


def per_device(
    features,
    partners,
    counts,
    shared_proj,
    value_proj,
    out_proj,
    ffn_in,
    ffn_in_bias,
    norm_gain,
    norm_bias,
    ffn_out,
    ffn_out_bias,
):
    img_count = lax.axis_size("img")
    row_devices = lax.axis_size("row")
    per_dev, rows, width = features.shape
    heads = HEADS_OF(width)
    head_dim = width // heads
    pair = 2 * head_dim
    keypoints = rows * row_devices
    hidden = ffn_in.shape[1]
    half = rows // 2
    kinds = len(OFFSETS)
    vmem = pl.BlockSpec(memory_space=pltpu.VMEM)
    smem = pl.BlockSpec(memory_space=pltpu.SMEM)
    return pl.pallas_call(
        functools.partial(kernel, img_count, row_devices),
        out_shape=jax.ShapeDtypeStruct(features.shape, F32),
        in_specs=[smem, smem] + [vmem] * 10,
        out_specs=vmem,
        scratch_shapes=[
            pltpu.VMEM((per_dev, rows, width), BF16),
            pltpu.VMEM((width, 2 * width), BF16),
            pltpu.VMEM((heads * pair, 2 * width), BF16),
            pltpu.VMEM((per_dev * rows, hidden), F32),
            pltpu.VMEM((kinds * per_dev, rows, width), BF16),
            pltpu.VMEM((row_devices, rows, pair), BF16),
            pltpu.VMEM((row_devices, rows, pair), BF16),
            pltpu.VMEM((2, row_devices, rows, pair), BF16),
            pltpu.VMEM((2, row_devices, rows, pair), BF16),
            pltpu.VMEM((pair, keypoints), BF16),
            pltpu.VMEM((keypoints, pair), BF16),
            pltpu.VMEM((pair, keypoints), BF16),
            pltpu.VMEM((keypoints, pair), BF16),
            pltpu.VMEM((row_devices, half, pair), F32),
            pltpu.VMEM((3, row_devices, half, pair), BF16),
            pltpu.VMEM((2, row_devices, half, pair), BF16),
            pltpu.VMEM((row_devices, half, pair), BF16),
            pltpu.VMEM((kinds, CAP, heads, half, pair), BF16),
            pltpu.VMEM((kinds, CAP, heads, half, pair), BF16),
            pltpu.VMEM((per_dev * rows, width), BF16),
            pltpu.SemaphoreType.DMA((kinds,)),
            pltpu.SemaphoreType.DMA((kinds,)),
            pltpu.SemaphoreType.DMA((6,)),
            pltpu.SemaphoreType.DMA((6,)),
            pltpu.SemaphoreType.DMA((6,)),
            pltpu.SemaphoreType.DMA((kinds,)),
            pltpu.SemaphoreType.DMA((kinds,)),
        ],
        compiler_params=pltpu.CompilerParams(
            collective_id=0, has_side_effects=True, vmem_limit_bytes=48 * 1024 * 1024
        ),
    )(
        partners.reshape(-1),
        counts,
        features,
        shared_proj,
        value_proj,
        out_proj,
        ffn_in,
        ffn_in_bias.reshape(1, -1),
        norm_gain.reshape(1, -1),
        norm_bias.reshape(1, -1),
        ffn_out,
        ffn_out_bias.reshape(1, -1),
    )


def solution(mesh):
    return jax.shard_map(
        per_device,
        mesh=mesh,
        in_specs=(P("img", "row", None), P(), P(), P(), P(), P(), P(), P(), P(), P(), P(), P()),
        out_specs=P("img", "row", None),
        check_vma=False,
    )
```

```python
import functools

import jax
import jax.numpy as jnp
from jax import lax
from jax.experimental import pallas as pl
from jax.experimental.pallas import tpu as pltpu
from jax.sharding import PartitionSpec as P

HEADS = 4
CAP = 3
OFFSETS = (1, -1, 2, -2)
PENALTY = -1e30
MESH = pl.DeviceIdType.MESH
F32 = jnp.float32
BF16 = jnp.bfloat16


def peer_order(count):
    if count == 16:
        return (1, 4, 15, 12, 5, 11, 3, 13, 2, 8, 6, 9, 14, 7, 10)
    return tuple(range(1, count))


def lanes(shape):
    return lax.broadcasted_iota(jnp.int32, shape, len(shape) - 1)


def kernel(
    img_count,
    row_devices,
    partners_hbm,
    counts_hbm,
    x_hbm,
    wq_hbm,
    wv_hbm,
    wo_hbm,
    f1_hbm,
    b1_hbm,
    gain_hbm,
    nbias_hbm,
    f2_hbm,
    b2_hbm,
    out_hbm,
    partners,
    counts,
    x_ref,
    wq_ref,
    wv_ref,
    wo_ref,
    f1_ref,
    b1_ref,
    gain_ref,
    nbias_ref,
    f2_ref,
    b2_ref,
    out_ref,
    in_sem,
    out_sem,
    xb,
    zsend,
    wh,
    w2,
    hid,
    zrecv,
    own_send,
    own_recv,
    part_send,
    part_recv,
    k_own,
    v_own,
    k_part,
    v_part,
    ret_acc,
    ret_send,
    msg_recv,
    sum_recv,
    back_send,
    back_recv,
    proj,
    z_send_sem,
    z_recv_sem,
    a_send_sem,
    a_recv_sem,
    l_sem,
    b_send_sem,
    b_recv_sem,
):
    per_dev, rows, width = x_ref.shape
    half = rows // 2
    head_dim = width // HEADS_OF(width)
    heads = width // head_dim
    pair = 2 * head_dim
    keypoints = rows * row_devices
    edges = 2 * per_dev
    scale = head_dim ** (-0.5)
    block = lax.axis_index("img")
    me = lax.axis_index("row")
    my_image = lax.div(me, heads)
    order = peer_order(row_devices)

    def img_peer(offset):
        return lax.rem(block + (offset + img_count), img_count)

    def row_peer(offset):
        return lax.rem(me + offset, row_devices)

    loads = [
        pltpu.make_async_copy(source, target, in_sem.at[n])
        for n, (source, target) in enumerate(
            (
                (partners_hbm, partners),
                (counts_hbm, counts),
                (x_hbm, x_ref),
                (wq_hbm, wq_ref),
                (wv_hbm, wv_ref),
                (f1_hbm, f1_ref),
                (b1_hbm, b1_ref),
                (wo_hbm, wo_ref),
                (gain_hbm, gain_ref),
                (nbias_hbm, nbias_ref),
                (f2_hbm, f2_ref),
                (b2_hbm, b2_ref),
            )
        )
    ]
    for load in loads:
        load.start()

    barrier = pltpu.get_barrier_semaphore()
    for offset in OFFSETS:
        pl.semaphore_signal(barrier, inc=1, device_id=(img_peer(offset), me), device_id_type=MESH)
    for offset in order:
        pl.semaphore_signal(
            barrier, inc=1, device_id=(block, row_peer(offset)), device_id_type=MESH
        )

    def entries_of(home):
        return [partners[e % 2, home * per_dev + e // 2] for e in range(edges)]

    def slots_between(entries, target):
        found, count = [], jnp.int32(0)
        for entry in entries:
            inside = lax.div(entry, per_dev) == target
            found.append((inside, count))
            count = count + jnp.where(inside, 1, 0)
        slots = []
        for c in range(CAP):
            edge, image = jnp.int32(0), jnp.int32(0)
            for e, (inside, rank) in enumerate(found):
                here = inside & (rank == c)
                edge = jnp.where(here, e + 1, edge)
                image = jnp.where(here, lax.rem(entries[e], per_dev) + 1, image)
            slots.append((edge, image))
        return found, slots

    loads[0].wait()
    incoming_slots = []
    for kind, offset in enumerate(OFFSETS):
        _, slots = slots_between(entries_of(img_peer(-offset)), block)
        incoming_slots.append([image for _, image in slots])
    loads[2].wait()
    xb[...] = x_ref[...].astype(BF16)
    for kind in range(len(OFFSETS)):
        for c in range(CAP):
            zsend[kind, c] = xb[jnp.maximum(incoming_slots[kind][c] - 1, 0)]

    pl.semaphore_wait(barrier, len(OFFSETS) + len(order))

    z_copies = []
    for kind, offset in enumerate(OFFSETS):
        copy = pltpu.make_async_remote_copy(
            src_ref=zsend.at[kind],
            dst_ref=zrecv.at[pl.ds(kind * CAP, CAP)],
            send_sem=z_send_sem.at[kind],
            recv_sem=z_recv_sem.at[kind],
            device_id=(img_peer(-offset), me),
            device_id_type=MESH,
        )
        copy.start()
        z_copies.append(copy)

    loads[3].wait()
    loads[4].wait()
    low = lanes((width, pair)) < head_dim
    for t in range(width // pair):
        q_t = wq_ref[:, t * pair : (t + 1) * pair].astype(F32)
        v_t = wv_ref[:, t * pair : (t + 1) * pair].astype(F32)
        first = jnp.where(low, q_t, pltpu.roll(v_t, head_dim, 1))
        second = jnp.where(low, pltpu.roll(q_t, head_dim, 1), v_t)
        wh[:, 2 * t * pair : (2 * t + 1) * pair] = first.astype(BF16)
        wh[:, (2 * t + 1) * pair : (2 * t + 2) * pair] = second.astype(BF16)

    def spread(phase, send, recv):
        for offset in order:
            peer = row_peer(offset)
            pltpu.make_async_remote_copy(
                src_ref=send.at[peer],
                dst_ref=recv.at[me],
                send_sem=a_send_sem.at[phase],
                recv_sem=a_recv_sem.at[phase],
                device_id=(block, peer),
                device_id_type=MESH,
            ).start()
        pltpu.make_async_copy(send.at[me], recv.at[me], l_sem.at[phase]).start()

    def arrived(phase, send, recv):
        rest = pl.ds(0, row_devices - 1)
        pltpu.make_async_copy(recv.at[rest], recv.at[rest], a_recv_sem.at[phase]).wait()
        pltpu.make_async_copy(send.at[me], recv.at[me], l_sem.at[phase]).wait()

    def left(phase, send):
        rest = pl.ds(0, row_devices - 1)
        pltpu.make_async_copy(send.at[rest], send.at[rest], a_send_sem.at[phase]).wait()

    def projected_heads(source, send, image):
        both = jnp.dot(source, wh[...], preferred_element_type=F32).astype(BF16)
        for h in range(heads):
            send[image * heads + h] = both[:, h * pair : (h + 1) * pair]

    for image in range(per_dev):
        projected_heads(xb[image], own_send, image)
    spread(0, own_send, own_recv)

    my_entries = entries_of(block)
    my_slots = []
    positions = [jnp.int32(0)] * edges
    for kind, offset in enumerate(OFFSETS):
        found, slots = slots_between(my_entries, img_peer(offset))
        my_slots.append([edge for edge, _ in slots])
        for e, (inside, rank) in enumerate(found):
            positions[e] = jnp.where(
                inside, kind * CAP + jnp.minimum(rank, CAP - 1), positions[e]
            )
    loads[1].wait()
    for load in loads[5:]:
        load.wait()

    hid[...] = (
        jnp.dot(
            xb[...].reshape(per_dev * rows, width),
            f1_ref[0:width, :],
            preferred_element_type=F32,
        )
        + b1_ref[...]
    )
    for h in range(heads):
        piece = wo_ref[h * head_dim : (h + 1) * head_dim, :]
        blank = jnp.zeros_like(piece)
        w2[h * pair : h * pair + head_dim, 0:width] = blank
        w2[h * pair : h * pair + head_dim, width : 2 * width] = piece
        w2[h * pair + head_dim : (h + 1) * pair, 0:width] = piece
        w2[h * pair + head_dim : (h + 1) * pair, width : 2 * width] = blank

    for copy in z_copies:
        copy.wait()
    for j in range(2):
        for image in range(per_dev):
            projected_heads(zrecv[positions[2 * image + j]], part_send.at[j], image)
        spread(1 + j, part_send.at[j], part_recv.at[j])

    chunk = min(256, keypoints)
    lane = lanes((keypoints, pair))
    place = lax.broadcasted_iota(jnp.int32, (keypoints, pair), 0)

    def prepare(source, count, k_ref, v_ref):
        flat = source[...].reshape(keypoints, pair).astype(F32)
        penalty = jnp.where((lane == head_dim) & (place >= count), PENALTY, 0.0)
        k_ref[...] = jnp.where(lane < head_dim, flat * scale, penalty).astype(BF16).T
        v_ref[...] = jnp.where(
            lane >= head_dim, flat, jnp.where(lane == 0, 1.0, 0.0)
        ).astype(BF16)

    def attend(asking, k_ref, v_ref, finish):
        per_chunk = chunk // rows
        low_chunk = lanes((chunk, pair)) < head_dim
        low_half = lanes((chunk // 2, pair)) < head_dim

        def one_chunk(c, carry):
            q = asking[pl.ds(c * per_chunk, per_chunk)].reshape(chunk, pair)
            q = jnp.where(low_chunk, q, jnp.ones((), BF16))
            scores = jnp.dot(q, k_ref[...], preferred_element_type=F32)
            peak = jnp.max(scores, axis=1, keepdims=True)
            raised = jnp.exp(scores - peak).astype(BF16)
            total = jnp.dot(raised, v_ref[...], preferred_element_type=F32)
            message = total / total[:, 0:1]
            split = message.reshape(per_chunk, 2, half, pair)
            upper = split[:, 0].reshape(chunk // 2, pair)
            lower = pltpu.roll(split[:, 1].reshape(chunk // 2, pair), head_dim, 1)
            finish(c, per_chunk, jnp.where(low_half, lower, upper).reshape(per_chunk, half, pair))
            return carry

        lax.fori_loop(0, keypoints // chunk, one_chunk, 0)

    arrived(0, own_send, own_recv)
    prepare(own_recv, counts[block * per_dev + my_image], k_own, v_own)
    for j in range(2):
        arrived(1 + j, part_send.at[j], part_recv.at[j])
        asked = partners[j, block * per_dev + my_image]
        prepare(part_recv.at[j], counts[asked], k_part, v_part)

        def to_partner(c, n, message, j=j):
            ret_send[j, pl.ds(c * n, n)] = message.astype(BF16)

        def to_own(c, n, message, j=j):
            if j == 0:
                ret_acc[pl.ds(c * n, n)] = message
            else:
                ret_send[2, pl.ds(c * n, n)] = (ret_acc[pl.ds(c * n, n)] + message).astype(BF16)

        attend(part_recv.at[j], k_own, v_own, to_partner)
        spread(3 + j, ret_send.at[j], msg_recv.at[j])
        attend(own_recv, k_part, v_part, to_own)
    spread(5, ret_send.at[2], sum_recv)

    arrived(3, ret_send.at[0], msg_recv.at[0])
    arrived(4, ret_send.at[1], msg_recv.at[1])
    back_copies = []
    for kind, offset in enumerate(OFFSETS):
        for c in range(CAP):
            edge = jnp.maximum(my_slots[kind][c] - 1, 0)
            image, j = lax.div(edge, 2), lax.rem(edge, 2)
            back_send[kind, c] = msg_recv[j, pl.ds(image * heads, heads)]
        copy = pltpu.make_async_remote_copy(
            src_ref=back_send.at[kind],
            dst_ref=back_recv.at[kind],
            send_sem=b_send_sem.at[kind],
            recv_sem=b_recv_sem.at[kind],
            device_id=(img_peer(offset), me),
            device_id_type=MESH,
        )
        copy.start()
        back_copies.append(copy)

    arrived(5, ret_send.at[2], sum_recv)
    for copy in back_copies:
        copy.wait()

    packed = []
    for image in range(per_dev):
        inbox = sum_recv[image * heads : (image + 1) * heads].astype(F32)
        degree = jnp.int32(2)
        for kind in range(len(OFFSETS)):
            for c in range(CAP):
                hit = jnp.where(incoming_slots[kind][c] == image + 1, 1, 0)
                degree = degree + hit
                inbox = inbox + hit.astype(F32) * back_recv[kind, c].astype(F32)
        packed.append((inbox / degree.astype(F32)).astype(BF16))
    stacked = jnp.concatenate(
        [jnp.concatenate([packed[i][h] for i in range(per_dev)], axis=0) for h in range(heads)],
        axis=1,
    )
    both = jnp.dot(stacked, w2[...], preferred_element_type=F32).astype(BF16)
    for image in range(per_dev):
        mine = both[image * half : (image + 1) * half]
        proj[image * rows : image * rows + half, :] = mine[:, 0:width]
        proj[image * rows + half : (image + 1) * rows, :] = mine[:, width : 2 * width]

    stores = []
    for image in range(per_dev):
        part = pl.ds(image * rows, rows)
        hidden = hid[part, :] + jnp.dot(
            proj[part, :], f1_ref[width : 2 * width, :], preferred_element_type=F32
        )
        center = jnp.mean(hidden, axis=1, keepdims=True)
        away = hidden - center
        spreads = jnp.mean(away * away, axis=1, keepdims=True)
        normed = away * lax.rsqrt(spreads + 1e-5) * gain_ref[...] + nbias_ref[...]
        active = (0.5 * normed * (1.0 + lax.erf(normed * (0.5**0.5)))).astype(BF16)
        out_ref[image] = (
            x_ref[image]
            + jnp.dot(active, f2_ref[...], preferred_element_type=F32)
            + b2_ref[...]
        )
        stores.append(
            pltpu.make_async_copy(out_ref.at[image], out_hbm.at[image], out_sem.at[image])
        )
        stores[-1].start()

    for phase, send in (
        (0, own_send),
        (1, part_send.at[0]),
        (2, part_send.at[1]),
        (3, ret_send.at[0]),
        (4, ret_send.at[1]),
        (5, ret_send.at[2]),
    ):
        left(phase, send)
    for store in stores:
        store.wait()


def HEADS_OF(width):
    return width // 64


def per_device(
    features,
    partners,
    counts,
    shared_proj,
    value_proj,
    out_proj,
    ffn_in,
    ffn_in_bias,
    norm_gain,
    norm_bias,
    ffn_out,
    ffn_out_bias,
):
    img_count = lax.axis_size("img")
    row_devices = lax.axis_size("row")
    per_dev, rows, width = features.shape
    heads = HEADS_OF(width)
    head_dim = width // heads
    pair = 2 * head_dim
    keypoints = rows * row_devices
    hidden = ffn_in.shape[1]
    half = rows // 2
    kinds = len(OFFSETS)
    anywhere = pl.BlockSpec(memory_space=pl.ANY)
    return pl.pallas_call(
        functools.partial(kernel, img_count, row_devices),
        out_shape=jax.ShapeDtypeStruct(features.shape, F32),
        in_specs=[anywhere] * 12,
        out_specs=anywhere,
        scratch_shapes=[
            pltpu.SMEM(partners.shape[::-1], jnp.int32),
            pltpu.SMEM(counts.shape, jnp.int32),
            pltpu.VMEM(features.shape, F32),
            pltpu.VMEM(shared_proj.shape, BF16),
            pltpu.VMEM(value_proj.shape, BF16),
            pltpu.VMEM(out_proj.shape, BF16),
            pltpu.VMEM(ffn_in.shape, BF16),
            pltpu.VMEM((1, hidden), F32),
            pltpu.VMEM((1, hidden), F32),
            pltpu.VMEM((1, hidden), F32),
            pltpu.VMEM(ffn_out.shape, BF16),
            pltpu.VMEM((1, width), F32),
            pltpu.VMEM(features.shape, F32),
            pltpu.SemaphoreType.DMA((12,)),
            pltpu.SemaphoreType.DMA((per_dev,)),
            pltpu.VMEM((per_dev, rows, width), BF16),
            pltpu.VMEM((kinds, CAP, rows, width), BF16),
            pltpu.VMEM((width, 2 * width), BF16),
            pltpu.VMEM((heads * pair, 2 * width), BF16),
            pltpu.VMEM((per_dev * rows, hidden), F32),
            pltpu.VMEM((kinds * CAP, rows, width), BF16),
            pltpu.VMEM((row_devices, rows, pair), BF16),
            pltpu.VMEM((row_devices, rows, pair), BF16),
            pltpu.VMEM((2, row_devices, rows, pair), BF16),
            pltpu.VMEM((2, row_devices, rows, pair), BF16),
            pltpu.VMEM((pair, keypoints), BF16),
            pltpu.VMEM((keypoints, pair), BF16),
            pltpu.VMEM((pair, keypoints), BF16),
            pltpu.VMEM((keypoints, pair), BF16),
            pltpu.VMEM((row_devices, half, pair), F32),
            pltpu.VMEM((3, row_devices, half, pair), BF16),
            pltpu.VMEM((2, row_devices, half, pair), BF16),
            pltpu.VMEM((row_devices, half, pair), BF16),
            pltpu.VMEM((kinds, CAP, heads, half, pair), BF16),
            pltpu.VMEM((kinds, CAP, heads, half, pair), BF16),
            pltpu.VMEM((per_dev * rows, width), BF16),
            pltpu.SemaphoreType.DMA((kinds,)),
            pltpu.SemaphoreType.DMA((kinds,)),
            pltpu.SemaphoreType.DMA((6,)),
            pltpu.SemaphoreType.DMA((6,)),
            pltpu.SemaphoreType.DMA((6,)),
            pltpu.SemaphoreType.DMA((kinds,)),
            pltpu.SemaphoreType.DMA((kinds,)),
        ],
        compiler_params=pltpu.CompilerParams(
            collective_id=0, has_side_effects=True, vmem_limit_bytes=60 * 1024 * 1024
        ),
    )(
        partners.T,
        counts,
        features,
        shared_proj,
        value_proj,
        out_proj,
        ffn_in,
        ffn_in_bias.reshape(1, -1),
        norm_gain.reshape(1, -1),
        norm_bias.reshape(1, -1),
        ffn_out,
        ffn_out_bias.reshape(1, -1),
    )


def solution(mesh):
    return jax.shard_map(
        per_device,
        mesh=mesh,
        in_specs=(P("img", "row", None), P(), P(), P(), P(), P(), P(), P(), P(), P(), P(), P()),
        out_specs=P("img", "row", None),
        check_vma=False,
    )
```

```python
import functools

import jax
import jax.numpy as jnp
from jax import lax
from jax.experimental import pallas as pl
from jax.experimental.pallas import tpu as pltpu
from jax.sharding import PartitionSpec as P

HEADS = 4
CAP = 3
OFFSETS = (1, -1, 2, -2)
PENALTY = -1e30
MESH = pl.DeviceIdType.MESH
F32 = jnp.float32
BF16 = jnp.bfloat16


def peer_order(count):
    if count == 16:
        return (1, 4, 15, 12, 5, 11, 3, 13, 2, 8, 6, 9, 14, 7, 10)
    return tuple(range(1, count))


def lanes(shape):
    return lax.broadcasted_iota(jnp.int32, shape, len(shape) - 1)


def kernel(
    img_count,
    row_devices,
    partners_hbm,
    counts_hbm,
    x_hbm,
    wq_hbm,
    wv_hbm,
    wo_hbm,
    f1_hbm,
    b1_hbm,
    gain_hbm,
    nbias_hbm,
    f2_hbm,
    b2_hbm,
    out_hbm,
    partners,
    counts,
    x_ref,
    wq_ref,
    wv_ref,
    wo_ref,
    f1_ref,
    b1_ref,
    gain_ref,
    nbias_ref,
    f2_ref,
    b2_ref,
    out_ref,
    in_sem,
    out_sem,
    xb,
    zsend,
    wh,
    w2,
    hid,
    zrecv,
    own_send,
    own_recv,
    part_send,
    part_recv,
    k_own,
    q_own,
    v_own,
    k_part,
    q_part,
    v_part,
    ahead_even,
    ahead_odd,
    ret_acc,
    ret_send,
    msg_recv,
    sum_recv,
    back_send,
    back_recv,
    proj,
    z_send_sem,
    z_recv_sem,
    a_send_sem,
    a_recv_sem,
    l_sem,
    b_send_sem,
    b_recv_sem,
):
    per_dev, rows, width = x_ref.shape
    half = rows // 2
    head_dim = width // HEADS_OF(width)
    heads = width // head_dim
    pair = 2 * head_dim
    keypoints = rows * row_devices
    edges = 2 * per_dev
    scale = head_dim ** (-0.5)
    block = lax.axis_index("img")
    me = lax.axis_index("row")
    my_image = lax.div(me, heads)
    ahead = (ahead_even, ahead_odd)
    order = peer_order(row_devices)

    def img_peer(offset):
        return lax.rem(block + (offset + img_count), img_count)

    def row_peer(offset):
        return lax.rem(me + offset, row_devices)

    loads = [
        pltpu.make_async_copy(source, target, in_sem.at[n])
        for n, (source, target) in enumerate(
            (
                (partners_hbm, partners),
                (counts_hbm, counts),
                (x_hbm, x_ref),
                (wq_hbm, wq_ref),
                (wv_hbm, wv_ref),
                (f1_hbm, f1_ref),
                (b1_hbm, b1_ref),
                (wo_hbm, wo_ref),
                (gain_hbm, gain_ref),
                (nbias_hbm, nbias_ref),
                (f2_hbm, f2_ref),
                (b2_hbm, b2_ref),
            )
        )
    ]
    for load in loads:
        load.start()

    barrier = pltpu.get_barrier_semaphore()
    for offset in OFFSETS:
        pl.semaphore_signal(barrier, inc=1, device_id=(img_peer(offset), me), device_id_type=MESH)
    for offset in order:
        pl.semaphore_signal(
            barrier, inc=1, device_id=(block, row_peer(offset)), device_id_type=MESH
        )

    def entries_of(home):
        return [partners[e % 2, home * per_dev + e // 2] for e in range(edges)]

    def slots_between(entries, target):
        found, count = [], jnp.int32(0)
        for entry in entries:
            inside = lax.div(entry, per_dev) == target
            found.append((inside, count))
            count = count + jnp.where(inside, 1, 0)
        slots = []
        for c in range(CAP):
            edge, image = jnp.int32(0), jnp.int32(0)
            for e, (inside, rank) in enumerate(found):
                here = inside & (rank == c)
                edge = jnp.where(here, e + 1, edge)
                image = jnp.where(here, lax.rem(entries[e], per_dev) + 1, image)
            slots.append((edge, image))
        return found, slots

    loads[0].wait()
    incoming_slots = []
    for kind, offset in enumerate(OFFSETS):
        _, slots = slots_between(entries_of(img_peer(-offset)), block)
        incoming_slots.append([image for _, image in slots])
    loads[2].wait()
    xb[...] = x_ref[...].astype(BF16)
    for kind in range(len(OFFSETS)):
        for c in range(CAP):
            zsend[kind, c] = xb[jnp.maximum(incoming_slots[kind][c] - 1, 0)]

    pl.semaphore_wait(barrier, len(OFFSETS) + len(order))

    z_copies = []
    for kind, offset in enumerate(OFFSETS):
        copy = pltpu.make_async_remote_copy(
            src_ref=zsend.at[kind],
            dst_ref=zrecv.at[pl.ds(kind * CAP, CAP)],
            send_sem=z_send_sem.at[kind],
            recv_sem=z_recv_sem.at[kind],
            device_id=(img_peer(-offset), me),
            device_id_type=MESH,
        )
        copy.start()
        z_copies.append(copy)

    loads[3].wait()
    loads[4].wait()
    low = lanes((width, pair)) < head_dim
    for t in range(width // pair):
        q_t = wq_ref[:, t * pair : (t + 1) * pair].astype(F32)
        v_t = wv_ref[:, t * pair : (t + 1) * pair].astype(F32)
        first = jnp.where(low, q_t, pltpu.roll(v_t, head_dim, 1))
        second = jnp.where(low, pltpu.roll(q_t, head_dim, 1), v_t)
        wh[:, 2 * t * pair : (2 * t + 1) * pair] = first.astype(BF16)
        wh[:, (2 * t + 1) * pair : (2 * t + 2) * pair] = second.astype(BF16)

    def spread(phase, send, recv):
        for offset in order:
            peer = row_peer(offset)
            pltpu.make_async_remote_copy(
                src_ref=send.at[peer],
                dst_ref=recv.at[me],
                send_sem=a_send_sem.at[phase],
                recv_sem=a_recv_sem.at[phase],
                device_id=(block, peer),
                device_id_type=MESH,
            ).start()
        pltpu.make_async_copy(send.at[me], recv.at[me], l_sem.at[phase]).start()

    def arrived(phase, send, recv):
        rest = pl.ds(0, row_devices - 1)
        pltpu.make_async_copy(recv.at[rest], recv.at[rest], a_recv_sem.at[phase]).wait()
        pltpu.make_async_copy(send.at[me], recv.at[me], l_sem.at[phase]).wait()

    def left(phase, send):
        rest = pl.ds(0, row_devices - 1)
        pltpu.make_async_copy(send.at[rest], send.at[rest], a_send_sem.at[phase]).wait()

    def projected_heads(source, send, image):
        both = jnp.dot(source, wh[...], preferred_element_type=F32).astype(BF16)
        for h in range(heads):
            send[image * heads + h] = both[:, h * pair : (h + 1) * pair]

    for image in range(per_dev):
        projected_heads(xb[image], own_send, image)
    spread(0, own_send, own_recv)

    my_entries = entries_of(block)
    my_slots = []
    positions = [jnp.int32(0)] * edges
    for kind, offset in enumerate(OFFSETS):
        found, slots = slots_between(my_entries, img_peer(offset))
        my_slots.append([edge for edge, _ in slots])
        for e, (inside, rank) in enumerate(found):
            positions[e] = jnp.where(
                inside, kind * CAP + jnp.minimum(rank, CAP - 1), positions[e]
            )
    loads[1].wait()
    for load in loads[5:]:
        load.wait()

    hid[...] = (
        jnp.dot(
            xb[...].reshape(per_dev * rows, width),
            f1_ref[0:width, :],
            preferred_element_type=F32,
        )
        + b1_ref[...]
    )
    for h in range(heads):
        piece = wo_ref[h * head_dim : (h + 1) * head_dim, :]
        blank = jnp.zeros_like(piece)
        w2[h * pair : h * pair + head_dim, 0:width] = blank
        w2[h * pair : h * pair + head_dim, width : 2 * width] = piece
        w2[h * pair + head_dim : (h + 1) * pair, 0:width] = piece
        w2[h * pair + head_dim : (h + 1) * pair, width : 2 * width] = blank

    for copy in z_copies:
        copy.wait()
    for j in range(2):
        for image in range(per_dev):
            projected_heads(zrecv[positions[2 * image + j]], part_send.at[j], image)
        spread(1 + j, part_send.at[j], part_recv.at[j])

    chunk = min(256, keypoints)
    per_chunk = chunk // rows
    lane = lanes((keypoints, pair))
    place = lax.broadcasted_iota(jnp.int32, (keypoints, pair), 0)
    level = lax.broadcasted_iota(jnp.int32, (pair, keypoints), 0)

    def prepare(source, count, k_ref, q_ref, v_ref):
        flat = source[...].reshape(keypoints, pair)
        penalty = jnp.where((lane == head_dim) & (place >= count), PENALTY, 0.0)
        k_ref[...] = jnp.where(lane < head_dim, flat.astype(F32) * scale, penalty).astype(BF16)
        turned = flat.T
        one = jnp.ones((), BF16)
        q_ref[...] = jnp.where(level < head_dim, turned, one)
        v_ref[...] = jnp.where(level < head_dim, one, turned)

    def attend(work):
        low_half = lanes((chunk // 2, pair)) < head_dim
        steps = [(job, c) for job in work for c in range(keypoints // chunk)]

        def score(n):
            (k_ref, q_ref, _, _), c = steps[n]
            ahead[n % 2][...] = jnp.dot(
                k_ref[...], q_ref[:, c * chunk : (c + 1) * chunk], preferred_element_type=F32
            )

        score(0)
        for n, ((_, _, v_ref, finish), c) in enumerate(steps):
            if n + 1 < len(steps):
                score(n + 1)
            scores = ahead[n % 2][...]
            peak = jnp.max(scores, axis=0, keepdims=True)
            raised = jnp.exp(scores - peak).astype(BF16)
            total = jnp.dot(v_ref[...], raised, preferred_element_type=F32)
            message = (total / total[0:1, :]).T
            split = message.reshape(per_chunk, 2, half, pair)
            upper = split[:, 0].reshape(chunk // 2, pair)
            lower = pltpu.roll(split[:, 1].reshape(chunk // 2, pair), head_dim, 1)
            finish(c, jnp.where(low_half, lower, upper).reshape(per_chunk, half, pair))

    arrived(0, own_send, own_recv)
    prepare(own_recv, counts[block * per_dev + my_image], k_own, q_own, v_own)
    for j in range(2):
        arrived(1 + j, part_send.at[j], part_recv.at[j])
        asked = partners[j, block * per_dev + my_image]
        prepare(part_recv.at[j], counts[asked], k_part, q_part, v_part)

        def to_partner(c, message, j=j):
            ret_send[j, c * per_chunk : (c + 1) * per_chunk] = message.astype(BF16)
            if (c + 1) * chunk == keypoints:
                spread(3 + j, ret_send.at[j], msg_recv.at[j])

        def to_own(c, message, j=j):
            part = slice(c * per_chunk, (c + 1) * per_chunk)
            if j == 0:
                ret_acc[part] = message
            else:
                ret_send[2, part] = (ret_acc[part] + message).astype(BF16)

        attend(((k_own, q_part, v_own, to_partner), (k_part, q_own, v_part, to_own)))
    spread(5, ret_send.at[2], sum_recv)

    arrived(3, ret_send.at[0], msg_recv.at[0])
    arrived(4, ret_send.at[1], msg_recv.at[1])
    back_copies = []
    for kind, offset in enumerate(OFFSETS):
        for c in range(CAP):
            edge = jnp.maximum(my_slots[kind][c] - 1, 0)
            image, j = lax.div(edge, 2), lax.rem(edge, 2)
            back_send[kind, c] = msg_recv[j, pl.ds(image * heads, heads)]
        copy = pltpu.make_async_remote_copy(
            src_ref=back_send.at[kind],
            dst_ref=back_recv.at[kind],
            send_sem=b_send_sem.at[kind],
            recv_sem=b_recv_sem.at[kind],
            device_id=(img_peer(offset), me),
            device_id_type=MESH,
        )
        copy.start()
        back_copies.append(copy)

    arrived(5, ret_send.at[2], sum_recv)
    for copy in back_copies:
        copy.wait()

    packed = []
    for image in range(per_dev):
        inbox = sum_recv[image * heads : (image + 1) * heads].astype(F32)
        degree = jnp.int32(2)
        for kind in range(len(OFFSETS)):
            for c in range(CAP):
                hit = jnp.where(incoming_slots[kind][c] == image + 1, 1, 0)
                degree = degree + hit
                inbox = inbox + hit.astype(F32) * back_recv[kind, c].astype(F32)
        packed.append((inbox / degree.astype(F32)).astype(BF16))
    stacked = jnp.concatenate(
        [jnp.concatenate([packed[i][h] for i in range(per_dev)], axis=0) for h in range(heads)],
        axis=1,
    )
    both = jnp.dot(stacked, w2[...], preferred_element_type=F32).astype(BF16)
    for image in range(per_dev):
        mine = both[image * half : (image + 1) * half]
        proj[image * rows : image * rows + half, :] = mine[:, 0:width]
        proj[image * rows + half : (image + 1) * rows, :] = mine[:, width : 2 * width]

    stores = []
    for image in range(per_dev):
        part = pl.ds(image * rows, rows)
        hidden = hid[part, :] + jnp.dot(
            proj[part, :], f1_ref[width : 2 * width, :], preferred_element_type=F32
        )
        center = jnp.mean(hidden, axis=1, keepdims=True)
        away = hidden - center
        spreads = jnp.mean(away * away, axis=1, keepdims=True)
        normed = away * lax.rsqrt(spreads + 1e-5) * gain_ref[...] + nbias_ref[...]
        active = (0.5 * normed * (1.0 + lax.erf(normed * (0.5**0.5)))).astype(BF16)
        out_ref[image] = (
            x_ref[image]
            + jnp.dot(active, f2_ref[...], preferred_element_type=F32)
            + b2_ref[...]
        )
        stores.append(
            pltpu.make_async_copy(out_ref.at[image], out_hbm.at[image], out_sem.at[image])
        )
        stores[-1].start()

    for phase, send in (
        (0, own_send),
        (1, part_send.at[0]),
        (2, part_send.at[1]),
        (3, ret_send.at[0]),
        (4, ret_send.at[1]),
        (5, ret_send.at[2]),
    ):
        left(phase, send)
    for store in stores:
        store.wait()


def HEADS_OF(width):
    return width // 64


def per_device(
    features,
    partners,
    counts,
    shared_proj,
    value_proj,
    out_proj,
    ffn_in,
    ffn_in_bias,
    norm_gain,
    norm_bias,
    ffn_out,
    ffn_out_bias,
):
    img_count = lax.axis_size("img")
    row_devices = lax.axis_size("row")
    per_dev, rows, width = features.shape
    heads = HEADS_OF(width)
    head_dim = width // heads
    pair = 2 * head_dim
    keypoints = rows * row_devices
    hidden = ffn_in.shape[1]
    half = rows // 2
    kinds = len(OFFSETS)
    anywhere = pl.BlockSpec(memory_space=pl.ANY)
    return pl.pallas_call(
        functools.partial(kernel, img_count, row_devices),
        out_shape=jax.ShapeDtypeStruct(features.shape, F32),
        in_specs=[anywhere] * 12,
        out_specs=anywhere,
        scratch_shapes=[
            pltpu.SMEM(partners.shape[::-1], jnp.int32),
            pltpu.SMEM(counts.shape, jnp.int32),
            pltpu.VMEM(features.shape, F32),
            pltpu.VMEM(shared_proj.shape, BF16),
            pltpu.VMEM(value_proj.shape, BF16),
            pltpu.VMEM(out_proj.shape, BF16),
            pltpu.VMEM(ffn_in.shape, BF16),
            pltpu.VMEM((1, hidden), F32),
            pltpu.VMEM((1, hidden), F32),
            pltpu.VMEM((1, hidden), F32),
            pltpu.VMEM(ffn_out.shape, BF16),
            pltpu.VMEM((1, width), F32),
            pltpu.VMEM(features.shape, F32),
            pltpu.SemaphoreType.DMA((12,)),
            pltpu.SemaphoreType.DMA((per_dev,)),
            pltpu.VMEM((per_dev, rows, width), BF16),
            pltpu.VMEM((kinds, CAP, rows, width), BF16),
            pltpu.VMEM((width, 2 * width), BF16),
            pltpu.VMEM((heads * pair, 2 * width), BF16),
            pltpu.VMEM((per_dev * rows, hidden), F32),
            pltpu.VMEM((kinds * CAP, rows, width), BF16),
            pltpu.VMEM((row_devices, rows, pair), BF16),
            pltpu.VMEM((row_devices, rows, pair), BF16),
            pltpu.VMEM((2, row_devices, rows, pair), BF16),
            pltpu.VMEM((2, row_devices, rows, pair), BF16),
            pltpu.VMEM((keypoints, pair), BF16),
            pltpu.VMEM((pair, keypoints), BF16),
            pltpu.VMEM((pair, keypoints), BF16),
            pltpu.VMEM((keypoints, pair), BF16),
            pltpu.VMEM((pair, keypoints), BF16),
            pltpu.VMEM((pair, keypoints), BF16),
            pltpu.VMEM((keypoints, min(256, keypoints)), F32),
            pltpu.VMEM((keypoints, min(256, keypoints)), F32),
            pltpu.VMEM((row_devices, half, pair), F32),
            pltpu.VMEM((3, row_devices, half, pair), BF16),
            pltpu.VMEM((2, row_devices, half, pair), BF16),
            pltpu.VMEM((row_devices, half, pair), BF16),
            pltpu.VMEM((kinds, CAP, heads, half, pair), BF16),
            pltpu.VMEM((kinds, CAP, heads, half, pair), BF16),
            pltpu.VMEM((per_dev * rows, width), BF16),
            pltpu.SemaphoreType.DMA((kinds,)),
            pltpu.SemaphoreType.DMA((kinds,)),
            pltpu.SemaphoreType.DMA((6,)),
            pltpu.SemaphoreType.DMA((6,)),
            pltpu.SemaphoreType.DMA((6,)),
            pltpu.SemaphoreType.DMA((kinds,)),
            pltpu.SemaphoreType.DMA((kinds,)),
        ],
        compiler_params=pltpu.CompilerParams(
            collective_id=0, has_side_effects=True, vmem_limit_bytes=60 * 1024 * 1024
        ),
    )(
        partners.T,
        counts,
        features,
        shared_proj,
        value_proj,
        out_proj,
        ffn_in,
        ffn_in_bias.reshape(1, -1),
        norm_gain.reshape(1, -1),
        norm_bias.reshape(1, -1),
        ffn_out,
        ffn_out_bias.reshape(1, -1),
    )


def solution(mesh):
    return jax.shard_map(
        per_device,
        mesh=mesh,
        in_specs=(P("img", "row", None), P(), P(), P(), P(), P(), P(), P(), P(), P(), P(), P()),
        out_specs=P("img", "row", None),
        check_vma=False,
    )
```

```python
import functools

import jax
import jax.numpy as jnp
from jax import lax
from jax.experimental import pallas as pl
from jax.experimental.pallas import tpu as pltpu
from jax.sharding import PartitionSpec as P

HEADS = 4
CAP = 3
OFFSETS = (1, -1, 2, -2)
PENALTY = -1e30
MESH = pl.DeviceIdType.MESH
F32 = jnp.float32
BF16 = jnp.bfloat16


def far_first(count):
    return sorted(range(count), key=lambda step: (-min(step, count - step), step))


def lanes(shape):
    return lax.broadcasted_iota(jnp.int32, shape, len(shape) - 1)


def kernel(
    img_count,
    row_devices,
    partners_hbm,
    counts_hbm,
    x_hbm,
    wq_hbm,
    wv_hbm,
    wo_hbm,
    f1_hbm,
    b1_hbm,
    gain_hbm,
    nbias_hbm,
    f2_hbm,
    b2_hbm,
    out_hbm,
    partners,
    counts,
    x_ref,
    wq_ref,
    wv_ref,
    wo_ref,
    f1_ref,
    b1_ref,
    gain_ref,
    nbias_ref,
    f2_ref,
    b2_ref,
    out_ref,
    in_sem,
    out_sem,
    xb,
    zsend,
    wh,
    w2,
    hid,
    zrecv,
    own_send,
    own_recv,
    part_send,
    part_recv,
    k_own,
    q_own,
    v_own,
    k_part,
    q_part,
    v_part,
    ahead_even,
    ahead_odd,
    ret_acc,
    ret_send,
    msg_recv,
    sum_recv,
    back_send,
    back_recv,
    proj,
    z_send_sem,
    z_recv_sem,
    a_send_sem,
    a_recv_sem,
    l_sem,
    b_send_sem,
    b_recv_sem,
):
    per_dev, rows, width = x_ref.shape
    half = rows // 2
    head_dim = width // HEADS_OF(width)
    heads = width // head_dim
    pair = 2 * head_dim
    keypoints = rows * row_devices
    edges = 2 * per_dev
    scale = head_dim ** (-0.5)
    block = lax.axis_index("img")
    me = lax.axis_index("row")
    my_image = lax.div(me, heads)
    my_head = lax.rem(me, heads)
    ahead = (ahead_even, ahead_odd)
    rings = far_first(per_dev)

    def img_peer(offset):
        return lax.rem(block + (offset + img_count), img_count)

    def image_at(dy):
        return lax.rem(my_image + dy, per_dev)

    def line(dy):
        for dx in far_first(heads):
            if dy or dx:
                yield image_at(dy) * heads + lax.rem(my_head + dx, heads)

    loads = [
        pltpu.make_async_copy(source, target, in_sem.at[n])
        for n, (source, target) in enumerate(
            (
                (partners_hbm, partners),
                (counts_hbm, counts),
                (x_hbm, x_ref),
                (wq_hbm, wq_ref),
                (wv_hbm, wv_ref),
                (f1_hbm, f1_ref),
                (b1_hbm, b1_ref),
                (wo_hbm, wo_ref),
                (gain_hbm, gain_ref),
                (nbias_hbm, nbias_ref),
                (f2_hbm, f2_ref),
                (b2_hbm, b2_ref),
            )
        )
    ]
    for load in loads:
        load.start()

    barrier = pltpu.get_barrier_semaphore()
    for offset in OFFSETS:
        pl.semaphore_signal(barrier, inc=1, device_id=(img_peer(offset), me), device_id_type=MESH)
    for dy in rings:
        for peer in line(dy):
            pl.semaphore_signal(barrier, inc=1, device_id=(block, peer), device_id_type=MESH)

    def entries_of(home):
        return [partners[e % 2, home * per_dev + e // 2] for e in range(edges)]

    def slots_between(entries, target):
        found, count = [], jnp.int32(0)
        for entry in entries:
            inside = lax.div(entry, per_dev) == target
            found.append((inside, count))
            count = count + jnp.where(inside, 1, 0)
        slots = []
        for c in range(CAP):
            edge, image = jnp.int32(0), jnp.int32(0)
            for e, (inside, rank) in enumerate(found):
                here = inside & (rank == c)
                edge = jnp.where(here, e + 1, edge)
                image = jnp.where(here, lax.rem(entries[e], per_dev) + 1, image)
            slots.append((edge, image))
        return found, slots

    loads[0].wait()
    incoming_slots = []
    for kind, offset in enumerate(OFFSETS):
        _, slots = slots_between(entries_of(img_peer(-offset)), block)
        incoming_slots.append([image for _, image in slots])
    loads[2].wait()
    xb[...] = x_ref[...].astype(BF16)
    for kind in range(len(OFFSETS)):
        for c in range(CAP):
            zsend[kind, c] = xb[jnp.maximum(incoming_slots[kind][c] - 1, 0)]

    pl.semaphore_wait(barrier, len(OFFSETS) + row_devices - 1)

    z_copies = []
    for kind, offset in enumerate(OFFSETS):
        copy = pltpu.make_async_remote_copy(
            src_ref=zsend.at[kind],
            dst_ref=zrecv.at[pl.ds(kind * CAP, CAP)],
            send_sem=z_send_sem.at[kind],
            recv_sem=z_recv_sem.at[kind],
            device_id=(img_peer(-offset), me),
            device_id_type=MESH,
        )
        copy.start()
        z_copies.append(copy)

    loads[3].wait()
    loads[4].wait()
    low = lanes((width, pair)) < head_dim
    for t in range(width // pair):
        q_t = wq_ref[:, t * pair : (t + 1) * pair].astype(F32)
        v_t = wv_ref[:, t * pair : (t + 1) * pair].astype(F32)
        first = jnp.where(low, q_t, pltpu.roll(v_t, head_dim, 1))
        second = jnp.where(low, pltpu.roll(q_t, head_dim, 1), v_t)
        wh[:, 2 * t * pair : (2 * t + 1) * pair] = first.astype(BF16)
        wh[:, (2 * t + 1) * pair : (2 * t + 2) * pair] = second.astype(BF16)

    def spread(phase, send, recv, dy):
        for peer in line(dy):
            pltpu.make_async_remote_copy(
                src_ref=send.at[peer],
                dst_ref=recv.at[me],
                send_sem=a_send_sem.at[phase],
                recv_sem=a_recv_sem.at[phase],
                device_id=(block, peer),
                device_id_type=MESH,
            ).start()
        if dy == 0:
            pltpu.make_async_copy(send.at[me], recv.at[me], l_sem.at[phase]).start()

    def arrived(phase, send, recv):
        rest = pl.ds(0, row_devices - 1)
        pltpu.make_async_copy(recv.at[rest], recv.at[rest], a_recv_sem.at[phase]).wait()
        pltpu.make_async_copy(send.at[me], recv.at[me], l_sem.at[phase]).wait()

    def left(phase, send):
        rest = pl.ds(0, row_devices - 1)
        pltpu.make_async_copy(send.at[rest], send.at[rest], a_send_sem.at[phase]).wait()

    def projected_heads(source, send, image):
        both = jnp.dot(source, wh[...], preferred_element_type=F32).astype(BF16)
        for h in range(heads):
            send[image * heads + h] = both[:, h * pair : (h + 1) * pair]

    for dy in rings:
        image = image_at(dy)
        projected_heads(xb[image], own_send, image)
        spread(0, own_send, own_recv, dy)

    my_entries = entries_of(block)
    my_slots = []
    positions = [jnp.int32(0)] * edges
    for kind, offset in enumerate(OFFSETS):
        found, slots = slots_between(my_entries, img_peer(offset))
        my_slots.append([edge for edge, _ in slots])
        for e, (inside, rank) in enumerate(found):
            positions[e] = jnp.where(
                inside, kind * CAP + jnp.minimum(rank, CAP - 1), positions[e]
            )
    loads[1].wait()
    for load in loads[5:]:
        load.wait()

    hid[...] = (
        jnp.dot(
            xb[...].reshape(per_dev * rows, width),
            f1_ref[0:width, :],
            preferred_element_type=F32,
        )
        + b1_ref[...]
    )
    for h in range(heads):
        piece = wo_ref[h * head_dim : (h + 1) * head_dim, :]
        blank = jnp.zeros_like(piece)
        w2[h * pair : h * pair + head_dim, 0:width] = blank
        w2[h * pair : h * pair + head_dim, width : 2 * width] = piece
        w2[h * pair + head_dim : (h + 1) * pair, 0:width] = piece
        w2[h * pair + head_dim : (h + 1) * pair, width : 2 * width] = blank

    for copy in z_copies:
        copy.wait()
    for j in range(2):
        for dy in rings:
            image = image_at(dy)
            at = positions[j]
            for other in range(1, per_dev):
                at = jnp.where(image == other, positions[2 * other + j], at)
            projected_heads(zrecv[at], part_send.at[j], image)
            spread(1 + j, part_send.at[j], part_recv.at[j], dy)

    chunk = rows * heads
    lane = lanes((keypoints, pair))
    place = lax.broadcasted_iota(jnp.int32, (keypoints, pair), 0)
    level = lax.broadcasted_iota(jnp.int32, (pair, keypoints), 0)

    def prepare(source, count, k_ref, q_ref, v_ref):
        flat = source[...].reshape(keypoints, pair)
        penalty = jnp.where((lane == head_dim) & (place >= count), PENALTY, 0.0)
        k_ref[...] = jnp.where(lane < head_dim, flat.astype(F32) * scale, penalty).astype(BF16)
        turned = flat.T
        one = jnp.ones((), BF16)
        q_ref[...] = jnp.where(level < head_dim, turned, one)
        v_ref[...] = jnp.where(level < head_dim, one, turned)

    def attend(work):
        low_half = lanes((chunk // 2, pair)) < head_dim
        steps = [(job, dy) for job in work for dy in rings]

        def score(n):
            (k_ref, q_ref, _, _), dy = steps[n]
            part = pl.ds(pl.multiple_of(image_at(dy) * chunk, chunk), chunk)
            ahead[n % 2][...] = jnp.dot(
                k_ref[...], q_ref[:, part], preferred_element_type=F32
            )

        score(0)
        for n, ((_, _, v_ref, finish), dy) in enumerate(steps):
            if n + 1 < len(steps):
                score(n + 1)
            scores = ahead[n % 2][...]
            peak = jnp.max(scores, axis=0, keepdims=True)
            raised = jnp.exp(scores - peak).astype(BF16)
            total = jnp.dot(v_ref[...], raised, preferred_element_type=F32)
            message = (total / total[0:1, :]).T
            split = message.reshape(heads, 2, half, pair)
            upper = split[:, 0].reshape(chunk // 2, pair)
            lower = pltpu.roll(split[:, 1].reshape(chunk // 2, pair), head_dim, 1)
            finish(dy, jnp.where(low_half, lower, upper).reshape(heads, half, pair))

    arrived(0, own_send, own_recv)
    prepare(own_recv, counts[block * per_dev + my_image], k_own, q_own, v_own)
    for j in range(2):
        arrived(1 + j, part_send.at[j], part_recv.at[j])
        asked = partners[j, block * per_dev + my_image]
        prepare(part_recv.at[j], counts[asked], k_part, q_part, v_part)

        def to_partner(dy, message, j=j):
            ret_send[j, pl.ds(image_at(dy) * heads, heads)] = message.astype(BF16)
            spread(3 + j, ret_send.at[j], msg_recv.at[j], dy)

        def to_own(dy, message, j=j):
            part = pl.ds(image_at(dy) * heads, heads)
            if j == 0:
                ret_acc[part] = message
            else:
                ret_send[2, part] = (ret_acc[part] + message).astype(BF16)
                spread(5, ret_send.at[2], sum_recv, dy)

        attend(((k_own, q_part, v_own, to_partner), (k_part, q_own, v_part, to_own)))

    arrived(3, ret_send.at[0], msg_recv.at[0])
    arrived(4, ret_send.at[1], msg_recv.at[1])
    back_copies = []
    for kind, offset in enumerate(OFFSETS):
        for c in range(CAP):
            edge = jnp.maximum(my_slots[kind][c] - 1, 0)
            image, j = lax.div(edge, 2), lax.rem(edge, 2)
            back_send[kind, c] = msg_recv[j, pl.ds(image * heads, heads)]
        copy = pltpu.make_async_remote_copy(
            src_ref=back_send.at[kind],
            dst_ref=back_recv.at[kind],
            send_sem=b_send_sem.at[kind],
            recv_sem=b_recv_sem.at[kind],
            device_id=(img_peer(offset), me),
            device_id_type=MESH,
        )
        copy.start()
        back_copies.append(copy)

    arrived(5, ret_send.at[2], sum_recv)
    for copy in back_copies:
        copy.wait()

    packed = []
    for image in range(per_dev):
        inbox = sum_recv[image * heads : (image + 1) * heads].astype(F32)
        degree = jnp.int32(2)
        for kind in range(len(OFFSETS)):
            for c in range(CAP):
                hit = jnp.where(incoming_slots[kind][c] == image + 1, 1, 0)
                degree = degree + hit
                inbox = inbox + hit.astype(F32) * back_recv[kind, c].astype(F32)
        packed.append((inbox / degree.astype(F32)).astype(BF16))
    stacked = jnp.concatenate(
        [jnp.concatenate([packed[i][h] for i in range(per_dev)], axis=0) for h in range(heads)],
        axis=1,
    )
    both = jnp.dot(stacked, w2[...], preferred_element_type=F32).astype(BF16)
    for image in range(per_dev):
        mine = both[image * half : (image + 1) * half]
        proj[image * rows : image * rows + half, :] = mine[:, 0:width]
        proj[image * rows + half : (image + 1) * rows, :] = mine[:, width : 2 * width]

    stores = []
    for image in range(per_dev):
        part = pl.ds(image * rows, rows)
        hidden = hid[part, :] + jnp.dot(
            proj[part, :], f1_ref[width : 2 * width, :], preferred_element_type=F32
        )
        center = jnp.mean(hidden, axis=1, keepdims=True)
        away = hidden - center
        spreads = jnp.mean(away * away, axis=1, keepdims=True)
        normed = away * lax.rsqrt(spreads + 1e-5) * gain_ref[...] + nbias_ref[...]
        active = (0.5 * normed * (1.0 + lax.erf(normed * (0.5**0.5)))).astype(BF16)
        out_ref[image] = (
            jnp.dot(active, f2_ref[...], preferred_element_type=F32) + b2_ref[...]
        )
        stores.append(
            pltpu.make_async_copy(out_ref.at[image], out_hbm.at[image], out_sem.at[image])
        )
        stores[-1].start()

    for phase, send in (
        (0, own_send),
        (1, part_send.at[0]),
        (2, part_send.at[1]),
        (3, ret_send.at[0]),
        (4, ret_send.at[1]),
        (5, ret_send.at[2]),
    ):
        left(phase, send)
    for store in stores:
        store.wait()


def HEADS_OF(width):
    return width // 64


def per_device(
    features,
    partners,
    counts,
    shared_proj,
    value_proj,
    out_proj,
    ffn_in,
    ffn_in_bias,
    norm_gain,
    norm_bias,
    ffn_out,
    ffn_out_bias,
):
    img_count = lax.axis_size("img")
    row_devices = lax.axis_size("row")
    per_dev, rows, width = features.shape
    heads = HEADS_OF(width)
    head_dim = width // heads
    pair = 2 * head_dim
    keypoints = rows * row_devices
    hidden = ffn_in.shape[1]
    half = rows // 2
    kinds = len(OFFSETS)
    anywhere = pl.BlockSpec(memory_space=pl.ANY)
    update = pl.pallas_call(
        functools.partial(kernel, img_count, row_devices),
        out_shape=jax.ShapeDtypeStruct(features.shape, F32),
        in_specs=[anywhere] * 12,
        out_specs=anywhere,
        scratch_shapes=[
            pltpu.SMEM(partners.shape[::-1], jnp.int32),
            pltpu.SMEM(counts.shape, jnp.int32),
            pltpu.VMEM(features.shape, F32),
            pltpu.VMEM(shared_proj.shape, BF16),
            pltpu.VMEM(value_proj.shape, BF16),
            pltpu.VMEM(out_proj.shape, BF16),
            pltpu.VMEM(ffn_in.shape, BF16),
            pltpu.VMEM((1, hidden), F32),
            pltpu.VMEM((1, hidden), F32),
            pltpu.VMEM((1, hidden), F32),
            pltpu.VMEM(ffn_out.shape, BF16),
            pltpu.VMEM((1, width), F32),
            pltpu.VMEM(features.shape, F32),
            pltpu.SemaphoreType.DMA((12,)),
            pltpu.SemaphoreType.DMA((per_dev,)),
            pltpu.VMEM((per_dev, rows, width), BF16),
            pltpu.VMEM((kinds, CAP, rows, width), BF16),
            pltpu.VMEM((width, 2 * width), BF16),
            pltpu.VMEM((heads * pair, 2 * width), BF16),
            pltpu.VMEM((per_dev * rows, hidden), F32),
            pltpu.VMEM((kinds * CAP, rows, width), BF16),
            pltpu.VMEM((row_devices, rows, pair), BF16),
            pltpu.VMEM((row_devices, rows, pair), BF16),
            pltpu.VMEM((2, row_devices, rows, pair), BF16),
            pltpu.VMEM((2, row_devices, rows, pair), BF16),
            pltpu.VMEM((keypoints, pair), BF16),
            pltpu.VMEM((pair, keypoints), BF16),
            pltpu.VMEM((pair, keypoints), BF16),
            pltpu.VMEM((keypoints, pair), BF16),
            pltpu.VMEM((pair, keypoints), BF16),
            pltpu.VMEM((pair, keypoints), BF16),
            pltpu.VMEM((keypoints, rows * heads), F32),
            pltpu.VMEM((keypoints, rows * heads), F32),
            pltpu.VMEM((row_devices, half, pair), F32),
            pltpu.VMEM((3, row_devices, half, pair), BF16),
            pltpu.VMEM((2, row_devices, half, pair), BF16),
            pltpu.VMEM((row_devices, half, pair), BF16),
            pltpu.VMEM((kinds, CAP, heads, half, pair), BF16),
            pltpu.VMEM((kinds, CAP, heads, half, pair), BF16),
            pltpu.VMEM((per_dev * rows, width), BF16),
            pltpu.SemaphoreType.DMA((kinds,)),
            pltpu.SemaphoreType.DMA((kinds,)),
            pltpu.SemaphoreType.DMA((6,)),
            pltpu.SemaphoreType.DMA((6,)),
            pltpu.SemaphoreType.DMA((6,)),
            pltpu.SemaphoreType.DMA((kinds,)),
            pltpu.SemaphoreType.DMA((kinds,)),
        ],
        compiler_params=pltpu.CompilerParams(
            collective_id=0, has_side_effects=True, vmem_limit_bytes=60 * 1024 * 1024
        ),
    )(
        partners.T,
        counts,
        features,
        shared_proj,
        value_proj,
        out_proj,
        ffn_in,
        ffn_in_bias.reshape(1, -1),
        norm_gain.reshape(1, -1),
        norm_bias.reshape(1, -1),
        ffn_out,
        ffn_out_bias.reshape(1, -1),
    )
    return features + update


def solution(mesh):
    return jax.shard_map(
        per_device,
        mesh=mesh,
        in_specs=(P("img", "row", None), P(), P(), P(), P(), P(), P(), P(), P(), P(), P(), P()),
        out_specs=P("img", "row", None),
        check_vma=False,
    )
```

```python
import functools

import jax
import jax.numpy as jnp
from jax import lax
from jax.experimental import pallas as pl
from jax.experimental.pallas import tpu as pltpu
from jax.sharding import PartitionSpec as P

HEADS = 4
CAP = 3
OFFSETS = (1, -1, 2, -2)
PENALTY = -1e30
MESH = pl.DeviceIdType.MESH
F32 = jnp.float32
BF16 = jnp.bfloat16


def far_first(count):
    return sorted(range(count), key=lambda step: (-min(step, count - step), step))


def lanes(shape):
    return lax.broadcasted_iota(jnp.int32, shape, len(shape) - 1)


def kernel(
    img_count,
    row_devices,
    partners_hbm,
    counts_hbm,
    x_hbm,
    wq_hbm,
    wv_hbm,
    wo_hbm,
    f1_hbm,
    b1_hbm,
    gain_hbm,
    nbias_hbm,
    f2_hbm,
    b2_hbm,
    out_hbm,
    partners,
    counts,
    x_ref,
    wq_ref,
    wv_ref,
    wo_ref,
    f1_ref,
    b1_ref,
    gain_ref,
    nbias_ref,
    f2_ref,
    b2_ref,
    out_ref,
    in_sem,
    out_sem,
    xb,
    zsend,
    wh,
    w2,
    hid,
    zrecv,
    own_send,
    own_recv,
    part_send,
    part_recv,
    k_own,
    q_own,
    v_own,
    k_part,
    v_part,
    ahead_even,
    ahead_odd,
    ret_acc,
    ret_send,
    msg_recv,
    sum_recv,
    back_send,
    back_recv,
    proj,
    z_send_sem,
    z_recv_sem,
    a_send_sem,
    a_recv_sem,
    p_recv_sem,
    l_sem,
    b_send_sem,
    b_recv_sem,
):
    per_dev, rows, width = x_ref.shape
    half = rows // 2
    head_dim = width // HEADS_OF(width)
    heads = width // head_dim
    pair = 2 * head_dim
    keypoints = rows * row_devices
    edges = 2 * per_dev
    scale = head_dim ** (-0.5)
    block = lax.axis_index("img")
    me = lax.axis_index("row")
    my_image = lax.div(me, heads)
    my_head = lax.rem(me, heads)
    ahead = (ahead_even, ahead_odd)
    rings = far_first(per_dev)

    def img_peer(offset):
        return lax.rem(block + (offset + img_count), img_count)

    def image_at(dy):
        return lax.rem(my_image + dy, per_dev)

    def line(dy):
        for dx in far_first(heads):
            if dy or dx:
                yield image_at(dy) * heads + lax.rem(my_head + dx, heads)

    loads = [
        pltpu.make_async_copy(source, target, in_sem.at[n])
        for n, (source, target) in enumerate(
            (
                (partners_hbm, partners),
                (counts_hbm, counts),
                (x_hbm, x_ref),
                (wq_hbm, wq_ref),
                (wv_hbm, wv_ref),
                (f1_hbm, f1_ref),
                (b1_hbm, b1_ref),
                (wo_hbm, wo_ref),
                (gain_hbm, gain_ref),
                (nbias_hbm, nbias_ref),
                (f2_hbm, f2_ref),
                (b2_hbm, b2_ref),
            )
        )
    ]
    for load in loads:
        load.start()

    barrier = pltpu.get_barrier_semaphore()
    for offset in OFFSETS:
        pl.semaphore_signal(barrier, inc=1, device_id=(img_peer(offset), me), device_id_type=MESH)
    for dy in rings:
        for peer in line(dy):
            pl.semaphore_signal(barrier, inc=1, device_id=(block, peer), device_id_type=MESH)

    def entries_of(home):
        return [partners[e % 2, home * per_dev + e // 2] for e in range(edges)]

    def slots_between(entries, target):
        found, count = [], jnp.int32(0)
        for entry in entries:
            inside = lax.div(entry, per_dev) == target
            found.append((inside, count))
            count = count + jnp.where(inside, 1, 0)
        slots = []
        for c in range(CAP):
            edge, image = jnp.int32(0), jnp.int32(0)
            for e, (inside, rank) in enumerate(found):
                here = inside & (rank == c)
                edge = jnp.where(here, e + 1, edge)
                image = jnp.where(here, lax.rem(entries[e], per_dev) + 1, image)
            slots.append((edge, image))
        return found, slots

    loads[0].wait()
    incoming_slots = []
    for kind, offset in enumerate(OFFSETS):
        _, slots = slots_between(entries_of(img_peer(-offset)), block)
        incoming_slots.append([image for _, image in slots])
    loads[2].wait()
    xb[...] = x_ref[...].astype(BF16)
    for kind in range(len(OFFSETS)):
        for c in range(CAP):
            zsend[kind, c] = xb[jnp.maximum(incoming_slots[kind][c] - 1, 0)]

    pl.semaphore_wait(barrier, len(OFFSETS) + row_devices - 1)

    z_copies = []
    for kind, offset in enumerate(OFFSETS):
        copy = pltpu.make_async_remote_copy(
            src_ref=zsend.at[kind],
            dst_ref=zrecv.at[pl.ds(kind * CAP, CAP)],
            send_sem=z_send_sem.at[kind],
            recv_sem=z_recv_sem.at[kind],
            device_id=(img_peer(-offset), me),
            device_id_type=MESH,
        )
        copy.start()
        z_copies.append(copy)

    loads[3].wait()
    loads[4].wait()
    low = lanes((width, pair)) < head_dim
    for t in range(width // pair):
        q_t = wq_ref[:, t * pair : (t + 1) * pair].astype(F32)
        v_t = wv_ref[:, t * pair : (t + 1) * pair].astype(F32)
        first = jnp.where(low, q_t, pltpu.roll(v_t, head_dim, 1))
        second = jnp.where(low, pltpu.roll(q_t, head_dim, 1), v_t)
        wh[:, 2 * t * pair : (2 * t + 1) * pair] = first.astype(BF16)
        wh[:, (2 * t + 1) * pair : (2 * t + 2) * pair] = second.astype(BF16)

    def spread(phase, send, recv, dy):
        for peer in line(dy):
            pltpu.make_async_remote_copy(
                src_ref=send.at[peer],
                dst_ref=recv.at[me],
                send_sem=a_send_sem.at[phase],
                recv_sem=(
                    p_recv_sem.at[phase - 1, dy] if phase in (1, 2) else a_recv_sem.at[phase]
                ),
                device_id=(block, peer),
                device_id_type=MESH,
            ).start()
        if dy == 0:
            pltpu.make_async_copy(send.at[me], recv.at[me], l_sem.at[phase]).start()

    def arrived(phase, send, recv):
        rest = pl.ds(0, row_devices - 1)
        pltpu.make_async_copy(recv.at[rest], recv.at[rest], a_recv_sem.at[phase]).wait()
        pltpu.make_async_copy(send.at[me], recv.at[me], l_sem.at[phase]).wait()

    def left(phase, send):
        rest = pl.ds(0, row_devices - 1)
        pltpu.make_async_copy(send.at[rest], send.at[rest], a_send_sem.at[phase]).wait()

    def projected_heads(source, send, image):
        both = jnp.dot(source, wh[...], preferred_element_type=F32).astype(BF16)
        for h in range(heads):
            send[image * heads + h] = both[:, h * pair : (h + 1) * pair]

    for dy in rings:
        image = image_at(dy)
        projected_heads(xb[image], own_send, image)
        spread(0, own_send, own_recv, dy)

    my_entries = entries_of(block)
    my_slots = []
    positions = [jnp.int32(0)] * edges
    for kind, offset in enumerate(OFFSETS):
        found, slots = slots_between(my_entries, img_peer(offset))
        my_slots.append([edge for edge, _ in slots])
        for e, (inside, rank) in enumerate(found):
            positions[e] = jnp.where(
                inside, kind * CAP + jnp.minimum(rank, CAP - 1), positions[e]
            )
    loads[1].wait()
    for load in loads[5:]:
        load.wait()

    hid[...] = (
        jnp.dot(
            xb[...].reshape(per_dev * rows, width),
            f1_ref[0:width, :],
            preferred_element_type=F32,
        )
        + b1_ref[...]
    )
    for h in range(heads):
        piece = wo_ref[h * head_dim : (h + 1) * head_dim, :]
        blank = jnp.zeros_like(piece)
        w2[h * pair : h * pair + head_dim, 0:width] = blank
        w2[h * pair : h * pair + head_dim, width : 2 * width] = piece
        w2[h * pair + head_dim : (h + 1) * pair, 0:width] = piece
        w2[h * pair + head_dim : (h + 1) * pair, width : 2 * width] = blank

    for copy in z_copies:
        copy.wait()
    for j in range(2):
        for dy in rings:
            image = image_at(dy)
            at = positions[j]
            for other in range(1, per_dev):
                at = jnp.where(image == other, positions[2 * other + j], at)
            projected_heads(zrecv[at], part_send.at[j], image)
            spread(1 + j, part_send.at[j], part_recv.at[j], dy)

    chunk = rows * heads
    def as_keys(flat, first, count):
        place = first + lax.broadcasted_iota(jnp.int32, flat.shape, 0)
        lane = lanes(flat.shape)
        penalty = jnp.where((lane == head_dim) & (place >= count), PENALTY, 0.0)
        return jnp.where(lane < head_dim, flat.astype(F32) * scale, penalty).astype(BF16)

    def turned(flat):
        across = flat.T
        level = lax.broadcasted_iota(jnp.int32, across.shape, 0)
        one = jnp.ones((), BF16)
        return jnp.where(level < head_dim, across, one), jnp.where(level < head_dim, one, across)

    def line_arrived(j, dy):
        count = heads if dy else heads - 1
        rest = part_recv.at[j].at[pl.ds(0, count)]
        pltpu.make_async_copy(rest, rest, p_recv_sem.at[j, dy]).wait()
        if dy == 0:
            pltpu.make_async_copy(
                part_send.at[j].at[me], part_recv.at[j].at[me], l_sem.at[1 + j]
            ).wait()

    def score(n):
        side, j, dy = steps[n]
        if side == "partner":
            line_arrived(j, dy)
            source = image_at(per_dev - dy)
            place = pl.ds(pl.multiple_of(source * chunk, chunk), chunk)
            flat = part_recv[j, pl.ds(source * heads, heads)].reshape(chunk, pair)
            k_part[j, place, :] = as_keys(flat, source * chunk, asked_counts[j])
            queries, values = turned(flat)
            v_part[j, :, place] = values
            keys = k_own[...]
        else:
            place = pl.ds(pl.multiple_of(image_at(dy) * chunk, chunk), chunk)
            queries = q_own[:, place]
            keys = k_part[j]
        ahead[n % 2][...] = jnp.dot(keys, queries, preferred_element_type=F32)

    low_half = lanes((chunk // 2, pair)) < head_dim

    def attend(n):
        side, j, dy = steps[n]
        values = v_own[...] if side == "partner" else v_part[j]
        scores = ahead[n % 2][...]
        peak = jnp.max(scores, axis=0, keepdims=True)
        raised = jnp.exp(scores - peak).astype(BF16)
        total = jnp.dot(values, raised, preferred_element_type=F32)
        split = (total / total[0:1, :]).T.reshape(heads, 2, half, pair)
        upper = split[:, 0].reshape(chunk // 2, pair)
        lower = pltpu.roll(split[:, 1].reshape(chunk // 2, pair), head_dim, 1)
        message = jnp.where(low_half, lower, upper).reshape(heads, half, pair)
        if side == "partner":
            ahead_by = (per_dev - dy) % per_dev
            ret_send[j, pl.ds(image_at(ahead_by) * heads, heads)] = message.astype(BF16)
            spread(3 + j, ret_send.at[j], msg_recv.at[j], ahead_by)
        else:
            part = pl.ds(image_at(dy) * heads, heads)
            if j == 0:
                ret_acc[part] = message
            else:
                ret_send[2, part] = (ret_acc[part] + message).astype(BF16)
                spread(5, ret_send.at[2], sum_recv, dy)

    steps = [(side, j, dy) for side in ("partner", "own") for j in range(2) for dy in rings]
    asked_counts = [counts[partners[j, block * per_dev + my_image]] for j in range(2)]
    arrived(0, own_send, own_recv)
    whole = own_recv[...].reshape(keypoints, pair)
    k_own[...] = as_keys(whole, 0, counts[block * per_dev + my_image])
    own_queries, own_values = turned(whole)
    q_own[...] = own_queries
    v_own[...] = own_values
    score(0)
    for n in range(len(steps)):
        if n + 1 < len(steps):
            score(n + 1)
        attend(n)

    arrived(3, ret_send.at[0], msg_recv.at[0])
    arrived(4, ret_send.at[1], msg_recv.at[1])
    back_copies = []
    for kind, offset in enumerate(OFFSETS):
        for c in range(CAP):
            edge = jnp.maximum(my_slots[kind][c] - 1, 0)
            image, j = lax.div(edge, 2), lax.rem(edge, 2)
            back_send[kind, c] = msg_recv[j, pl.ds(image * heads, heads)]
        copy = pltpu.make_async_remote_copy(
            src_ref=back_send.at[kind],
            dst_ref=back_recv.at[kind],
            send_sem=b_send_sem.at[kind],
            recv_sem=b_recv_sem.at[kind],
            device_id=(img_peer(offset), me),
            device_id_type=MESH,
        )
        copy.start()
        back_copies.append(copy)

    arrived(5, ret_send.at[2], sum_recv)
    for copy in back_copies:
        copy.wait()

    packed = []
    for image in range(per_dev):
        inbox = sum_recv[image * heads : (image + 1) * heads].astype(F32)
        degree = jnp.int32(2)
        for kind in range(len(OFFSETS)):
            for c in range(CAP):
                hit = jnp.where(incoming_slots[kind][c] == image + 1, 1, 0)
                degree = degree + hit
                inbox = inbox + hit.astype(F32) * back_recv[kind, c].astype(F32)
        packed.append((inbox / degree.astype(F32)).astype(BF16))
    stacked = jnp.concatenate(
        [jnp.concatenate([packed[i][h] for i in range(per_dev)], axis=0) for h in range(heads)],
        axis=1,
    )
    both = jnp.dot(stacked, w2[...], preferred_element_type=F32).astype(BF16)
    for image in range(per_dev):
        mine = both[image * half : (image + 1) * half]
        proj[image * rows : image * rows + half, :] = mine[:, 0:width]
        proj[image * rows + half : (image + 1) * rows, :] = mine[:, width : 2 * width]

    stores = []
    for image in range(per_dev):
        part = pl.ds(image * rows, rows)
        hidden = hid[part, :] + jnp.dot(
            proj[part, :], f1_ref[width : 2 * width, :], preferred_element_type=F32
        )
        center = jnp.mean(hidden, axis=1, keepdims=True)
        away = hidden - center
        spreads = jnp.mean(away * away, axis=1, keepdims=True)
        normed = away * lax.rsqrt(spreads + 1e-5) * gain_ref[...] + nbias_ref[...]
        active = (0.5 * normed * (1.0 + lax.erf(normed * (0.5**0.5)))).astype(BF16)
        out_ref[image] = (
            jnp.dot(active, f2_ref[...], preferred_element_type=F32) + b2_ref[...]
        )
        stores.append(
            pltpu.make_async_copy(out_ref.at[image], out_hbm.at[image], out_sem.at[image])
        )
        stores[-1].start()

    for phase, send in (
        (0, own_send),
        (1, part_send.at[0]),
        (2, part_send.at[1]),
        (3, ret_send.at[0]),
        (4, ret_send.at[1]),
        (5, ret_send.at[2]),
    ):
        left(phase, send)
    for store in stores:
        store.wait()


def HEADS_OF(width):
    return width // 64


def per_device(
    features,
    partners,
    counts,
    shared_proj,
    value_proj,
    out_proj,
    ffn_in,
    ffn_in_bias,
    norm_gain,
    norm_bias,
    ffn_out,
    ffn_out_bias,
):
    img_count = lax.axis_size("img")
    row_devices = lax.axis_size("row")
    per_dev, rows, width = features.shape
    heads = HEADS_OF(width)
    head_dim = width // heads
    pair = 2 * head_dim
    keypoints = rows * row_devices
    hidden = ffn_in.shape[1]
    half = rows // 2
    kinds = len(OFFSETS)
    anywhere = pl.BlockSpec(memory_space=pl.ANY)
    update = pl.pallas_call(
        functools.partial(kernel, img_count, row_devices),
        out_shape=jax.ShapeDtypeStruct(features.shape, F32),
        in_specs=[anywhere] * 12,
        out_specs=anywhere,
        scratch_shapes=[
            pltpu.SMEM(partners.shape[::-1], jnp.int32),
            pltpu.SMEM(counts.shape, jnp.int32),
            pltpu.VMEM(features.shape, F32),
            pltpu.VMEM(shared_proj.shape, BF16),
            pltpu.VMEM(value_proj.shape, BF16),
            pltpu.VMEM(out_proj.shape, BF16),
            pltpu.VMEM(ffn_in.shape, BF16),
            pltpu.VMEM((1, hidden), F32),
            pltpu.VMEM((1, hidden), F32),
            pltpu.VMEM((1, hidden), F32),
            pltpu.VMEM(ffn_out.shape, BF16),
            pltpu.VMEM((1, width), F32),
            pltpu.VMEM(features.shape, F32),
            pltpu.SemaphoreType.DMA((12,)),
            pltpu.SemaphoreType.DMA((per_dev,)),
            pltpu.VMEM((per_dev, rows, width), BF16),
            pltpu.VMEM((kinds, CAP, rows, width), BF16),
            pltpu.VMEM((width, 2 * width), BF16),
            pltpu.VMEM((heads * pair, 2 * width), BF16),
            pltpu.VMEM((per_dev * rows, hidden), F32),
            pltpu.VMEM((kinds * CAP, rows, width), BF16),
            pltpu.VMEM((row_devices, rows, pair), BF16),
            pltpu.VMEM((row_devices, rows, pair), BF16),
            pltpu.VMEM((2, row_devices, rows, pair), BF16),
            pltpu.VMEM((2, row_devices, rows, pair), BF16),
            pltpu.VMEM((keypoints, pair), BF16),
            pltpu.VMEM((pair, keypoints), BF16),
            pltpu.VMEM((pair, keypoints), BF16),
            pltpu.VMEM((2, keypoints, pair), BF16),
            pltpu.VMEM((2, pair, keypoints), BF16),
            pltpu.VMEM((keypoints, rows * heads), F32),
            pltpu.VMEM((keypoints, rows * heads), F32),
            pltpu.VMEM((row_devices, half, pair), F32),
            pltpu.VMEM((3, row_devices, half, pair), BF16),
            pltpu.VMEM((2, row_devices, half, pair), BF16),
            pltpu.VMEM((row_devices, half, pair), BF16),
            pltpu.VMEM((kinds, CAP, heads, half, pair), BF16),
            pltpu.VMEM((kinds, CAP, heads, half, pair), BF16),
            pltpu.VMEM((per_dev * rows, width), BF16),
            pltpu.SemaphoreType.DMA((kinds,)),
            pltpu.SemaphoreType.DMA((kinds,)),
            pltpu.SemaphoreType.DMA((6,)),
            pltpu.SemaphoreType.DMA((6,)),
            pltpu.SemaphoreType.DMA((2, per_dev)),
            pltpu.SemaphoreType.DMA((6,)),
            pltpu.SemaphoreType.DMA((kinds,)),
            pltpu.SemaphoreType.DMA((kinds,)),
        ],
        compiler_params=pltpu.CompilerParams(
            collective_id=0, has_side_effects=True, vmem_limit_bytes=60 * 1024 * 1024
        ),
    )(
        partners.T,
        counts,
        features,
        shared_proj,
        value_proj,
        out_proj,
        ffn_in,
        ffn_in_bias.reshape(1, -1),
        norm_gain.reshape(1, -1),
        norm_bias.reshape(1, -1),
        ffn_out,
        ffn_out_bias.reshape(1, -1),
    )
    return features + update


def solution(mesh):
    return jax.shard_map(
        per_device,
        mesh=mesh,
        in_specs=(P("img", "row", None), P(), P(), P(), P(), P(), P(), P(), P(), P(), P(), P()),
        out_specs=P("img", "row", None),
        check_vma=False,
    )
```

```python
import functools

import jax
import jax.numpy as jnp
from jax import lax
from jax.experimental import pallas as pl
from jax.experimental.pallas import tpu as pltpu
from jax.sharding import PartitionSpec as P

HEADS = 4
CAP = 3
OFFSETS = (1, -1, 2, -2)
PENALTY = -1e30
MESH = pl.DeviceIdType.MESH
F32 = jnp.float32
BF16 = jnp.bfloat16


def far_first(count):
    return sorted(range(count), key=lambda step: (-min(step, count - step), step))


def lanes(shape):
    return lax.broadcasted_iota(jnp.int32, shape, len(shape) - 1)


def kernel(
    img_count,
    row_devices,
    partners_hbm,
    counts_hbm,
    x_hbm,
    wq_hbm,
    wv_hbm,
    wo_hbm,
    f1_hbm,
    b1_hbm,
    gain_hbm,
    nbias_hbm,
    f2_hbm,
    b2_hbm,
    out_hbm,
    partners,
    counts,
    x_ref,
    wq_ref,
    wv_ref,
    wo_ref,
    f1_ref,
    b1_ref,
    gain_ref,
    nbias_ref,
    f2_ref,
    b2_ref,
    out_ref,
    in_sem,
    out_sem,
    xb,
    zsend,
    wh,
    w2,
    hid,
    zrecv_first,
    zrecv_second,
    own_send,
    own_recv,
    part_send,
    part_recv,
    k_own,
    q_own,
    v_own,
    k_part,
    v_part,
    ahead_even,
    ahead_odd,
    ret_acc,
    ret_send,
    msg_recv,
    sum_recv,
    back_send,
    back_recv,
    proj,
    z_send_sem,
    z_recv_sem,
    a_send_sem,
    a_recv_sem,
    p_recv_sem,
    l_sem,
    b_send_sem,
    b_recv_sem,
):
    per_dev, rows, width = x_ref.shape
    half = rows // 2
    head_dim = width // HEADS_OF(width)
    heads = width // head_dim
    pair = 2 * head_dim
    keypoints = rows * row_devices
    edges = 2 * per_dev
    scale = head_dim ** (-0.5)
    block = lax.axis_index("img")
    me = lax.axis_index("row")
    my_image = lax.div(me, heads)
    my_head = lax.rem(me, heads)
    ahead = (ahead_even, ahead_odd)
    rings = far_first(per_dev)
    zrecv = (zrecv_first, zrecv_second)

    def img_peer(offset):
        return lax.rem(block + (offset + img_count), img_count)

    def image_at(dy):
        return lax.rem(my_image + dy, per_dev)

    def line(dy):
        for dx in far_first(heads):
            if dy or dx:
                yield image_at(dy) * heads + lax.rem(my_head + dx, heads)

    loads = [
        pltpu.make_async_copy(source, target, in_sem.at[n])
        for n, (source, target) in enumerate(
            (
                (partners_hbm, partners),
                (counts_hbm, counts),
                (x_hbm, x_ref),
                (wq_hbm, wq_ref),
                (wv_hbm, wv_ref),
                (f1_hbm, f1_ref),
                (b1_hbm, b1_ref),
                (wo_hbm, wo_ref),
                (gain_hbm, gain_ref),
                (nbias_hbm, nbias_ref),
                (f2_hbm, f2_ref),
                (b2_hbm, b2_ref),
            )
        )
    ]
    for load in loads:
        load.start()

    barrier = pltpu.get_barrier_semaphore()
    for offset in OFFSETS:
        pl.semaphore_signal(barrier, inc=1, device_id=(img_peer(offset), me), device_id_type=MESH)
    for dy in rings:
        for peer in line(dy):
            pl.semaphore_signal(barrier, inc=1, device_id=(block, peer), device_id_type=MESH)

    def entries_of(home):
        return [partners[e % 2, home * per_dev + e // 2] for e in range(edges)]

    def slots_between(entries, target):
        found, count = [], jnp.int32(0)
        for entry in entries:
            inside = lax.div(entry, per_dev) == target
            found.append((inside, count))
            count = count + jnp.where(inside, 1, 0)
        slots = []
        for c in range(CAP):
            edge, image = jnp.int32(0), jnp.int32(0)
            for e, (inside, rank) in enumerate(found):
                here = inside & (rank == c)
                edge = jnp.where(here, e + 1, edge)
                image = jnp.where(here, lax.rem(entries[e], per_dev) + 1, image)
            slots.append((edge, image))
        return found, slots

    loads[0].wait()
    incoming_slots = []
    for kind, offset in enumerate(OFFSETS):
        _, slots = slots_between(entries_of(img_peer(-offset)), block)
        incoming_slots.append([image for _, image in slots])
    loads[2].wait()
    xb[...] = x_ref[...].astype(BF16)
    for part in range(2):
        for kind in range(len(OFFSETS)):
            for c in range(CAP):
                zsend[part, kind, c] = xb[
                    jnp.maximum(incoming_slots[kind][c] - 1, 0), part * half : (part + 1) * half
                ]

    pl.semaphore_wait(barrier, len(OFFSETS) + row_devices - 1)

    z_copies = []
    for part in range(2):
        for kind, offset in enumerate(OFFSETS):
            copy = pltpu.make_async_remote_copy(
                src_ref=zsend.at[part, kind],
                dst_ref=zrecv[part].at[pl.ds(kind * CAP, CAP)],
                send_sem=z_send_sem.at[part, kind],
                recv_sem=z_recv_sem.at[part, kind],
                device_id=(img_peer(-offset), me),
                device_id_type=MESH,
            )
            copy.start()
            z_copies.append(copy)

    loads[3].wait()
    loads[4].wait()
    low = lanes((width, pair)) < head_dim
    for t in range(width // pair):
        q_t = wq_ref[:, t * pair : (t + 1) * pair].astype(F32)
        v_t = wv_ref[:, t * pair : (t + 1) * pair].astype(F32)
        first = jnp.where(low, q_t, pltpu.roll(v_t, head_dim, 1))
        second = jnp.where(low, pltpu.roll(q_t, head_dim, 1), v_t)
        wh[:, 2 * t * pair : (2 * t + 1) * pair] = first.astype(BF16)
        wh[:, (2 * t + 1) * pair : (2 * t + 2) * pair] = second.astype(BF16)

    def spread(phase, send, recv, dy, rows_of=None):
        def block_of(ref, which):
            return ref.at[which] if rows_of is None else ref.at[which, rows_of]

        for peer in line(dy):
            pltpu.make_async_remote_copy(
                src_ref=block_of(send, peer),
                dst_ref=block_of(recv, me),
                send_sem=a_send_sem.at[phase],
                recv_sem=(
                    p_recv_sem.at[phase - 1, dy] if phase in (1, 2) else a_recv_sem.at[phase]
                ),
                device_id=(block, peer),
                device_id_type=MESH,
            ).start()
        if dy == 0:
            pltpu.make_async_copy(
                block_of(send, me), block_of(recv, me), l_sem.at[phase]
            ).start()

    def arrived(phase, send, recv):
        rest = pl.ds(0, row_devices - 1)
        pltpu.make_async_copy(recv.at[rest], recv.at[rest], a_recv_sem.at[phase]).wait()
        pltpu.make_async_copy(send.at[me], recv.at[me], l_sem.at[phase]).wait()

    def left(phase, send):
        rest = pl.ds(0, row_devices - 1)
        pltpu.make_async_copy(send.at[rest], send.at[rest], a_send_sem.at[phase]).wait()

    def projected_heads(source, send, image, rows_of):
        both = jnp.dot(source, wh[...], preferred_element_type=F32).astype(BF16)
        for h in range(heads):
            send[image * heads + h, rows_of] = both[:, h * pair : (h + 1) * pair]

    for dy in rings:
        image = image_at(dy)
        projected_heads(xb[image], own_send, image, pl.ds(0, rows))
        spread(0, own_send, own_recv, dy)

    my_entries = entries_of(block)
    my_slots = []
    positions = [jnp.int32(0)] * edges
    for kind, offset in enumerate(OFFSETS):
        found, slots = slots_between(my_entries, img_peer(offset))
        my_slots.append([edge for edge, _ in slots])
        for e, (inside, rank) in enumerate(found):
            positions[e] = jnp.where(
                inside, kind * CAP + jnp.minimum(rank, CAP - 1), positions[e]
            )
    loads[1].wait()
    for load in loads[5:]:
        load.wait()

    hid[...] = (
        jnp.dot(
            xb[...].reshape(per_dev * rows, width),
            f1_ref[0:width, :],
            preferred_element_type=F32,
        )
        + b1_ref[...]
    )
    for h in range(heads):
        piece = wo_ref[h * head_dim : (h + 1) * head_dim, :]
        blank = jnp.zeros_like(piece)
        w2[h * pair : h * pair + head_dim, 0:width] = blank
        w2[h * pair : h * pair + head_dim, width : 2 * width] = piece
        w2[h * pair + head_dim : (h + 1) * pair, 0:width] = piece
        w2[h * pair + head_dim : (h + 1) * pair, width : 2 * width] = blank

    for part in range(2):
        for kind in range(len(OFFSETS)):
            z_copies[part * len(OFFSETS) + kind].wait_recv()
        rows_of = pl.ds(part * half, half)
        for j in range(2):
            for dy in rings:
                image = image_at(dy)
                at = positions[j]
                for other in range(1, per_dev):
                    at = jnp.where(image == other, positions[2 * other + j], at)
                projected_heads(zrecv[part][at], part_send.at[j], image, rows_of)
                spread(1 + j, part_send.at[j], part_recv.at[j], dy, rows_of)

    chunk = rows * heads
    def as_keys(flat, first, count):
        place = first + lax.broadcasted_iota(jnp.int32, flat.shape, 0)
        lane = lanes(flat.shape)
        penalty = jnp.where((lane == head_dim) & (place >= count), PENALTY, 0.0)
        return jnp.where(lane < head_dim, flat.astype(F32) * scale, penalty).astype(BF16)

    def turned(flat):
        across = flat.T
        level = lax.broadcasted_iota(jnp.int32, across.shape, 0)
        one = jnp.ones((), BF16)
        return jnp.where(level < head_dim, across, one), jnp.where(level < head_dim, one, across)

    def line_arrived(j, dy):
        count = heads if dy else heads - 1
        rest = part_recv.at[j].at[pl.ds(0, count)]
        pltpu.make_async_copy(rest, rest, p_recv_sem.at[j, dy]).wait()
        if dy == 0:
            pltpu.make_async_copy(
                part_send.at[j].at[me], part_recv.at[j].at[me], l_sem.at[1 + j]
            ).wait()

    def score(n):
        side, j, dy = steps[n]
        if side == "partner":
            line_arrived(j, dy)
            source = image_at(per_dev - dy)
            place = pl.ds(pl.multiple_of(source * chunk, chunk), chunk)
            flat = part_recv[j, pl.ds(source * heads, heads)].reshape(chunk, pair)
            k_part[j, place, :] = as_keys(flat, source * chunk, asked_counts[j])
            queries, values = turned(flat)
            v_part[j, :, place] = values
            keys = k_own[...]
        else:
            place = pl.ds(pl.multiple_of(image_at(dy) * chunk, chunk), chunk)
            queries = q_own[:, place]
            keys = k_part[j]
        ahead[n % 2][...] = jnp.dot(keys, queries, preferred_element_type=F32)

    low_half = lanes((chunk // 2, pair)) < head_dim

    def attend(n):
        side, j, dy = steps[n]
        values = v_own[...] if side == "partner" else v_part[j]
        scores = ahead[n % 2][...]
        peak = jnp.max(scores, axis=0, keepdims=True)
        raised = jnp.exp(scores - peak).astype(BF16)
        total = jnp.dot(values, raised, preferred_element_type=F32)
        split = (total / total[0:1, :]).T.reshape(heads, 2, half, pair)
        upper = split[:, 0].reshape(chunk // 2, pair)
        lower = pltpu.roll(split[:, 1].reshape(chunk // 2, pair), head_dim, 1)
        message = jnp.where(low_half, lower, upper).reshape(heads, half, pair)
        if side == "partner":
            ahead_by = (per_dev - dy) % per_dev
            ret_send[j, pl.ds(image_at(ahead_by) * heads, heads)] = message.astype(BF16)
            spread(3 + j, ret_send.at[j], msg_recv.at[j], ahead_by)
        else:
            part = pl.ds(image_at(dy) * heads, heads)
            if j == 0:
                ret_acc[part] = message
            else:
                ret_send[2, part] = (ret_acc[part] + message).astype(BF16)
                spread(5, ret_send.at[2], sum_recv, dy)

    steps = [(side, j, dy) for side in ("partner", "own") for j in range(2) for dy in rings]
    asked_counts = [counts[partners[j, block * per_dev + my_image]] for j in range(2)]
    arrived(0, own_send, own_recv)
    whole = own_recv[...].reshape(keypoints, pair)
    k_own[...] = as_keys(whole, 0, counts[block * per_dev + my_image])
    own_queries, own_values = turned(whole)
    q_own[...] = own_queries
    v_own[...] = own_values
    score(0)
    for n in range(len(steps)):
        if n + 1 < len(steps):
            score(n + 1)
        attend(n)

    arrived(3, ret_send.at[0], msg_recv.at[0])
    arrived(4, ret_send.at[1], msg_recv.at[1])
    back_copies = []
    for kind, offset in enumerate(OFFSETS):
        for c in range(CAP):
            edge = jnp.maximum(my_slots[kind][c] - 1, 0)
            image, j = lax.div(edge, 2), lax.rem(edge, 2)
            back_send[kind, c] = msg_recv[j, pl.ds(image * heads, heads)]
        copy = pltpu.make_async_remote_copy(
            src_ref=back_send.at[kind],
            dst_ref=back_recv.at[kind],
            send_sem=b_send_sem.at[kind],
            recv_sem=b_recv_sem.at[kind],
            device_id=(img_peer(offset), me),
            device_id_type=MESH,
        )
        copy.start()
        back_copies.append(copy)

    arrived(5, ret_send.at[2], sum_recv)
    inboxes, degrees = [], []
    for image in range(per_dev):
        inboxes.append(sum_recv[image * heads : (image + 1) * heads].astype(F32))
        degree = jnp.int32(2)
        for slots in incoming_slots:
            for slot in slots:
                degree = degree + jnp.where(slot == image + 1, 1, 0)
        degrees.append(degree.astype(F32))
    for kind in range(len(OFFSETS)):
        back_copies[kind].wait_recv()
        for c in range(CAP):
            message = back_recv[kind, c].astype(F32)
            for image in range(per_dev):
                hit = jnp.where(incoming_slots[kind][c] == image + 1, 1.0, 0.0)
                inboxes[image] = inboxes[image] + hit * message
    packed = [
        (inbox / degree).astype(BF16) for inbox, degree in zip(inboxes, degrees, strict=True)
    ]
    stacked = jnp.concatenate(
        [jnp.concatenate([packed[i][h] for i in range(per_dev)], axis=0) for h in range(heads)],
        axis=1,
    )
    both = jnp.dot(stacked, w2[...], preferred_element_type=F32).astype(BF16)
    for image in range(per_dev):
        mine = both[image * half : (image + 1) * half]
        proj[image * rows : image * rows + half, :] = mine[:, 0:width]
        proj[image * rows + half : (image + 1) * rows, :] = mine[:, width : 2 * width]

    stores = []
    for image in range(per_dev):
        part = pl.ds(image * rows, rows)
        hidden = hid[part, :] + jnp.dot(
            proj[part, :], f1_ref[width : 2 * width, :], preferred_element_type=F32
        )
        center = jnp.mean(hidden, axis=1, keepdims=True)
        away = hidden - center
        spreads = jnp.mean(away * away, axis=1, keepdims=True)
        normed = away * lax.rsqrt(spreads + 1e-5) * gain_ref[...] + nbias_ref[...]
        active = (0.5 * normed * (1.0 + lax.erf(normed * (0.5**0.5)))).astype(BF16)
        out_ref[image] = (
            jnp.dot(active, f2_ref[...], preferred_element_type=F32) + b2_ref[...]
        )
        stores.append(
            pltpu.make_async_copy(out_ref.at[image], out_hbm.at[image], out_sem.at[image])
        )
        stores[-1].start()

    for phase, send in (
        (0, own_send),
        (1, part_send.at[0]),
        (2, part_send.at[1]),
        (3, ret_send.at[0]),
        (4, ret_send.at[1]),
        (5, ret_send.at[2]),
    ):
        left(phase, send)
    for copy in z_copies + back_copies:
        copy.wait_send()
    for store in stores:
        store.wait()


def HEADS_OF(width):
    return width // 64


def per_device(
    features,
    partners,
    counts,
    shared_proj,
    value_proj,
    out_proj,
    ffn_in,
    ffn_in_bias,
    norm_gain,
    norm_bias,
    ffn_out,
    ffn_out_bias,
):
    img_count = lax.axis_size("img")
    row_devices = lax.axis_size("row")
    per_dev, rows, width = features.shape
    heads = HEADS_OF(width)
    head_dim = width // heads
    pair = 2 * head_dim
    keypoints = rows * row_devices
    hidden = ffn_in.shape[1]
    half = rows // 2
    kinds = len(OFFSETS)
    anywhere = pl.BlockSpec(memory_space=pl.ANY)
    update = pl.pallas_call(
        functools.partial(kernel, img_count, row_devices),
        out_shape=jax.ShapeDtypeStruct(features.shape, F32),
        in_specs=[anywhere] * 12,
        out_specs=anywhere,
        scratch_shapes=[
            pltpu.SMEM(partners.shape[::-1], jnp.int32),
            pltpu.SMEM(counts.shape, jnp.int32),
            pltpu.VMEM(features.shape, F32),
            pltpu.VMEM(shared_proj.shape, BF16),
            pltpu.VMEM(value_proj.shape, BF16),
            pltpu.VMEM(out_proj.shape, BF16),
            pltpu.VMEM(ffn_in.shape, BF16),
            pltpu.VMEM((1, hidden), F32),
            pltpu.VMEM((1, hidden), F32),
            pltpu.VMEM((1, hidden), F32),
            pltpu.VMEM(ffn_out.shape, BF16),
            pltpu.VMEM((1, width), F32),
            pltpu.VMEM(features.shape, F32),
            pltpu.SemaphoreType.DMA((12,)),
            pltpu.SemaphoreType.DMA((per_dev,)),
            pltpu.VMEM((per_dev, rows, width), BF16),
            pltpu.VMEM((2, kinds, CAP, half, width), BF16),
            pltpu.VMEM((width, 2 * width), BF16),
            pltpu.VMEM((heads * pair, 2 * width), BF16),
            pltpu.VMEM((per_dev * rows, hidden), F32),
            pltpu.VMEM((kinds * CAP, half, width), BF16),
            pltpu.VMEM((kinds * CAP, half, width), BF16),
            pltpu.VMEM((row_devices, rows, pair), BF16),
            pltpu.VMEM((row_devices, rows, pair), BF16),
            pltpu.VMEM((2, row_devices, rows, pair), BF16),
            pltpu.VMEM((2, row_devices, rows, pair), BF16),
            pltpu.VMEM((keypoints, pair), BF16),
            pltpu.VMEM((pair, keypoints), BF16),
            pltpu.VMEM((pair, keypoints), BF16),
            pltpu.VMEM((2, keypoints, pair), BF16),
            pltpu.VMEM((2, pair, keypoints), BF16),
            pltpu.VMEM((keypoints, rows * heads), F32),
            pltpu.VMEM((keypoints, rows * heads), F32),
            pltpu.VMEM((row_devices, half, pair), F32),
            pltpu.VMEM((3, row_devices, half, pair), BF16),
            pltpu.VMEM((2, row_devices, half, pair), BF16),
            pltpu.VMEM((row_devices, half, pair), BF16),
            pltpu.VMEM((kinds, CAP, heads, half, pair), BF16),
            pltpu.VMEM((kinds, CAP, heads, half, pair), BF16),
            pltpu.VMEM((per_dev * rows, width), BF16),
            pltpu.SemaphoreType.DMA((2, kinds)),
            pltpu.SemaphoreType.DMA((2, kinds)),
            pltpu.SemaphoreType.DMA((6,)),
            pltpu.SemaphoreType.DMA((6,)),
            pltpu.SemaphoreType.DMA((2, per_dev)),
            pltpu.SemaphoreType.DMA((6,)),
            pltpu.SemaphoreType.DMA((kinds,)),
            pltpu.SemaphoreType.DMA((kinds,)),
        ],
        compiler_params=pltpu.CompilerParams(
            collective_id=0, has_side_effects=True, vmem_limit_bytes=60 * 1024 * 1024
        ),
    )(
        partners.T,
        counts,
        features,
        shared_proj,
        value_proj,
        out_proj,
        ffn_in,
        ffn_in_bias.reshape(1, -1),
        norm_gain.reshape(1, -1),
        norm_bias.reshape(1, -1),
        ffn_out,
        ffn_out_bias.reshape(1, -1),
    )
    return features + update


def solution(mesh):
    return jax.shard_map(
        per_device,
        mesh=mesh,
        in_specs=(P("img", "row", None), P(), P(), P(), P(), P(), P(), P(), P(), P(), P(), P()),
        out_specs=P("img", "row", None),
        check_vma=False,
    )
```

```python
import functools

import jax
import jax.numpy as jnp
from jax import lax
from jax.experimental import pallas as pl
from jax.experimental.pallas import tpu as pltpu
from jax.sharding import PartitionSpec as P

HEADS = 4
CAP = 3
OFFSETS = (1, -1, 2, -2)
PENALTY = -1e30
MESH = pl.DeviceIdType.MESH
F32 = jnp.float32
BF16 = jnp.bfloat16


def far_first(count):
    return sorted(range(count), key=lambda step: (-min(step, count - step), step))


def lanes(shape):
    return lax.broadcasted_iota(jnp.int32, shape, len(shape) - 1)


def kernel(
    img_count,
    row_devices,
    partners_hbm,
    counts_hbm,
    x_hbm,
    wq_hbm,
    wv_hbm,
    wo_hbm,
    f1_hbm,
    b1_hbm,
    gain_hbm,
    nbias_hbm,
    f2_hbm,
    b2_hbm,
    out_hbm,
    partners,
    counts,
    x_ref,
    wq_ref,
    wv_ref,
    wo_ref,
    f1_ref,
    b1_ref,
    gain_ref,
    nbias_ref,
    f2_ref,
    b2_ref,
    out_ref,
    in_sem,
    out_sem,
    xb,
    zsend,
    wh,
    w2,
    hid,
    zrecv_first,
    zrecv_second,
    own_send,
    own_recv,
    part_send,
    part_recv,
    k_own,
    q_own,
    v_own,
    k_part,
    v_part,
    ahead_even,
    ahead_odd,
    ret_acc,
    ret_send,
    msg_recv,
    sum_recv,
    back_send,
    back_recv,
    proj,
    z_send_sem,
    z_recv_sem,
    a_send_sem,
    a_recv_sem,
    p_recv_sem,
    l_sem,
    b_send_sem,
    b_recv_sem,
):
    per_dev, rows, width = x_ref.shape
    half = rows // 2
    head_dim = width // HEADS_OF(width)
    heads = width // head_dim
    pair = 2 * head_dim
    keypoints = rows * row_devices
    edges = 2 * per_dev
    scale = head_dim ** (-0.5)
    block = lax.axis_index("img")
    me = lax.axis_index("row")
    my_image = lax.div(me, heads)
    my_head = lax.rem(me, heads)
    ahead = (ahead_even, ahead_odd)
    rings = far_first(per_dev)
    zrecv = (zrecv_first, zrecv_second)

    def img_peer(offset):
        return lax.rem(block + (offset + img_count), img_count)

    def image_at(dy):
        return lax.rem(my_image + dy, per_dev)

    def line(dy):
        for dx in far_first(heads):
            if dy or dx:
                yield image_at(dy) * heads + lax.rem(my_head + dx, heads)

    loads = [
        pltpu.make_async_copy(source, target, in_sem.at[n])
        for n, (source, target) in enumerate(
            (
                (partners_hbm, partners),
                (counts_hbm, counts),
                (x_hbm, x_ref),
                (wq_hbm, wq_ref),
                (wv_hbm, wv_ref),
                (f1_hbm, f1_ref),
                (b1_hbm, b1_ref),
                (wo_hbm, wo_ref),
                (gain_hbm, gain_ref),
                (nbias_hbm, nbias_ref),
                (f2_hbm, f2_ref),
                (b2_hbm, b2_ref),
            )
        )
    ]
    for load in loads:
        load.start()

    barrier = pltpu.get_barrier_semaphore()
    for offset in OFFSETS:
        pl.semaphore_signal(barrier, inc=1, device_id=(img_peer(offset), me), device_id_type=MESH)
    for dy in rings:
        for peer in line(dy):
            pl.semaphore_signal(barrier, inc=1, device_id=(block, peer), device_id_type=MESH)

    def entries_of(home):
        return [partners[e % 2, home * per_dev + e // 2] for e in range(edges)]

    def slots_between(entries, target):
        found, count = [], jnp.int32(0)
        for entry in entries:
            inside = lax.div(entry, per_dev) == target
            found.append((inside, count))
            count = count + jnp.where(inside, 1, 0)
        slots = []
        for c in range(CAP):
            edge, image = jnp.int32(0), jnp.int32(0)
            for e, (inside, rank) in enumerate(found):
                here = inside & (rank == c)
                edge = jnp.where(here, e + 1, edge)
                image = jnp.where(here, lax.rem(entries[e], per_dev) + 1, image)
            slots.append((edge, image))
        return found, slots

    loads[0].wait()
    incoming_slots = []
    for kind, offset in enumerate(OFFSETS):
        _, slots = slots_between(entries_of(img_peer(-offset)), block)
        incoming_slots.append([image for _, image in slots])
    loads[2].wait()
    xb[...] = x_ref[...].astype(BF16)
    for part in range(2):
        for kind in range(len(OFFSETS)):
            for c in range(CAP):
                zsend[part, kind, c] = xb[
                    jnp.maximum(incoming_slots[kind][c] - 1, 0), part * half : (part + 1) * half
                ]

    pl.semaphore_wait(barrier, len(OFFSETS) + row_devices - 1)

    z_copies = []
    for part in range(2):
        for kind, offset in enumerate(OFFSETS):
            copy = pltpu.make_async_remote_copy(
                src_ref=zsend.at[part, kind],
                dst_ref=zrecv[part].at[pl.ds(kind * CAP, CAP)],
                send_sem=z_send_sem.at[part, kind],
                recv_sem=z_recv_sem.at[part, kind],
                device_id=(img_peer(-offset), me),
                device_id_type=MESH,
            )
            copy.start()
            z_copies.append(copy)

    loads[3].wait()
    loads[4].wait()
    low = lanes((width, pair)) < head_dim
    for t in range(width // pair):
        q_t = wq_ref[:, t * pair : (t + 1) * pair].astype(F32)
        v_t = wv_ref[:, t * pair : (t + 1) * pair].astype(F32)
        first = jnp.where(low, q_t, pltpu.roll(v_t, head_dim, 1))
        second = jnp.where(low, pltpu.roll(q_t, head_dim, 1), v_t)
        wh[:, 2 * t * pair : (2 * t + 1) * pair] = first.astype(BF16)
        wh[:, (2 * t + 1) * pair : (2 * t + 2) * pair] = second.astype(BF16)

    def spread(phase, send, recv, dy, rows_of=None):
        def block_of(ref, which):
            return ref.at[which] if rows_of is None else ref.at[which, rows_of]

        for peer in line(dy):
            pltpu.make_async_remote_copy(
                src_ref=block_of(send, peer),
                dst_ref=block_of(recv, me),
                send_sem=a_send_sem.at[phase],
                recv_sem=(
                    p_recv_sem.at[dy] if phase == 1 else a_recv_sem.at[phase]
                ),
                device_id=(block, peer),
                device_id_type=MESH,
            ).start()
        if dy == 0:
            pltpu.make_async_copy(
                block_of(send, me), block_of(recv, me), l_sem.at[phase]
            ).start()

    def arrived(phase, send, recv):
        rest = pl.ds(0, row_devices - 1)
        pltpu.make_async_copy(recv.at[rest], recv.at[rest], a_recv_sem.at[phase]).wait()
        pltpu.make_async_copy(send.at[me], recv.at[me], l_sem.at[phase]).wait()

    def left(phase, send):
        rest = pl.ds(0, row_devices - 1)
        pltpu.make_async_copy(send.at[rest], send.at[rest], a_send_sem.at[phase]).wait()

    def projected_heads(source, send, image, rows_of):
        both = jnp.dot(source, wh[...], preferred_element_type=F32).astype(BF16)
        for h in range(heads):
            send[image * heads + h, rows_of] = both[:, h * pair : (h + 1) * pair]

    for dy in rings:
        image = image_at(dy)
        projected_heads(xb[image], own_send, image, pl.ds(0, rows))
        spread(0, own_send, own_recv, dy)

    my_entries = entries_of(block)
    my_slots = []
    positions = [jnp.int32(0)] * edges
    for kind, offset in enumerate(OFFSETS):
        found, slots = slots_between(my_entries, img_peer(offset))
        my_slots.append([edge for edge, _ in slots])
        for e, (inside, rank) in enumerate(found):
            positions[e] = jnp.where(
                inside, kind * CAP + jnp.minimum(rank, CAP - 1), positions[e]
            )
    loads[1].wait()
    for load in loads[5:]:
        load.wait()

    hid[...] = (
        jnp.dot(
            xb[...].reshape(per_dev * rows, width),
            f1_ref[0:width, :],
            preferred_element_type=F32,
        )
        + b1_ref[...]
    )
    for h in range(heads):
        piece = wo_ref[h * head_dim : (h + 1) * head_dim, :]
        blank = jnp.zeros_like(piece)
        w2[h * pair : h * pair + head_dim, 0:width] = blank
        w2[h * pair : h * pair + head_dim, width : 2 * width] = piece
        w2[h * pair + head_dim : (h + 1) * pair, 0:width] = piece
        w2[h * pair + head_dim : (h + 1) * pair, width : 2 * width] = blank

    low_rows = lanes((half, pair)) < head_dim
    for part in range(2):
        for kind in range(len(OFFSETS)):
            z_copies[part * len(OFFSETS) + kind].wait_recv()
        rows_of = pl.ds(part * half, half)
        for dy in rings:
            image = image_at(dy)
            sides = []
            for j in range(2):
                at = positions[j]
                for other in range(1, per_dev):
                    at = jnp.where(image == other, positions[2 * other + j], at)
                sides.append(jnp.dot(zrecv[part][at], wh[...], preferred_element_type=F32))
            for h in range(heads):
                one, two = (side[:, h * pair : (h + 1) * pair] for side in sides)
                keys = jnp.where(low_rows, one, pltpu.roll(two, head_dim, 1))
                values = jnp.where(low_rows, pltpu.roll(one, head_dim, 1), two)
                part_send[0, image * heads + h, rows_of] = keys.astype(BF16)
                part_send[1, image * heads + h, rows_of] = values.astype(BF16)
            spread(1, part_send.at[0], part_recv.at[0], dy, rows_of)
    for part in range(2):
        for dy in rings:
            spread(2, part_send.at[1], part_recv.at[1], dy, pl.ds(part * half, half))

    chunk = rows * heads
    def as_keys(flat, first, count, upper):
        place = first + lax.broadcasted_iota(jnp.int32, flat.shape, 0)
        lane = lanes(flat.shape)
        inside = (lane >= head_dim) if upper else (lane < head_dim)
        penalty = jnp.where((lane == (0 if upper else head_dim)) & (place >= count), PENALTY, 0.0)
        return jnp.where(inside, flat.astype(F32) * scale, penalty).astype(BF16)

    def beside_ones(across, upper):
        ones = jnp.ones(across.shape, BF16)
        return jnp.concatenate([ones, across] if upper else [across, ones], axis=0)

    def line_arrived(dy):
        count = heads if dy else heads - 1
        rest = part_recv.at[0].at[pl.ds(0, count)]
        pltpu.make_async_copy(rest, rest, p_recv_sem.at[dy]).wait()
        if dy == 0:
            pltpu.make_async_copy(
                part_send.at[0].at[me], part_recv.at[0].at[me], l_sem.at[1]
            ).wait()

    def score(n):
        side, j, dy = steps[n]
        if side == "partner":
            if j == 0:
                line_arrived(dy)
            source = image_at(per_dev - dy)
            place = pl.ds(pl.multiple_of(source * chunk, chunk), chunk)
            flat = part_recv[0, pl.ds(source * heads, heads)].reshape(chunk, pair)
            k_part[j, place, :] = as_keys(flat, source * chunk, asked_counts[j], j == 1)
            queries = beside_ones(flat.T[j * head_dim : (j + 1) * head_dim], False)
            keys = k_own[...]
        else:
            if j == 0 and dy == rings[0]:
                arrived(2, part_send.at[1], part_recv.at[1])
                across = part_recv[1].reshape(keypoints, pair).T
                v_part[0] = beside_ones(across[0:head_dim], True)
                v_part[1] = beside_ones(across[head_dim:pair], True)
            place = pl.ds(pl.multiple_of(image_at(dy) * chunk, chunk), chunk)
            queries = q_own[j, :, place]
            keys = k_part[j]
        ahead[n % 2][...] = jnp.dot(keys, queries, preferred_element_type=F32)

    low_half = lanes((chunk // 2, pair)) < head_dim

    def attend(n):
        side, j, dy = steps[n]
        values = v_own[...] if side == "partner" else v_part[j]
        scores = ahead[n % 2][...]
        peak = jnp.max(scores, axis=0, keepdims=True)
        raised = jnp.exp(scores - peak).astype(BF16)
        total = jnp.dot(values, raised, preferred_element_type=F32)
        split = (total / total[0:1, :]).T.reshape(heads, 2, half, pair)
        upper = split[:, 0].reshape(chunk // 2, pair)
        lower = pltpu.roll(split[:, 1].reshape(chunk // 2, pair), head_dim, 1)
        message = jnp.where(low_half, lower, upper).reshape(heads, half, pair)
        if side == "partner":
            ahead_by = (per_dev - dy) % per_dev
            ret_send[j, pl.ds(image_at(ahead_by) * heads, heads)] = message.astype(BF16)
            spread(3 + j, ret_send.at[j], msg_recv.at[j], ahead_by)
        else:
            part = pl.ds(image_at(dy) * heads, heads)
            if j == 0:
                ret_acc[part] = message
            else:
                ret_send[2, part] = (ret_acc[part] + message).astype(BF16)
                spread(5, ret_send.at[2], sum_recv, dy)

    steps = [("partner", j, dy) for dy in rings for j in range(2)]
    steps += [("own", j, dy) for j in range(2) for dy in rings]
    asked_counts = [counts[partners[j, block * per_dev + my_image]] for j in range(2)]
    arrived(0, own_send, own_recv)
    whole = own_recv[...].reshape(keypoints, pair)
    k_own[...] = as_keys(whole, 0, counts[block * per_dev + my_image], False)
    across = whole.T
    q_own[0] = beside_ones(across[0:head_dim], False)
    q_own[1] = beside_ones(across[0:head_dim], True)
    v_own[...] = beside_ones(across[head_dim:pair], True)
    score(0)
    for n in range(len(steps)):
        if n + 1 < len(steps):
            score(n + 1)
        attend(n)

    arrived(3, ret_send.at[0], msg_recv.at[0])
    arrived(4, ret_send.at[1], msg_recv.at[1])
    back_copies = []
    for kind, offset in enumerate(OFFSETS):
        for c in range(CAP):
            edge = jnp.maximum(my_slots[kind][c] - 1, 0)
            image, j = lax.div(edge, 2), lax.rem(edge, 2)
            back_send[kind, c] = msg_recv[j, pl.ds(image * heads, heads)]
        copy = pltpu.make_async_remote_copy(
            src_ref=back_send.at[kind],
            dst_ref=back_recv.at[kind],
            send_sem=b_send_sem.at[kind],
            recv_sem=b_recv_sem.at[kind],
            device_id=(img_peer(offset), me),
            device_id_type=MESH,
        )
        copy.start()
        back_copies.append(copy)

    arrived(5, ret_send.at[2], sum_recv)
    inboxes, degrees = [], []
    for image in range(per_dev):
        inboxes.append(sum_recv[image * heads : (image + 1) * heads].astype(F32))
        degree = jnp.int32(2)
        for slots in incoming_slots:
            for slot in slots:
                degree = degree + jnp.where(slot == image + 1, 1, 0)
        degrees.append(degree.astype(F32))
    for kind in range(len(OFFSETS)):
        back_copies[kind].wait_recv()
        for c in range(CAP):
            message = back_recv[kind, c].astype(F32)
            for image in range(per_dev):
                hit = jnp.where(incoming_slots[kind][c] == image + 1, 1.0, 0.0)
                inboxes[image] = inboxes[image] + hit * message
    packed = [
        (inbox / degree).astype(BF16) for inbox, degree in zip(inboxes, degrees, strict=True)
    ]
    stacked = jnp.concatenate(
        [jnp.concatenate([packed[i][h] for i in range(per_dev)], axis=0) for h in range(heads)],
        axis=1,
    )
    both = jnp.dot(stacked, w2[...], preferred_element_type=F32).astype(BF16)
    for image in range(per_dev):
        mine = both[image * half : (image + 1) * half]
        proj[image * rows : image * rows + half, :] = mine[:, 0:width]
        proj[image * rows + half : (image + 1) * rows, :] = mine[:, width : 2 * width]

    stores = []
    for image in range(per_dev):
        part = pl.ds(image * rows, rows)
        hidden = hid[part, :] + jnp.dot(
            proj[part, :], f1_ref[width : 2 * width, :], preferred_element_type=F32
        )
        center = jnp.mean(hidden, axis=1, keepdims=True)
        away = hidden - center
        spreads = jnp.mean(away * away, axis=1, keepdims=True)
        normed = away * lax.rsqrt(spreads + 1e-5) * gain_ref[...] + nbias_ref[...]
        active = (0.5 * normed * (1.0 + lax.erf(normed * (0.5**0.5)))).astype(BF16)
        out_ref[image] = (
            jnp.dot(active, f2_ref[...], preferred_element_type=F32) + b2_ref[...]
        )
        stores.append(
            pltpu.make_async_copy(out_ref.at[image], out_hbm.at[image], out_sem.at[image])
        )
        stores[-1].start()

    for phase, send in (
        (0, own_send),
        (1, part_send.at[0]),
        (2, part_send.at[1]),
        (3, ret_send.at[0]),
        (4, ret_send.at[1]),
        (5, ret_send.at[2]),
    ):
        left(phase, send)
    for copy in z_copies + back_copies:
        copy.wait_send()
    for store in stores:
        store.wait()


def HEADS_OF(width):
    return width // 64


def per_device(
    features,
    partners,
    counts,
    shared_proj,
    value_proj,
    out_proj,
    ffn_in,
    ffn_in_bias,
    norm_gain,
    norm_bias,
    ffn_out,
    ffn_out_bias,
):
    img_count = lax.axis_size("img")
    row_devices = lax.axis_size("row")
    per_dev, rows, width = features.shape
    heads = HEADS_OF(width)
    head_dim = width // heads
    pair = 2 * head_dim
    keypoints = rows * row_devices
    hidden = ffn_in.shape[1]
    half = rows // 2
    kinds = len(OFFSETS)
    anywhere = pl.BlockSpec(memory_space=pl.ANY)
    update = pl.pallas_call(
        functools.partial(kernel, img_count, row_devices),
        out_shape=jax.ShapeDtypeStruct(features.shape, F32),
        in_specs=[anywhere] * 12,
        out_specs=anywhere,
        scratch_shapes=[
            pltpu.SMEM(partners.shape[::-1], jnp.int32),
            pltpu.SMEM(counts.shape, jnp.int32),
            pltpu.VMEM(features.shape, F32),
            pltpu.VMEM(shared_proj.shape, BF16),
            pltpu.VMEM(value_proj.shape, BF16),
            pltpu.VMEM(out_proj.shape, BF16),
            pltpu.VMEM(ffn_in.shape, BF16),
            pltpu.VMEM((1, hidden), F32),
            pltpu.VMEM((1, hidden), F32),
            pltpu.VMEM((1, hidden), F32),
            pltpu.VMEM(ffn_out.shape, BF16),
            pltpu.VMEM((1, width), F32),
            pltpu.VMEM(features.shape, F32),
            pltpu.SemaphoreType.DMA((12,)),
            pltpu.SemaphoreType.DMA((per_dev,)),
            pltpu.VMEM((per_dev, rows, width), BF16),
            pltpu.VMEM((2, kinds, CAP, half, width), BF16),
            pltpu.VMEM((width, 2 * width), BF16),
            pltpu.VMEM((heads * pair, 2 * width), BF16),
            pltpu.VMEM((per_dev * rows, hidden), F32),
            pltpu.VMEM((kinds * CAP, half, width), BF16),
            pltpu.VMEM((kinds * CAP, half, width), BF16),
            pltpu.VMEM((row_devices, rows, pair), BF16),
            pltpu.VMEM((row_devices, rows, pair), BF16),
            pltpu.VMEM((2, row_devices, rows, pair), BF16),
            pltpu.VMEM((2, row_devices, rows, pair), BF16),
            pltpu.VMEM((keypoints, pair), BF16),
            pltpu.VMEM((2, pair, keypoints), BF16),
            pltpu.VMEM((pair, keypoints), BF16),
            pltpu.VMEM((2, keypoints, pair), BF16),
            pltpu.VMEM((2, pair, keypoints), BF16),
            pltpu.VMEM((keypoints, rows * heads), F32),
            pltpu.VMEM((keypoints, rows * heads), F32),
            pltpu.VMEM((row_devices, half, pair), F32),
            pltpu.VMEM((3, row_devices, half, pair), BF16),
            pltpu.VMEM((2, row_devices, half, pair), BF16),
            pltpu.VMEM((row_devices, half, pair), BF16),
            pltpu.VMEM((kinds, CAP, heads, half, pair), BF16),
            pltpu.VMEM((kinds, CAP, heads, half, pair), BF16),
            pltpu.VMEM((per_dev * rows, width), BF16),
            pltpu.SemaphoreType.DMA((2, kinds)),
            pltpu.SemaphoreType.DMA((2, kinds)),
            pltpu.SemaphoreType.DMA((6,)),
            pltpu.SemaphoreType.DMA((6,)),
            pltpu.SemaphoreType.DMA((per_dev,)),
            pltpu.SemaphoreType.DMA((6,)),
            pltpu.SemaphoreType.DMA((kinds,)),
            pltpu.SemaphoreType.DMA((kinds,)),
        ],
        compiler_params=pltpu.CompilerParams(
            collective_id=0, has_side_effects=True, vmem_limit_bytes=60 * 1024 * 1024
        ),
    )(
        partners.T,
        counts,
        features,
        shared_proj,
        value_proj,
        out_proj,
        ffn_in,
        ffn_in_bias.reshape(1, -1),
        norm_gain.reshape(1, -1),
        norm_bias.reshape(1, -1),
        ffn_out,
        ffn_out_bias.reshape(1, -1),
    )
    return features + update


def solution(mesh):
    return jax.shard_map(
        per_device,
        mesh=mesh,
        in_specs=(P("img", "row", None), P(), P(), P(), P(), P(), P(), P(), P(), P(), P(), P()),
        out_specs=P("img", "row", None),
        check_vma=False,
    )
```

```python
import functools

import jax
import jax.numpy as jnp
from jax import lax
from jax.experimental import pallas as pl
from jax.experimental.pallas import tpu as pltpu
from jax.sharding import PartitionSpec as P

HEADS = 4
CAP = 3
OFFSETS = (1, -1, 2, -2)
PENALTY = -1e30
MESH = pl.DeviceIdType.MESH
F32 = jnp.float32
BF16 = jnp.bfloat16


def far_first(count):
    return sorted(range(count), key=lambda step: (-min(step, count - step), step))


def lanes(shape):
    return lax.broadcasted_iota(jnp.int32, shape, len(shape) - 1)


def kernel(
    img_count,
    row_devices,
    partners_hbm,
    counts_hbm,
    x_hbm,
    wq_hbm,
    wv_hbm,
    wo_hbm,
    f1_hbm,
    b1_hbm,
    gain_hbm,
    nbias_hbm,
    f2_hbm,
    b2_hbm,
    out_hbm,
    partners,
    counts,
    x_ref,
    wq_ref,
    wv_ref,
    wo_ref,
    f1_ref,
    b1_ref,
    gain_ref,
    nbias_ref,
    f2_ref,
    b2_ref,
    out_ref,
    in_sem,
    out_sem,
    xb,
    zsend,
    wh,
    w2,
    hid,
    zrecv_first,
    zrecv_second,
    own_send,
    own_recv,
    part_send,
    part_recv,
    k_own,
    q_own,
    v_own,
    k_part,
    v_part,
    ahead_even,
    ahead_odd,
    ret_acc,
    msg_send,
    sum_send,
    msg_recv,
    sum_recv,
    back_send,
    back_recv,
    proj,
    z_send_sem,
    z_recv_sem,
    a_send_sem,
    a_recv_sem,
    p_recv_sem,
    l_sem,
    b_send_sem,
    b_recv_sem,
):
    per_dev, rows, width = x_ref.shape
    half = rows // 2
    head_dim = width // HEADS_OF(width)
    heads = width // head_dim
    pair = 2 * head_dim
    keypoints = rows * row_devices
    edges = 2 * per_dev
    scale = head_dim ** (-0.5)
    block = lax.axis_index("img")
    me = lax.axis_index("row")
    my_image = lax.div(me, heads)
    my_head = lax.rem(me, heads)
    ahead = (ahead_even, ahead_odd)
    rings = far_first(per_dev)
    zrecv = (zrecv_first, zrecv_second)

    def img_peer(offset):
        return lax.rem(block + (offset + img_count), img_count)

    def image_at(dy):
        return lax.rem(my_image + dy, per_dev)

    def line(dy):
        for dx in far_first(heads):
            if dy or dx:
                yield image_at(dy) * heads + lax.rem(my_head + dx, heads)

    loads = [
        pltpu.make_async_copy(source, target, in_sem.at[n])
        for n, (source, target) in enumerate(
            (
                (partners_hbm, partners),
                (counts_hbm, counts),
                (x_hbm, x_ref),
                (wq_hbm, wq_ref),
                (wv_hbm, wv_ref),
                (f1_hbm, f1_ref),
                (b1_hbm, b1_ref),
                (wo_hbm, wo_ref),
                (gain_hbm, gain_ref),
                (nbias_hbm, nbias_ref),
                (f2_hbm, f2_ref),
                (b2_hbm, b2_ref),
            )
        )
    ]
    for load in loads:
        load.start()

    barrier = pltpu.get_barrier_semaphore()
    for offset in OFFSETS:
        pl.semaphore_signal(barrier, inc=1, device_id=(img_peer(offset), me), device_id_type=MESH)
    for dy in rings:
        for peer in line(dy):
            pl.semaphore_signal(barrier, inc=1, device_id=(block, peer), device_id_type=MESH)

    def entries_of(home):
        return [partners[e % 2, home * per_dev + e // 2] for e in range(edges)]

    def slots_between(entries, target):
        found, count = [], jnp.int32(0)
        for entry in entries:
            inside = lax.div(entry, per_dev) == target
            found.append((inside, count))
            count = count + jnp.where(inside, 1, 0)
        slots = []
        for c in range(CAP):
            edge, image = jnp.int32(0), jnp.int32(0)
            for e, (inside, rank) in enumerate(found):
                here = inside & (rank == c)
                edge = jnp.where(here, e + 1, edge)
                image = jnp.where(here, lax.rem(entries[e], per_dev) + 1, image)
            slots.append((edge, image))
        return found, slots

    loads[0].wait()
    incoming_slots = []
    for kind, offset in enumerate(OFFSETS):
        _, slots = slots_between(entries_of(img_peer(-offset)), block)
        incoming_slots.append([image for _, image in slots])
    loads[2].wait()
    xb[...] = x_ref[...].astype(BF16)
    for part in range(2):
        for kind in range(len(OFFSETS)):
            for c in range(CAP):
                zsend[part, kind, c] = xb[
                    jnp.maximum(incoming_slots[kind][c] - 1, 0), part * half : (part + 1) * half
                ]

    pl.semaphore_wait(barrier, len(OFFSETS) + row_devices - 1)

    z_copies = []
    for part in range(2):
        for kind, offset in enumerate(OFFSETS):
            copy = pltpu.make_async_remote_copy(
                src_ref=zsend.at[part, kind],
                dst_ref=zrecv[part].at[pl.ds(kind * CAP, CAP)],
                send_sem=z_send_sem.at[part, kind],
                recv_sem=z_recv_sem.at[part, kind],
                device_id=(img_peer(-offset), me),
                device_id_type=MESH,
            )
            copy.start()
            z_copies.append(copy)

    loads[3].wait()
    loads[4].wait()
    low = lanes((width, pair)) < head_dim
    for t in range(width // pair):
        q_t = wq_ref[:, t * pair : (t + 1) * pair].astype(F32)
        v_t = wv_ref[:, t * pair : (t + 1) * pair].astype(F32)
        first = jnp.where(low, q_t, pltpu.roll(v_t, head_dim, 1))
        second = jnp.where(low, pltpu.roll(q_t, head_dim, 1), v_t)
        wh[:, 2 * t * pair : (2 * t + 1) * pair] = first.astype(BF16)
        wh[:, (2 * t + 1) * pair : (2 * t + 2) * pair] = second.astype(BF16)

    def spread(phase, send, recv, dy, rows_of=None):
        def block_of(ref, which):
            return ref.at[which] if rows_of is None else ref.at[which, rows_of]

        for peer in line(dy):
            pltpu.make_async_remote_copy(
                src_ref=block_of(send, peer),
                dst_ref=block_of(recv, me),
                send_sem=a_send_sem.at[phase],
                recv_sem=(
                    p_recv_sem.at[dy] if phase == 1 else a_recv_sem.at[phase]
                ),
                device_id=(block, peer),
                device_id_type=MESH,
            ).start()
        if dy == 0:
            pltpu.make_async_copy(
                block_of(send, me), block_of(recv, me), l_sem.at[phase]
            ).start()

    def arrived(phase, send, recv):
        rest = pl.ds(0, row_devices - 1)
        pltpu.make_async_copy(recv.at[rest], recv.at[rest], a_recv_sem.at[phase]).wait()
        pltpu.make_async_copy(send.at[me], recv.at[me], l_sem.at[phase]).wait()

    def left(phase, send):
        rest = pl.ds(0, row_devices - 1)
        pltpu.make_async_copy(send.at[rest], send.at[rest], a_send_sem.at[phase]).wait()

    def projected_heads(source, send, image, rows_of):
        both = jnp.dot(source, wh[...], preferred_element_type=F32).astype(BF16)
        for h in range(heads):
            send[image * heads + h, rows_of] = both[:, h * pair : (h + 1) * pair]

    for dy in rings:
        image = image_at(dy)
        projected_heads(xb[image], own_send, image, pl.ds(0, rows))
        spread(0, own_send, own_recv, dy)

    my_entries = entries_of(block)
    my_slots = []
    positions = [jnp.int32(0)] * edges
    for kind, offset in enumerate(OFFSETS):
        found, slots = slots_between(my_entries, img_peer(offset))
        my_slots.append([edge for edge, _ in slots])
        for e, (inside, rank) in enumerate(found):
            positions[e] = jnp.where(
                inside, kind * CAP + jnp.minimum(rank, CAP - 1), positions[e]
            )
    loads[1].wait()
    for load in loads[5:]:
        load.wait()

    hid[...] = (
        jnp.dot(
            xb[...].reshape(per_dev * rows, width),
            f1_ref[0:width, :],
            preferred_element_type=F32,
        )
        + b1_ref[...]
    )
    for h in range(heads):
        piece = wo_ref[h * head_dim : (h + 1) * head_dim, :]
        blank = jnp.zeros_like(piece)
        w2[h * pair : h * pair + head_dim, 0:width] = blank
        w2[h * pair : h * pair + head_dim, width : 2 * width] = piece
        w2[h * pair + head_dim : (h + 1) * pair, 0:width] = piece
        w2[h * pair + head_dim : (h + 1) * pair, width : 2 * width] = blank

    low_rows = lanes((half, pair)) < head_dim
    for part in range(2):
        for kind in range(len(OFFSETS)):
            z_copies[part * len(OFFSETS) + kind].wait_recv()
        rows_of = pl.ds(part * half, half)
        for dy in rings:
            image = image_at(dy)
            sides = []
            for j in range(2):
                at = positions[j]
                for other in range(1, per_dev):
                    at = jnp.where(image == other, positions[2 * other + j], at)
                sides.append(jnp.dot(zrecv[part][at], wh[...], preferred_element_type=F32))
            for h in range(heads):
                one, two = (side[:, h * pair : (h + 1) * pair] for side in sides)
                keys = jnp.where(low_rows, one, pltpu.roll(two, head_dim, 1))
                values = jnp.where(low_rows, pltpu.roll(one, head_dim, 1), two)
                part_send[0, image * heads + h, rows_of] = keys.astype(BF16)
                part_send[1, image * heads + h, rows_of] = values.astype(BF16)
            spread(1, part_send.at[0], part_recv.at[0], dy, rows_of)
    for dy in rings:
        spread(2, part_send.at[1], part_recv.at[1], dy)

    chunk = rows * heads
    def as_keys(flat, first, count, upper):
        place = first + lax.broadcasted_iota(jnp.int32, flat.shape, 0)
        lane = lanes(flat.shape)
        inside = (lane >= head_dim) if upper else (lane < head_dim)
        penalty = jnp.where((lane == (0 if upper else head_dim)) & (place >= count), PENALTY, 0.0)
        return jnp.where(inside, flat.astype(F32) * scale, penalty).astype(BF16)

    def beside_ones(across, upper):
        ones = jnp.ones(across.shape, BF16)
        return jnp.concatenate([ones, across] if upper else [across, ones], axis=0)

    def line_arrived(dy):
        count = heads if dy else heads - 1
        rest = part_recv.at[0].at[pl.ds(0, count)]
        pltpu.make_async_copy(rest, rest, p_recv_sem.at[dy]).wait()
        if dy == 0:
            pltpu.make_async_copy(
                part_send.at[0].at[me], part_recv.at[0].at[me], l_sem.at[1]
            ).wait()

    def score(n):
        side, j, dy = steps[n]
        if side == "partner":
            if j == 0:
                line_arrived(dy)
            source = image_at(per_dev - dy)
            place = pl.ds(pl.multiple_of(source * chunk, chunk), chunk)
            flat = part_recv[0, pl.ds(source * heads, heads)].reshape(chunk, pair)
            k_part[j, place, :] = as_keys(flat, source * chunk, asked_counts[j], j == 1)
            queries = beside_ones(flat.T[j * head_dim : (j + 1) * head_dim], False)
            keys = k_own[...]
        else:
            if j == 0 and dy == rings[0]:
                arrived(2, part_send.at[1], part_recv.at[1])
                across = part_recv[1].reshape(keypoints, pair).T
                v_part[0] = beside_ones(across[0:head_dim], True)
                v_part[1] = beside_ones(across[head_dim:pair], True)
            place = pl.ds(pl.multiple_of(image_at(dy) * chunk, chunk), chunk)
            queries = q_own[j, :, place]
            keys = k_part[j]
        ahead[n % 2][...] = jnp.dot(keys, queries, preferred_element_type=F32)

    low_half = lanes((chunk // 2, pair)) < head_dim

    def attend(n):
        side, j, dy = steps[n]
        values = v_own[...] if side == "partner" else v_part[j]
        scores = ahead[n % 2][...]
        peak = jnp.max(scores, axis=0, keepdims=True)
        raised = jnp.exp(scores - peak).astype(BF16)
        total = jnp.dot(values, raised, preferred_element_type=F32)
        split = (total / total[0:1, :]).T.reshape(heads, 2, half, pair)
        upper = split[:, 0].reshape(chunk // 2, pair)
        lower = pltpu.roll(split[:, 1].reshape(chunk // 2, pair), head_dim, 1)
        message = jnp.where(low_half, lower, upper).reshape(heads, half, pair)
        if side == "partner":
            ahead_by = (per_dev - dy) % per_dev
            msg_send[pl.ds(image_at(ahead_by) * heads, heads), j] = message.astype(BF16)
            if j == 1:
                spread(3, msg_send, msg_recv, ahead_by)
        else:
            part = pl.ds(image_at(dy) * heads, heads)
            if j == 0:
                ret_acc[part] = message
            else:
                sum_send[part] = (ret_acc[part] + message).astype(BF16)
                spread(4, sum_send, sum_recv, dy)

    steps = [("partner", j, dy) for dy in rings for j in range(2)]
    steps += [("own", j, dy) for j in range(2) for dy in rings]
    asked_counts = [counts[partners[j, block * per_dev + my_image]] for j in range(2)]
    arrived(0, own_send, own_recv)
    whole = own_recv[...].reshape(keypoints, pair)
    k_own[...] = as_keys(whole, 0, counts[block * per_dev + my_image], False)
    across = whole.T
    q_own[0] = beside_ones(across[0:head_dim], False)
    q_own[1] = beside_ones(across[0:head_dim], True)
    v_own[...] = beside_ones(across[head_dim:pair], True)
    score(0)
    for n in range(len(steps)):
        if n + 1 < len(steps):
            score(n + 1)
        attend(n)

    arrived(3, msg_send, msg_recv)
    back_copies = []
    for kind, offset in enumerate(OFFSETS):
        for c in range(CAP):
            edge = jnp.maximum(my_slots[kind][c] - 1, 0)
            image, j = lax.div(edge, 2), lax.rem(edge, 2)
            back_send[kind, c] = msg_recv[pl.ds(image * heads, heads), j]
        copy = pltpu.make_async_remote_copy(
            src_ref=back_send.at[kind],
            dst_ref=back_recv.at[kind],
            send_sem=b_send_sem.at[kind],
            recv_sem=b_recv_sem.at[kind],
            device_id=(img_peer(offset), me),
            device_id_type=MESH,
        )
        copy.start()
        back_copies.append(copy)

    arrived(4, sum_send, sum_recv)
    inboxes, degrees = [], []
    for image in range(per_dev):
        inboxes.append(sum_recv[image * heads : (image + 1) * heads].astype(F32))
        degree = jnp.int32(2)
        for slots in incoming_slots:
            for slot in slots:
                degree = degree + jnp.where(slot == image + 1, 1, 0)
        degrees.append(degree.astype(F32))
    for kind in range(len(OFFSETS)):
        back_copies[kind].wait_recv()
        for c in range(CAP):
            message = back_recv[kind, c].astype(F32)
            for image in range(per_dev):
                hit = jnp.where(incoming_slots[kind][c] == image + 1, 1.0, 0.0)
                inboxes[image] = inboxes[image] + hit * message
    packed = [
        (inbox / degree).astype(BF16) for inbox, degree in zip(inboxes, degrees, strict=True)
    ]
    stacked = jnp.concatenate(
        [jnp.concatenate([packed[i][h] for i in range(per_dev)], axis=0) for h in range(heads)],
        axis=1,
    )
    both = jnp.dot(stacked, w2[...], preferred_element_type=F32).astype(BF16)
    for image in range(per_dev):
        mine = both[image * half : (image + 1) * half]
        proj[image * rows : image * rows + half, :] = mine[:, 0:width]
        proj[image * rows + half : (image + 1) * rows, :] = mine[:, width : 2 * width]

    stores = []
    for image in range(per_dev):
        part = pl.ds(image * rows, rows)
        hidden = hid[part, :] + jnp.dot(
            proj[part, :], f1_ref[width : 2 * width, :], preferred_element_type=F32
        )
        center = jnp.mean(hidden, axis=1, keepdims=True)
        away = hidden - center
        spreads = jnp.mean(away * away, axis=1, keepdims=True)
        normed = away * lax.rsqrt(spreads + 1e-5) * gain_ref[...] + nbias_ref[...]
        active = (0.5 * normed * (1.0 + lax.erf(normed * (0.5**0.5)))).astype(BF16)
        out_ref[image] = (
            jnp.dot(active, f2_ref[...], preferred_element_type=F32) + b2_ref[...]
        )
        stores.append(
            pltpu.make_async_copy(out_ref.at[image], out_hbm.at[image], out_sem.at[image])
        )
        stores[-1].start()

    for phase, send in (
        (0, own_send),
        (1, part_send.at[0]),
        (2, part_send.at[1]),
        (3, msg_send),
        (4, sum_send),
    ):
        left(phase, send)
    for copy in z_copies + back_copies:
        copy.wait_send()
    for store in stores:
        store.wait()


def HEADS_OF(width):
    return width // 64


def per_device(
    features,
    partners,
    counts,
    shared_proj,
    value_proj,
    out_proj,
    ffn_in,
    ffn_in_bias,
    norm_gain,
    norm_bias,
    ffn_out,
    ffn_out_bias,
):
    img_count = lax.axis_size("img")
    row_devices = lax.axis_size("row")
    per_dev, rows, width = features.shape
    heads = HEADS_OF(width)
    head_dim = width // heads
    pair = 2 * head_dim
    keypoints = rows * row_devices
    hidden = ffn_in.shape[1]
    half = rows // 2
    kinds = len(OFFSETS)
    anywhere = pl.BlockSpec(memory_space=pl.ANY)
    update = pl.pallas_call(
        functools.partial(kernel, img_count, row_devices),
        out_shape=jax.ShapeDtypeStruct(features.shape, F32),
        in_specs=[anywhere] * 12,
        out_specs=anywhere,
        scratch_shapes=[
            pltpu.SMEM(partners.shape[::-1], jnp.int32),
            pltpu.SMEM(counts.shape, jnp.int32),
            pltpu.VMEM(features.shape, F32),
            pltpu.VMEM(shared_proj.shape, BF16),
            pltpu.VMEM(value_proj.shape, BF16),
            pltpu.VMEM(out_proj.shape, BF16),
            pltpu.VMEM(ffn_in.shape, BF16),
            pltpu.VMEM((1, hidden), F32),
            pltpu.VMEM((1, hidden), F32),
            pltpu.VMEM((1, hidden), F32),
            pltpu.VMEM(ffn_out.shape, BF16),
            pltpu.VMEM((1, width), F32),
            pltpu.VMEM(features.shape, F32),
            pltpu.SemaphoreType.DMA((12,)),
            pltpu.SemaphoreType.DMA((per_dev,)),
            pltpu.VMEM((per_dev, rows, width), BF16),
            pltpu.VMEM((2, kinds, CAP, half, width), BF16),
            pltpu.VMEM((width, 2 * width), BF16),
            pltpu.VMEM((heads * pair, 2 * width), BF16),
            pltpu.VMEM((per_dev * rows, hidden), F32),
            pltpu.VMEM((kinds * CAP, half, width), BF16),
            pltpu.VMEM((kinds * CAP, half, width), BF16),
            pltpu.VMEM((row_devices, rows, pair), BF16),
            pltpu.VMEM((row_devices, rows, pair), BF16),
            pltpu.VMEM((2, row_devices, rows, pair), BF16),
            pltpu.VMEM((2, row_devices, rows, pair), BF16),
            pltpu.VMEM((keypoints, pair), BF16),
            pltpu.VMEM((2, pair, keypoints), BF16),
            pltpu.VMEM((pair, keypoints), BF16),
            pltpu.VMEM((2, keypoints, pair), BF16),
            pltpu.VMEM((2, pair, keypoints), BF16),
            pltpu.VMEM((keypoints, rows * heads), F32),
            pltpu.VMEM((keypoints, rows * heads), F32),
            pltpu.VMEM((row_devices, half, pair), F32),
            pltpu.VMEM((row_devices, 2, half, pair), BF16),
            pltpu.VMEM((row_devices, half, pair), BF16),
            pltpu.VMEM((row_devices, 2, half, pair), BF16),
            pltpu.VMEM((row_devices, half, pair), BF16),
            pltpu.VMEM((kinds, CAP, heads, half, pair), BF16),
            pltpu.VMEM((kinds, CAP, heads, half, pair), BF16),
            pltpu.VMEM((per_dev * rows, width), BF16),
            pltpu.SemaphoreType.DMA((2, kinds)),
            pltpu.SemaphoreType.DMA((2, kinds)),
            pltpu.SemaphoreType.DMA((5,)),
            pltpu.SemaphoreType.DMA((5,)),
            pltpu.SemaphoreType.DMA((per_dev,)),
            pltpu.SemaphoreType.DMA((5,)),
            pltpu.SemaphoreType.DMA((kinds,)),
            pltpu.SemaphoreType.DMA((kinds,)),
        ],
        compiler_params=pltpu.CompilerParams(
            collective_id=0, has_side_effects=True, vmem_limit_bytes=60 * 1024 * 1024
        ),
    )(
        partners.T,
        counts,
        features,
        shared_proj,
        value_proj,
        out_proj,
        ffn_in,
        ffn_in_bias.reshape(1, -1),
        norm_gain.reshape(1, -1),
        norm_bias.reshape(1, -1),
        ffn_out,
        ffn_out_bias.reshape(1, -1),
    )
    return features + update


def solution(mesh):
    return jax.shard_map(
        per_device,
        mesh=mesh,
        in_specs=(P("img", "row", None), P(), P(), P(), P(), P(), P(), P(), P(), P(), P(), P()),
        out_specs=P("img", "row", None),
        check_vma=False,
    )
```

```python
import functools

import jax
import jax.numpy as jnp
from jax import lax
from jax.experimental import pallas as pl
from jax.experimental.pallas import tpu as pltpu
from jax.sharding import PartitionSpec as P

HEADS = 4
CAP = 3
OFFSETS = (1, -1, 2, -2)
PENALTY = -1e30
MESH = pl.DeviceIdType.MESH
F32 = jnp.float32
BF16 = jnp.bfloat16


def far_first(count):
    return sorted(range(count), key=lambda step: (-min(step, count - step), step))


def lanes(shape):
    return lax.broadcasted_iota(jnp.int32, shape, len(shape) - 1)


def kernel(
    img_count,
    row_devices,
    partners_hbm,
    counts_hbm,
    x_hbm,
    wq_hbm,
    wv_hbm,
    wo_hbm,
    f1_hbm,
    b1_hbm,
    gain_hbm,
    nbias_hbm,
    f2_hbm,
    b2_hbm,
    out_0,
    out_1,
    out_2,
    out_3,
    partners,
    counts,
    x_ref,
    wq_ref,
    wv_ref,
    wo_ref,
    f1_ref,
    b1_ref,
    gain_ref,
    nbias_ref,
    f2_ref,
    b2_ref,
    in_sem,
    xb,
    zsend,
    wh,
    w2,
    hid,
    zrecv_first,
    zrecv_second,
    own_send,
    own_recv,
    part_send,
    part_recv,
    k_own,
    q_own,
    v_own,
    k_part,
    v_part,
    ahead_even,
    ahead_odd,
    ret_acc,
    msg_send,
    sum_send,
    msg_recv,
    sum_recv,
    back_send,
    back_recv,
    proj,
    z_send_sem,
    z_recv_sem,
    a_send_sem,
    a_recv_sem,
    p_recv_sem,
    l_sem,
    b_send_sem,
    b_recv_sem,
):
    per_dev, rows, width = x_ref.shape
    half = rows // 2
    head_dim = width // HEADS_OF(width)
    heads = width // head_dim
    pair = 2 * head_dim
    keypoints = rows * row_devices
    edges = 2 * per_dev
    scale = head_dim ** (-0.5)
    block = lax.axis_index("img")
    me = lax.axis_index("row")
    my_image = lax.div(me, heads)
    my_head = lax.rem(me, heads)
    ahead = (ahead_even, ahead_odd)
    rings = far_first(per_dev)
    zrecv = (zrecv_first, zrecv_second)

    def img_peer(offset):
        return lax.rem(block + (offset + img_count), img_count)

    def image_at(dy):
        return lax.rem(my_image + dy, per_dev)

    def line(dy):
        for dx in far_first(heads):
            if dy or dx:
                yield image_at(dy) * heads + lax.rem(my_head + dx, heads)

    loads = [
        pltpu.make_async_copy(source, target, in_sem.at[n])
        for n, (source, target) in enumerate(
            (
                (partners_hbm, partners),
                (counts_hbm, counts),
                (x_hbm, x_ref),
                (wq_hbm, wq_ref),
                (wv_hbm, wv_ref),
                (f1_hbm, f1_ref),
                (b1_hbm, b1_ref),
                (wo_hbm, wo_ref),
                (gain_hbm, gain_ref),
                (nbias_hbm, nbias_ref),
                (f2_hbm, f2_ref),
                (b2_hbm, b2_ref),
            )
        )
    ]
    for load in loads:
        load.start()

    barrier = pltpu.get_barrier_semaphore()
    for offset in OFFSETS:
        pl.semaphore_signal(barrier, inc=1, device_id=(img_peer(offset), me), device_id_type=MESH)
    for dy in rings:
        for peer in line(dy):
            pl.semaphore_signal(barrier, inc=1, device_id=(block, peer), device_id_type=MESH)

    def entries_of(home):
        return [partners[e % 2, home * per_dev + e // 2] for e in range(edges)]

    def slots_between(entries, target):
        found, count = [], jnp.int32(0)
        for entry in entries:
            inside = lax.div(entry, per_dev) == target
            found.append((inside, count))
            count = count + jnp.where(inside, 1, 0)
        slots = []
        for c in range(CAP):
            edge, image = jnp.int32(0), jnp.int32(0)
            for e, (inside, rank) in enumerate(found):
                here = inside & (rank == c)
                edge = jnp.where(here, e + 1, edge)
                image = jnp.where(here, lax.rem(entries[e], per_dev) + 1, image)
            slots.append((edge, image))
        return found, slots

    loads[0].wait()
    incoming_slots = []
    for kind, offset in enumerate(OFFSETS):
        _, slots = slots_between(entries_of(img_peer(-offset)), block)
        incoming_slots.append([image for _, image in slots])
    loads[2].wait()
    xb[...] = x_ref[...].astype(BF16)
    for part in range(2):
        for kind in range(len(OFFSETS)):
            for c in range(CAP):
                zsend[part, kind, c] = xb[
                    jnp.maximum(incoming_slots[kind][c] - 1, 0), part * half : (part + 1) * half
                ]

    pl.semaphore_wait(barrier, len(OFFSETS) + row_devices - 1)

    z_copies = []
    for part in range(2):
        for kind, offset in enumerate(OFFSETS):
            copy = pltpu.make_async_remote_copy(
                src_ref=zsend.at[part, kind],
                dst_ref=zrecv[part].at[pl.ds(kind * CAP, CAP)],
                send_sem=z_send_sem.at[part, kind],
                recv_sem=z_recv_sem.at[part, kind],
                device_id=(img_peer(-offset), me),
                device_id_type=MESH,
            )
            copy.start()
            z_copies.append(copy)

    loads[3].wait()
    loads[4].wait()
    low = lanes((width, pair)) < head_dim
    for t in range(width // pair):
        q_t = wq_ref[:, t * pair : (t + 1) * pair].astype(F32)
        v_t = wv_ref[:, t * pair : (t + 1) * pair].astype(F32)
        first = jnp.where(low, q_t, pltpu.roll(v_t, head_dim, 1))
        second = jnp.where(low, pltpu.roll(q_t, head_dim, 1), v_t)
        wh[:, 2 * t * pair : (2 * t + 1) * pair] = first.astype(BF16)
        wh[:, (2 * t + 1) * pair : (2 * t + 2) * pair] = second.astype(BF16)

    def spread(phase, send, recv, dy, rows_of=None):
        def block_of(ref, which):
            return ref.at[which] if rows_of is None else ref.at[which, rows_of]

        for peer in line(dy):
            pltpu.make_async_remote_copy(
                src_ref=block_of(send, peer),
                dst_ref=block_of(recv, me),
                send_sem=a_send_sem.at[phase],
                recv_sem=(
                    p_recv_sem.at[dy] if phase == 1 else a_recv_sem.at[phase]
                ),
                device_id=(block, peer),
                device_id_type=MESH,
            ).start()
        if dy == 0:
            pltpu.make_async_copy(
                block_of(send, me), block_of(recv, me), l_sem.at[phase]
            ).start()

    def arrived(phase, send, recv):
        rest = pl.ds(0, row_devices - 1)
        pltpu.make_async_copy(recv.at[rest], recv.at[rest], a_recv_sem.at[phase]).wait()
        pltpu.make_async_copy(send.at[me], recv.at[me], l_sem.at[phase]).wait()

    def left(phase, send):
        rest = pl.ds(0, row_devices - 1)
        pltpu.make_async_copy(send.at[rest], send.at[rest], a_send_sem.at[phase]).wait()

    def projected_heads(source, send, image, rows_of):
        both = jnp.dot(source, wh[...], preferred_element_type=F32).astype(BF16)
        for h in range(heads):
            send[image * heads + h, rows_of] = both[:, h * pair : (h + 1) * pair]

    for dy in rings:
        image = image_at(dy)
        projected_heads(xb[image], own_send, image, pl.ds(0, rows))
        spread(0, own_send, own_recv, dy)

    my_entries = entries_of(block)
    my_slots = []
    positions = [jnp.int32(0)] * edges
    for kind, offset in enumerate(OFFSETS):
        found, slots = slots_between(my_entries, img_peer(offset))
        my_slots.append([edge for edge, _ in slots])
        for e, (inside, rank) in enumerate(found):
            positions[e] = jnp.where(
                inside, kind * CAP + jnp.minimum(rank, CAP - 1), positions[e]
            )
    loads[1].wait()
    for load in loads[5:]:
        load.wait()

    hid[...] = (
        jnp.dot(
            xb[...].reshape(per_dev * rows, width),
            f1_ref[0:width, :],
            preferred_element_type=F32,
        )
        + b1_ref[...]
    )
    for h in range(heads):
        piece = wo_ref[h * head_dim : (h + 1) * head_dim, :]
        blank = jnp.zeros_like(piece)
        w2[h * pair : h * pair + head_dim, 0:width] = blank
        w2[h * pair : h * pair + head_dim, width : 2 * width] = piece
        w2[h * pair + head_dim : (h + 1) * pair, 0:width] = piece
        w2[h * pair + head_dim : (h + 1) * pair, width : 2 * width] = blank

    low_rows = lanes((half, pair)) < head_dim
    for part in range(2):
        for kind in range(len(OFFSETS)):
            z_copies[part * len(OFFSETS) + kind].wait_recv()
        rows_of = pl.ds(part * half, half)
        for dy in rings:
            image = image_at(dy)
            sides = []
            for j in range(2):
                at = positions[j]
                for other in range(1, per_dev):
                    at = jnp.where(image == other, positions[2 * other + j], at)
                sides.append(jnp.dot(zrecv[part][at], wh[...], preferred_element_type=F32))
            for h in range(heads):
                one, two = (side[:, h * pair : (h + 1) * pair] for side in sides)
                keys = jnp.where(low_rows, one, pltpu.roll(two, head_dim, 1))
                values = jnp.where(low_rows, pltpu.roll(one, head_dim, 1), two)
                part_send[0, image * heads + h, rows_of] = keys.astype(BF16)
                part_send[1, image * heads + h, rows_of] = values.astype(BF16)
            spread(1, part_send.at[0], part_recv.at[0], dy, rows_of)
    for dy in rings:
        spread(2, part_send.at[1], part_recv.at[1], dy)

    chunk = rows * heads
    def as_keys(flat, first, count, upper):
        place = first + lax.broadcasted_iota(jnp.int32, flat.shape, 0)
        lane = lanes(flat.shape)
        inside = (lane >= head_dim) if upper else (lane < head_dim)
        penalty = jnp.where((lane == (0 if upper else head_dim)) & (place >= count), PENALTY, 0.0)
        return jnp.where(inside, flat.astype(F32) * scale, penalty).astype(BF16)

    def beside_ones(across, upper):
        ones = jnp.ones(across.shape, BF16)
        return jnp.concatenate([ones, across] if upper else [across, ones], axis=0)

    def line_arrived(dy):
        count = heads if dy else heads - 1
        rest = part_recv.at[0].at[pl.ds(0, count)]
        pltpu.make_async_copy(rest, rest, p_recv_sem.at[dy]).wait()
        if dy == 0:
            pltpu.make_async_copy(
                part_send.at[0].at[me], part_recv.at[0].at[me], l_sem.at[1]
            ).wait()

    def score(n):
        side, j, dy = steps[n]
        if side == "partner":
            if j == 0:
                line_arrived(dy)
            source = image_at(per_dev - dy)
            place = pl.ds(pl.multiple_of(source * chunk, chunk), chunk)
            flat = part_recv[0, pl.ds(source * heads, heads)].reshape(chunk, pair)
            k_part[j, place, :] = as_keys(flat, source * chunk, asked_counts[j], j == 1)
            queries = beside_ones(flat.T[j * head_dim : (j + 1) * head_dim], False)
            keys = k_own[...]
        else:
            if j == 0 and dy == rings[0]:
                arrived(2, part_send.at[1], part_recv.at[1])
                across = part_recv[1].reshape(keypoints, pair).T
                v_part[0] = beside_ones(across[0:head_dim], True)
                v_part[1] = beside_ones(across[head_dim:pair], True)
            place = pl.ds(pl.multiple_of(image_at(dy) * chunk, chunk), chunk)
            queries = q_own[j, :, place]
            keys = k_part[j]
        ahead[n % 2][...] = jnp.dot(keys, queries, preferred_element_type=F32)

    low_half = lanes((chunk // 2, pair)) < head_dim

    def attend(n):
        side, j, dy = steps[n]
        values = v_own[...] if side == "partner" else v_part[j]
        scores = ahead[n % 2][...]
        peak = jnp.max(scores, axis=0, keepdims=True)
        raised = jnp.exp(scores - peak).astype(BF16)
        total = jnp.dot(values, raised, preferred_element_type=F32)
        split = (total / total[0:1, :]).T.reshape(heads, 2, half, pair)
        upper = split[:, 0].reshape(chunk // 2, pair)
        lower = pltpu.roll(split[:, 1].reshape(chunk // 2, pair), head_dim, 1)
        message = jnp.where(low_half, lower, upper).reshape(heads, half, pair)
        if side == "partner":
            ahead_by = (per_dev - dy) % per_dev
            msg_send[pl.ds(image_at(ahead_by) * heads, heads), j] = message.astype(BF16)
            if j == 1:
                spread(3, msg_send, msg_recv, ahead_by)
        else:
            part = pl.ds(image_at(dy) * heads, heads)
            if j == 0:
                ret_acc[part] = message
            else:
                sum_send[part] = (ret_acc[part] + message).astype(BF16)
                spread(4, sum_send, sum_recv, dy)

    steps = [("partner", j, dy) for dy in rings for j in range(2)]
    steps += [("own", j, dy) for j in range(2) for dy in rings]
    asked_counts = [counts[partners[j, block * per_dev + my_image]] for j in range(2)]
    arrived(0, own_send, own_recv)
    whole = own_recv[...].reshape(keypoints, pair)
    k_own[...] = as_keys(whole, 0, counts[block * per_dev + my_image], False)
    across = whole.T
    q_own[0] = beside_ones(across[0:head_dim], False)
    q_own[1] = beside_ones(across[0:head_dim], True)
    v_own[...] = beside_ones(across[head_dim:pair], True)
    score(0)
    for n in range(len(steps)):
        if n + 1 < len(steps):
            score(n + 1)
        attend(n)

    arrived(3, msg_send, msg_recv)
    back_copies = []
    for kind, offset in enumerate(OFFSETS):
        for c in range(CAP):
            edge = jnp.maximum(my_slots[kind][c] - 1, 0)
            image, j = lax.div(edge, 2), lax.rem(edge, 2)
            back_send[kind, c] = msg_recv[pl.ds(image * heads, heads), j]
        copy = pltpu.make_async_remote_copy(
            src_ref=back_send.at[kind],
            dst_ref=back_recv.at[kind],
            send_sem=b_send_sem.at[kind],
            recv_sem=b_recv_sem.at[kind],
            device_id=(img_peer(offset), me),
            device_id_type=MESH,
        )
        copy.start()
        back_copies.append(copy)

    arrived(4, sum_send, sum_recv)
    inboxes, degrees = [], []
    for image in range(per_dev):
        inboxes.append(sum_recv[image * heads : (image + 1) * heads].astype(F32))
        degree = jnp.int32(2)
        for slots in incoming_slots:
            for slot in slots:
                degree = degree + jnp.where(slot == image + 1, 1, 0)
        degrees.append(degree.astype(F32))
    for kind in range(len(OFFSETS)):
        back_copies[kind].wait_recv()
        for c in range(CAP):
            message = back_recv[kind, c].astype(F32)
            for image in range(per_dev):
                hit = jnp.where(incoming_slots[kind][c] == image + 1, 1.0, 0.0)
                inboxes[image] = inboxes[image] + hit * message
    packed = [
        (inbox / degree).astype(BF16) for inbox, degree in zip(inboxes, degrees, strict=True)
    ]
    stacked = jnp.concatenate(
        [jnp.concatenate([packed[i][h] for i in range(per_dev)], axis=0) for h in range(heads)],
        axis=1,
    )
    both = jnp.dot(stacked, w2[...], preferred_element_type=F32).astype(BF16)
    for image in range(per_dev):
        mine = both[image * half : (image + 1) * half]
        proj[image * rows : image * rows + half, :] = mine[:, 0:width]
        proj[image * rows + half : (image + 1) * rows, :] = mine[:, width : 2 * width]

    outs = (out_0, out_1, out_2, out_3)
    for image in range(per_dev):
        part = pl.ds(image * rows, rows)
        hidden = hid[part, :] + jnp.dot(
            proj[part, :], f1_ref[width : 2 * width, :], preferred_element_type=F32
        )
        center = jnp.mean(hidden, axis=1, keepdims=True)
        away = hidden - center
        spreads = jnp.mean(away * away, axis=1, keepdims=True)
        normed = away * lax.rsqrt(spreads + 1e-5) * gain_ref[...] + nbias_ref[...]
        active = (0.5 * normed * (1.0 + lax.erf(normed * (0.5**0.5)))).astype(BF16)
        outs[image][...] = (
            jnp.dot(active, f2_ref[...], preferred_element_type=F32) + b2_ref[...]
        )

    for phase, send in (
        (0, own_send),
        (1, part_send.at[0]),
        (2, part_send.at[1]),
        (3, msg_send),
        (4, sum_send),
    ):
        left(phase, send)
    for copy in z_copies + back_copies:
        copy.wait_send()


def HEADS_OF(width):
    return width // 64


def per_device(
    features,
    partners,
    counts,
    shared_proj,
    value_proj,
    out_proj,
    ffn_in,
    ffn_in_bias,
    norm_gain,
    norm_bias,
    ffn_out,
    ffn_out_bias,
):
    img_count = lax.axis_size("img")
    row_devices = lax.axis_size("row")
    per_dev, rows, width = features.shape
    heads = HEADS_OF(width)
    head_dim = width // heads
    pair = 2 * head_dim
    keypoints = rows * row_devices
    hidden = ffn_in.shape[1]
    half = rows // 2
    kinds = len(OFFSETS)
    anywhere = pl.BlockSpec(memory_space=pl.ANY)
    update = pl.pallas_call(
        functools.partial(kernel, img_count, row_devices),
        out_shape=[jax.ShapeDtypeStruct(features.shape[1:], F32)] * per_dev,
        in_specs=[anywhere] * 12,
        out_specs=[pl.BlockSpec(memory_space=pltpu.VMEM)] * per_dev,
        scratch_shapes=[
            pltpu.SMEM(partners.shape[::-1], jnp.int32),
            pltpu.SMEM(counts.shape, jnp.int32),
            pltpu.VMEM(features.shape, F32),
            pltpu.VMEM(shared_proj.shape, BF16),
            pltpu.VMEM(value_proj.shape, BF16),
            pltpu.VMEM(out_proj.shape, BF16),
            pltpu.VMEM(ffn_in.shape, BF16),
            pltpu.VMEM((1, hidden), F32),
            pltpu.VMEM((1, hidden), F32),
            pltpu.VMEM((1, hidden), F32),
            pltpu.VMEM(ffn_out.shape, BF16),
            pltpu.VMEM((1, width), F32),
            pltpu.SemaphoreType.DMA((12,)),
            pltpu.VMEM((per_dev, rows, width), BF16),
            pltpu.VMEM((2, kinds, CAP, half, width), BF16),
            pltpu.VMEM((width, 2 * width), BF16),
            pltpu.VMEM((heads * pair, 2 * width), BF16),
            pltpu.VMEM((per_dev * rows, hidden), F32),
            pltpu.VMEM((kinds * CAP, half, width), BF16),
            pltpu.VMEM((kinds * CAP, half, width), BF16),
            pltpu.VMEM((row_devices, rows, pair), BF16),
            pltpu.VMEM((row_devices, rows, pair), BF16),
            pltpu.VMEM((2, row_devices, rows, pair), BF16),
            pltpu.VMEM((2, row_devices, rows, pair), BF16),
            pltpu.VMEM((keypoints, pair), BF16),
            pltpu.VMEM((2, pair, keypoints), BF16),
            pltpu.VMEM((pair, keypoints), BF16),
            pltpu.VMEM((2, keypoints, pair), BF16),
            pltpu.VMEM((2, pair, keypoints), BF16),
            pltpu.VMEM((keypoints, rows * heads), F32),
            pltpu.VMEM((keypoints, rows * heads), F32),
            pltpu.VMEM((row_devices, half, pair), F32),
            pltpu.VMEM((row_devices, 2, half, pair), BF16),
            pltpu.VMEM((row_devices, half, pair), BF16),
            pltpu.VMEM((row_devices, 2, half, pair), BF16),
            pltpu.VMEM((row_devices, half, pair), BF16),
            pltpu.VMEM((kinds, CAP, heads, half, pair), BF16),
            pltpu.VMEM((kinds, CAP, heads, half, pair), BF16),
            pltpu.VMEM((per_dev * rows, width), BF16),
            pltpu.SemaphoreType.DMA((2, kinds)),
            pltpu.SemaphoreType.DMA((2, kinds)),
            pltpu.SemaphoreType.DMA((5,)),
            pltpu.SemaphoreType.DMA((5,)),
            pltpu.SemaphoreType.DMA((per_dev,)),
            pltpu.SemaphoreType.DMA((5,)),
            pltpu.SemaphoreType.DMA((kinds,)),
            pltpu.SemaphoreType.DMA((kinds,)),
        ],
        compiler_params=pltpu.CompilerParams(
            collective_id=0, has_side_effects=True, vmem_limit_bytes=67043328 - 10550 * 1024
        ),
    )(
        partners.T,
        counts,
        features,
        shared_proj,
        value_proj,
        out_proj,
        ffn_in,
        ffn_in_bias.reshape(1, -1),
        norm_gain.reshape(1, -1),
        norm_bias.reshape(1, -1),
        ffn_out,
        ffn_out_bias.reshape(1, -1),
    )
    return features + jnp.stack(update)


def solution(mesh):
    return jax.shard_map(
        per_device,
        mesh=mesh,
        in_specs=(P("img", "row", None), P(), P(), P(), P(), P(), P(), P(), P(), P(), P(), P()),
        out_specs=P("img", "row", None),
        check_vma=False,
    )
```

```python
import functools

import jax
import jax.numpy as jnp
from jax import lax
from jax.experimental import pallas as pl
from jax.experimental.pallas import tpu as pltpu
from jax.sharding import PartitionSpec as P

HEADS = 4
CAP = 3
OFFSETS = (1, -1, 2, -2)
PENALTY = -1e30
MESH = pl.DeviceIdType.MESH
F32 = jnp.float32
BF16 = jnp.bfloat16


def far_first(count):
    return sorted(range(count), key=lambda step: (-min(step, count - step), step))


def lanes(shape):
    return lax.broadcasted_iota(jnp.int32, shape, len(shape) - 1)


def kernel(
    img_count,
    row_devices,
    partners_hbm,
    counts_hbm,
    x_hbm,
    wq_hbm,
    wv_hbm,
    wo_hbm,
    f1_hbm,
    b1_hbm,
    gain_hbm,
    nbias_hbm,
    f2_hbm,
    b2_hbm,
    out_0,
    out_1,
    out_2,
    out_3,
    partners,
    counts,
    x_ref,
    wq_ref,
    wv_ref,
    wo_ref,
    f1_ref,
    b1_ref,
    gain_ref,
    nbias_ref,
    f2_ref,
    b2_ref,
    in_sem,
    xb,
    zsend,
    wh,
    w2,
    hid,
    zrecv_first,
    zrecv_second,
    own_send,
    own_recv,
    part_send,
    part_recv,
    k_own,
    q_own,
    v_own,
    k_part,
    v_part,
    ahead_even,
    ahead_odd,
    ret_acc,
    msg_send,
    sum_send,
    msg_recv,
    sum_recv,
    back_send,
    back_recv,
    proj,
    z_send_sem,
    z_recv_sem,
    a_send_sem,
    a_recv_sem,
    p_recv_sem,
    l_sem,
    b_send_sem,
    b_recv_sem,
):
    per_dev, rows, width = x_ref.shape
    half = rows // 2
    head_dim = width // HEADS_OF(width)
    heads = width // head_dim
    pair = 2 * head_dim
    keypoints = rows * row_devices
    edges = 2 * per_dev
    scale = head_dim ** (-0.5)
    block = lax.axis_index("img")
    me = lax.axis_index("row")
    my_image = lax.div(me, heads)
    my_head = lax.rem(me, heads)
    ahead = (ahead_even, ahead_odd)
    rings = far_first(per_dev)
    zrecv = (zrecv_first, zrecv_second)

    def img_peer(offset):
        return lax.rem(block + (offset + img_count), img_count)

    def image_at(dy):
        return lax.rem(my_image + dy, per_dev)

    def line(dy):
        for dx in far_first(heads):
            if dy or dx:
                yield image_at(dy) * heads + lax.rem(my_head + dx, heads)

    loads = [
        pltpu.make_async_copy(source, target, in_sem.at[n])
        for n, (source, target) in enumerate(
            (
                (partners_hbm, partners),
                (counts_hbm, counts),
                (x_hbm, x_ref),
                (wq_hbm, wq_ref),
                (wv_hbm, wv_ref),
                (f1_hbm, f1_ref),
                (b1_hbm, b1_ref),
                (wo_hbm, wo_ref),
                (gain_hbm, gain_ref),
                (nbias_hbm, nbias_ref),
                (f2_hbm, f2_ref),
                (b2_hbm, b2_ref),
            )
        )
    ]
    for load in loads:
        load.start()

    barrier = pltpu.get_barrier_semaphore()
    for offset in OFFSETS:
        pl.semaphore_signal(barrier, inc=1, device_id=(img_peer(offset), me), device_id_type=MESH)
    for dy in rings:
        for peer in line(dy):
            pl.semaphore_signal(barrier, inc=1, device_id=(block, peer), device_id_type=MESH)

    def entries_of(home):
        return [partners[e % 2, home * per_dev + e // 2] for e in range(edges)]

    def slots_between(entries, target):
        found, count = [], jnp.int32(0)
        for entry in entries:
            inside = lax.div(entry, per_dev) == target
            found.append((inside, count))
            count = count + jnp.where(inside, 1, 0)
        slots = []
        for c in range(CAP):
            edge, image = jnp.int32(0), jnp.int32(0)
            for e, (inside, rank) in enumerate(found):
                here = inside & (rank == c)
                edge = jnp.where(here, e + 1, edge)
                image = jnp.where(here, lax.rem(entries[e], per_dev) + 1, image)
            slots.append((edge, image))
        return found, slots

    loads[0].wait()
    incoming_slots = []
    for kind, offset in enumerate(OFFSETS):
        _, slots = slots_between(entries_of(img_peer(-offset)), block)
        incoming_slots.append([image for _, image in slots])
    loads[2].wait()
    xb[...] = x_ref[...].astype(BF16)
    for part in range(2):
        for kind in range(len(OFFSETS)):
            for c in range(CAP):
                zsend[part, kind, c] = xb[
                    jnp.maximum(incoming_slots[kind][c] - 1, 0), part * half : (part + 1) * half
                ]

    pl.semaphore_wait(barrier, len(OFFSETS) + row_devices - 1)

    z_copies = []
    for part in range(2):
        for kind, offset in enumerate(OFFSETS):
            copy = pltpu.make_async_remote_copy(
                src_ref=zsend.at[part, kind],
                dst_ref=zrecv[part].at[pl.ds(kind * CAP, CAP)],
                send_sem=z_send_sem.at[part, kind],
                recv_sem=z_recv_sem.at[part, kind],
                device_id=(img_peer(-offset), me),
                device_id_type=MESH,
            )
            copy.start()
            z_copies.append(copy)

    loads[3].wait()
    loads[4].wait()
    low = lanes((width, pair)) < head_dim
    for t in range(width // pair):
        q_t = wq_ref[:, t * pair : (t + 1) * pair].astype(F32)
        v_t = wv_ref[:, t * pair : (t + 1) * pair].astype(F32)
        first = jnp.where(low, q_t, pltpu.roll(v_t, head_dim, 1))
        second = jnp.where(low, pltpu.roll(q_t, head_dim, 1), v_t)
        wh[:, 2 * t * pair : (2 * t + 1) * pair] = first.astype(BF16)
        wh[:, (2 * t + 1) * pair : (2 * t + 2) * pair] = second.astype(BF16)

    def spread(phase, send, recv, dy, rows_of=None):
        def block_of(ref, which):
            return ref.at[which] if rows_of is None else ref.at[which, rows_of]

        for peer in line(dy):
            pltpu.make_async_remote_copy(
                src_ref=block_of(send, peer),
                dst_ref=block_of(recv, me),
                send_sem=a_send_sem.at[phase],
                recv_sem=(
                    p_recv_sem.at[dy] if phase == 1 else a_recv_sem.at[phase]
                ),
                device_id=(block, peer),
                device_id_type=MESH,
            ).start()
        if dy == 0:
            pltpu.make_async_copy(
                block_of(send, me), block_of(recv, me), l_sem.at[phase]
            ).start()

    def arrived(phase, send, recv):
        rest = pl.ds(0, row_devices - 1)
        pltpu.make_async_copy(recv.at[rest], recv.at[rest], a_recv_sem.at[phase]).wait()
        pltpu.make_async_copy(send.at[me], recv.at[me], l_sem.at[phase]).wait()

    def left(phase, send):
        rest = pl.ds(0, row_devices - 1)
        pltpu.make_async_copy(send.at[rest], send.at[rest], a_send_sem.at[phase]).wait()

    def projected_heads(source, send, image, rows_of):
        both = jnp.dot(source, wh[...], preferred_element_type=F32).astype(BF16)
        for h in range(heads):
            send[image * heads + h, rows_of] = both[:, h * pair : (h + 1) * pair]

    for dy in rings:
        image = image_at(dy)
        projected_heads(xb[image], own_send, image, pl.ds(0, rows))
        spread(0, own_send, own_recv, dy)

    my_entries = entries_of(block)
    my_slots = []
    positions = [jnp.int32(0)] * edges
    for kind, offset in enumerate(OFFSETS):
        found, slots = slots_between(my_entries, img_peer(offset))
        my_slots.append([edge for edge, _ in slots])
        for e, (inside, rank) in enumerate(found):
            positions[e] = jnp.where(
                inside, kind * CAP + jnp.minimum(rank, CAP - 1), positions[e]
            )
    loads[1].wait()
    for load in loads[5:]:
        load.wait()

    hid[...] = (
        jnp.dot(
            xb[...].reshape(per_dev * rows, width),
            f1_ref[0:width, :],
            preferred_element_type=F32,
        )
        + b1_ref[...]
    )
    for h in range(heads):
        piece = wo_ref[h * head_dim : (h + 1) * head_dim, :]
        blank = jnp.zeros_like(piece)
        w2[h * pair : h * pair + head_dim, 0:width] = blank
        w2[h * pair : h * pair + head_dim, width : 2 * width] = piece
        w2[h * pair + head_dim : (h + 1) * pair, 0:width] = piece
        w2[h * pair + head_dim : (h + 1) * pair, width : 2 * width] = blank

    low_rows = lanes((half, pair)) < head_dim
    for part in range(2):
        for kind in range(len(OFFSETS)):
            z_copies[part * len(OFFSETS) + kind].wait_recv()
        rows_of = pl.ds(part * half, half)
        for dy in rings:
            image = image_at(dy)
            sides = []
            for j in range(2):
                at = positions[j]
                for other in range(1, per_dev):
                    at = jnp.where(image == other, positions[2 * other + j], at)
                sides.append(jnp.dot(zrecv[part][at], wh[...], preferred_element_type=F32))
            for h in range(heads):
                one, two = (side[:, h * pair : (h + 1) * pair] for side in sides)
                keys = jnp.where(low_rows, one, pltpu.roll(two, head_dim, 1))
                values = jnp.where(low_rows, pltpu.roll(one, head_dim, 1), two)
                part_send[0, image * heads + h, rows_of] = keys.astype(BF16)
                part_send[1, image * heads + h, rows_of] = values.astype(BF16)
            spread(1, part_send.at[0], part_recv.at[0], dy, rows_of)
    for dy in rings:
        spread(2, part_send.at[1], part_recv.at[1], dy)

    chunk = rows * heads
    def as_keys(flat, first, count, upper):
        place = first + lax.broadcasted_iota(jnp.int32, flat.shape, 0)
        lane = lanes(flat.shape)
        inside = (lane >= head_dim) if upper else (lane < head_dim)
        penalty = jnp.where((lane == (0 if upper else head_dim)) & (place >= count), PENALTY, 0.0)
        return jnp.where(inside, flat.astype(F32) * scale, penalty).astype(BF16)

    def beside_ones(across, upper):
        ones = jnp.ones(across.shape, BF16)
        return jnp.concatenate([ones, across] if upper else [across, ones], axis=0)

    def line_arrived(dy):
        count = heads if dy else heads - 1
        rest = part_recv.at[0].at[pl.ds(0, count)]
        pltpu.make_async_copy(rest, rest, p_recv_sem.at[dy]).wait()
        if dy == 0:
            pltpu.make_async_copy(
                part_send.at[0].at[me], part_recv.at[0].at[me], l_sem.at[1]
            ).wait()

    def score(n):
        side, j, dy = steps[n]
        if side == "partner":
            if j == 0:
                line_arrived(dy)
            source = image_at(per_dev - dy)
            place = pl.ds(pl.multiple_of(source * chunk, chunk), chunk)
            flat = part_recv[0, pl.ds(source * heads, heads)].reshape(chunk, pair)
            k_part[j, place, :] = as_keys(flat, source * chunk, asked_counts[j], j == 1)
            queries = beside_ones(flat.T[j * head_dim : (j + 1) * head_dim], False)
            keys = k_own[...]
        else:
            if j == 0 and dy == rings[0]:
                arrived(2, part_send.at[1], part_recv.at[1])
                across = part_recv[1].reshape(keypoints, pair).T
                v_part[0] = beside_ones(across[0:head_dim], True)
                v_part[1] = beside_ones(across[head_dim:pair], True)
            place = pl.ds(pl.multiple_of(image_at(dy) * chunk, chunk), chunk)
            queries = q_own[j, :, place]
            keys = k_part[j]
        ahead[n % 2][...] = jnp.dot(keys, queries, preferred_element_type=F32)

    low_half = lanes((chunk // 2, pair)) < head_dim

    def attend(n):
        side, j, dy = steps[n]
        values = v_own[...] if side == "partner" else v_part[j]
        scores = ahead[n % 2][...]
        peak = jnp.max(scores, axis=0, keepdims=True)
        raised = jnp.exp(scores - peak).astype(BF16)
        total = jnp.dot(values, raised, preferred_element_type=F32)
        split = (total / total[0:1, :]).T.reshape(heads, 2, half, pair)
        upper = split[:, 0].reshape(chunk // 2, pair)
        lower = pltpu.roll(split[:, 1].reshape(chunk // 2, pair), head_dim, 1)
        message = jnp.where(low_half, lower, upper).reshape(heads, half, pair)
        if side == "partner":
            ahead_by = (per_dev - dy) % per_dev
            msg_send[pl.ds(image_at(ahead_by) * heads, heads), j] = message.astype(BF16)
            if j == 1:
                spread(3, msg_send, msg_recv, ahead_by)
        else:
            part = pl.ds(image_at(dy) * heads, heads)
            if j == 0:
                ret_acc[part] = message
            else:
                sum_send[part] = (ret_acc[part] + message).astype(BF16)
                spread(4, sum_send, sum_recv, dy)

    steps = [("partner", j, dy) for dy in rings for j in range(2)]
    steps += [("own", j, dy) for j in range(2) for dy in rings]
    asked_counts = [counts[partners[j, block * per_dev + my_image]] for j in range(2)]
    arrived(0, own_send, own_recv)
    whole = own_recv[...].reshape(keypoints, pair)
    k_own[...] = as_keys(whole, 0, counts[block * per_dev + my_image], False)
    across = whole.T
    q_own[0] = beside_ones(across[0:head_dim], False)
    q_own[1] = beside_ones(across[0:head_dim], True)
    v_own[...] = beside_ones(across[head_dim:pair], True)
    back_copies = []

    def send_back():
        arrived(3, msg_send, msg_recv)
        for kind, offset in enumerate(OFFSETS):
            for c in range(CAP):
                edge = jnp.maximum(my_slots[kind][c] - 1, 0)
                image, j = lax.div(edge, 2), lax.rem(edge, 2)
                back_send[kind, c] = msg_recv[pl.ds(image * heads, heads), j]
            copy = pltpu.make_async_remote_copy(
                src_ref=back_send.at[kind],
                dst_ref=back_recv.at[kind],
                send_sem=b_send_sem.at[kind],
                recv_sem=b_recv_sem.at[kind],
                device_id=(img_peer(offset), me),
                device_id_type=MESH,
            )
            copy.start()
            back_copies.append(copy)

    score(0)
    for n in range(len(steps)):
        if n + 1 < len(steps):
            score(n + 1)
        attend(n)
        if n + 3 == len(steps):
            send_back()

    arrived(4, sum_send, sum_recv)
    inboxes, degrees = [], []
    for image in range(per_dev):
        inboxes.append(sum_recv[image * heads : (image + 1) * heads].astype(F32))
        degree = jnp.int32(2)
        for slots in incoming_slots:
            for slot in slots:
                degree = degree + jnp.where(slot == image + 1, 1, 0)
        degrees.append(degree.astype(F32))
    for kind in range(len(OFFSETS)):
        back_copies[kind].wait_recv()
        for c in range(CAP):
            message = back_recv[kind, c].astype(F32)
            for image in range(per_dev):
                hit = jnp.where(incoming_slots[kind][c] == image + 1, 1.0, 0.0)
                inboxes[image] = inboxes[image] + hit * message
    packed = [
        (inbox / degree).astype(BF16) for inbox, degree in zip(inboxes, degrees, strict=True)
    ]
    stacked = jnp.concatenate(
        [jnp.concatenate([packed[i][h] for i in range(per_dev)], axis=0) for h in range(heads)],
        axis=1,
    )
    both = jnp.dot(stacked, w2[...], preferred_element_type=F32).astype(BF16)
    for image in range(per_dev):
        mine = both[image * half : (image + 1) * half]
        proj[image * rows : image * rows + half, :] = mine[:, 0:width]
        proj[image * rows + half : (image + 1) * rows, :] = mine[:, width : 2 * width]

    outs = (out_0, out_1, out_2, out_3)
    for image in range(per_dev):
        part = pl.ds(image * rows, rows)
        hidden = hid[part, :] + jnp.dot(
            proj[part, :], f1_ref[width : 2 * width, :], preferred_element_type=F32
        )
        center = jnp.mean(hidden, axis=1, keepdims=True)
        away = hidden - center
        spreads = jnp.mean(away * away, axis=1, keepdims=True)
        normed = away * lax.rsqrt(spreads + 1e-5) * gain_ref[...] + nbias_ref[...]
        active = (0.5 * normed * (1.0 + lax.erf(normed * (0.5**0.5)))).astype(BF16)
        outs[image][...] = (
            jnp.dot(active, f2_ref[...], preferred_element_type=F32) + b2_ref[...]
        )

    for phase, send in (
        (0, own_send),
        (1, part_send.at[0]),
        (2, part_send.at[1]),
        (3, msg_send),
        (4, sum_send),
    ):
        left(phase, send)
    for copy in z_copies + back_copies:
        copy.wait_send()


def HEADS_OF(width):
    return width // 64


def per_device(
    features,
    partners,
    counts,
    shared_proj,
    value_proj,
    out_proj,
    ffn_in,
    ffn_in_bias,
    norm_gain,
    norm_bias,
    ffn_out,
    ffn_out_bias,
):
    img_count = lax.axis_size("img")
    row_devices = lax.axis_size("row")
    per_dev, rows, width = features.shape
    heads = HEADS_OF(width)
    head_dim = width // heads
    pair = 2 * head_dim
    keypoints = rows * row_devices
    hidden = ffn_in.shape[1]
    half = rows // 2
    kinds = len(OFFSETS)
    anywhere = pl.BlockSpec(memory_space=pl.ANY)
    update = pl.pallas_call(
        functools.partial(kernel, img_count, row_devices),
        out_shape=[jax.ShapeDtypeStruct(features.shape[1:], F32)] * per_dev,
        in_specs=[anywhere] * 12,
        out_specs=[pl.BlockSpec(memory_space=pltpu.VMEM)] * per_dev,
        scratch_shapes=[
            pltpu.SMEM(partners.shape[::-1], jnp.int32),
            pltpu.SMEM(counts.shape, jnp.int32),
            pltpu.VMEM(features.shape, F32),
            pltpu.VMEM(shared_proj.shape, BF16),
            pltpu.VMEM(value_proj.shape, BF16),
            pltpu.VMEM(out_proj.shape, BF16),
            pltpu.VMEM(ffn_in.shape, BF16),
            pltpu.VMEM((1, hidden), F32),
            pltpu.VMEM((1, hidden), F32),
            pltpu.VMEM((1, hidden), F32),
            pltpu.VMEM(ffn_out.shape, BF16),
            pltpu.VMEM((1, width), F32),
            pltpu.SemaphoreType.DMA((12,)),
            pltpu.VMEM((per_dev, rows, width), BF16),
            pltpu.VMEM((2, kinds, CAP, half, width), BF16),
            pltpu.VMEM((width, 2 * width), BF16),
            pltpu.VMEM((heads * pair, 2 * width), BF16),
            pltpu.VMEM((per_dev * rows, hidden), F32),
            pltpu.VMEM((kinds * CAP, half, width), BF16),
            pltpu.VMEM((kinds * CAP, half, width), BF16),
            pltpu.VMEM((row_devices, rows, pair), BF16),
            pltpu.VMEM((row_devices, rows, pair), BF16),
            pltpu.VMEM((2, row_devices, rows, pair), BF16),
            pltpu.VMEM((2, row_devices, rows, pair), BF16),
            pltpu.VMEM((keypoints, pair), BF16),
            pltpu.VMEM((2, pair, keypoints), BF16),
            pltpu.VMEM((pair, keypoints), BF16),
            pltpu.VMEM((2, keypoints, pair), BF16),
            pltpu.VMEM((2, pair, keypoints), BF16),
            pltpu.VMEM((keypoints, rows * heads), F32),
            pltpu.VMEM((keypoints, rows * heads), F32),
            pltpu.VMEM((row_devices, half, pair), F32),
            pltpu.VMEM((row_devices, 2, half, pair), BF16),
            pltpu.VMEM((row_devices, half, pair), BF16),
            pltpu.VMEM((row_devices, 2, half, pair), BF16),
            pltpu.VMEM((row_devices, half, pair), BF16),
            pltpu.VMEM((kinds, CAP, heads, half, pair), BF16),
            pltpu.VMEM((kinds, CAP, heads, half, pair), BF16),
            pltpu.VMEM((per_dev * rows, width), BF16),
            pltpu.SemaphoreType.DMA((2, kinds)),
            pltpu.SemaphoreType.DMA((2, kinds)),
            pltpu.SemaphoreType.DMA((5,)),
            pltpu.SemaphoreType.DMA((5,)),
            pltpu.SemaphoreType.DMA((per_dev,)),
            pltpu.SemaphoreType.DMA((5,)),
            pltpu.SemaphoreType.DMA((kinds,)),
            pltpu.SemaphoreType.DMA((kinds,)),
        ],
        compiler_params=pltpu.CompilerParams(
            collective_id=0, has_side_effects=True, vmem_limit_bytes=67043328 - 10550 * 1024
        ),
    )(
        partners.T,
        counts,
        features,
        shared_proj,
        value_proj,
        out_proj,
        ffn_in,
        ffn_in_bias.reshape(1, -1),
        norm_gain.reshape(1, -1),
        norm_bias.reshape(1, -1),
        ffn_out,
        ffn_out_bias.reshape(1, -1),
    )
    return features + jnp.stack(update)


def solution(mesh):
    return jax.shard_map(
        per_device,
        mesh=mesh,
        in_specs=(P("img", "row", None), P(), P(), P(), P(), P(), P(), P(), P(), P(), P(), P()),
        out_specs=P("img", "row", None),
        check_vma=False,
    )
```
